32 devices in a mesh: group: 8 (over y, x, core), shard: 4 (over z).
Axes of the slice: x: 2, y: 2, z: 4, core: 2. Of those that a mesh axis runs over, the one named last changes fastest.
Arguments:
- tokens: bfloat16 [2, 8, 2048, 768], P(None, 'group', 'shard'), may hold values from -6 to 6
- cond: float32 [2, 8, 128], P(None, 'group'), may hold values from -6 to 6
- seg_ids: int32 [2, 8, 2048], P(None, 'group'), may hold values from 0 to 12, as said below
- parents: int32 [2, 8, 13], P(None, 'group'), may hold values from 0 to 4, as said below
- cotangent: bfloat16 [2, 8, 2048, 768], P(None, 'group', 'shard'), may hold values from -6 to 6
- w_qkv: bfloat16 [768, 2304], P('shard'), may hold values from -0.21875 to 0.21875
- w_out: bfloat16 [768, 768], P('shard'), may hold values from -1.75 to 1.75
- w_fc1: bfloat16 [768, 3072], P('shard'), may hold values from -0.21875 to 0.21875
- b_fc1: bfloat16 [3072], P('shard'), may hold values from -3 to 3
- w_fc2: bfloat16 [3072, 768], P('shard'), may hold values from -0.109375 to 0.109375
- b_fc2: bfloat16 [768], P('shard'), may hold values from -3 to 3
- w_ada: bfloat16 [128, 4608], P(None, 'shard'), may hold values from -0.5 to 0.5
- b_ada: bfloat16 [4608], P('shard'), may hold values from -3 to 3
- gain1: bfloat16 [768], P('shard'), may hold values from 0.25 to 1.75
- gain2: bfloat16 [768], P('shard'), may hold values from 0.25 to 1.75
Outputs:
- out: bfloat16 [2, 8, 2048, 768], P(None, 'group', 'shard')
- grad_tokens: bfloat16 [2, 8, 2048, 768], P(None, 'group', 'shard')
- grad_cond: float32 [2, 8, 128], P(None, 'group')
- grad_w_qkv: float32 [768, 2304], P('shard')
- grad_w_out: float32 [768, 768], P('shard')
- grad_w_fc1: float32 [768, 3072], P('shard')
- grad_b_fc1: float32 [3072], P('shard')
- grad_w_fc2: float32 [3072, 768], P('shard')
- grad_b_fc2: float32 [768], P('shard')
- grad_w_ada: float32 [128, 4608], P(None, 'shard')
- grad_b_ada: float32 [4608], P('shard')
- grad_gain1: float32 [768], P('shard')
- grad_gain2: float32 [768], P('shard')
The draws below stay inside these ranges and needn't reach their ends.
Inputs may be any that keep to these rules, and one draw needn't show every extreme that they name: `seg_ids`: along each tree's 2048 tokens the segment ids never fall, and every one of the 13 segments holds at least one token. In each tree segment 0 is the trunk with parents[0] = 0, segments 1 to 4 are branches with parent 0, and segments 5 to 12 are leaves, two on each branch.
All inputs are finite; a program needn't handle non-finite values.
Results may differ from the reference program's by a relative error of at most 0.02.
The reference program's roundings to bfloat16 on the way count: a program that leaves them out, or rounds other values in their place, can miss the bound.
Values may be sent and summed in bfloat16 or wider, within the bound.
No kernel may reach another device: no remote copies, remote signals or barrier semaphores. Data moves between devices by JAX's collectives and lax.ppermute only.
A program may use at most 256 MiB of HBM per device.

```python
import math
import jax
import jax.numpy as jnp
from jax import lax

D = 768
HEADS = 12
FF = 3072
C = 128
MB = 2
SEGS = 13
TREE = 2048
N_GROUP = 8


def draw_seg_ids(key, part):
    low_len = max(1, TREE // 40)
    high_len = max(low_len + 1, 3 * TREE // 40)
    others = jax.random.randint(key, (MB, N_GROUP, SEGS - 1), low_len, high_len).astype(jnp.int32)
    trunk = TREE - jnp.sum(others, axis=-1, keepdims=True)
    lengths = jnp.concatenate([trunk, others], axis=-1)
    seg_ends = jnp.cumsum(lengths, axis=-1)
    places = jnp.arange(TREE, dtype=jnp.int32)
    return jnp.sum((places[None, None, :, None] >= seg_ends[:, :, None, :]).astype(jnp.int32), axis=-1).astype(jnp.int32)


def draw_parents(key, part):
    leaf_base = jnp.array([1, 1, 2, 2, 3, 3, 4, 4], jnp.int32)
    leaf_rows = jnp.broadcast_to(leaf_base, (MB, N_GROUP, 8))
    shuffled = jax.random.permutation(key, leaf_rows, axis=-1, independent=True)
    head_rows = jnp.zeros((MB, N_GROUP, 5), jnp.int32)
    return jnp.concatenate([head_rows, shuffled], axis=-1).astype(jnp.int32)


def level_of(rng, extent, shards, smallest, top_value):
    level = 1.0
    for dim, blocks in shards:
        draws = jax.random.uniform(jax.random.fold_in(jax.random.fold_in(rng, 6), dim), (blocks,), jnp.float32, smallest / len(shards), top_value / len(shards))
        level = level * jnp.repeat(jnp.exp(draws), extent[dim] // blocks).reshape((-1,) + (1,) * (len(extent) - 1 - dim))
    return level


def bell_draw(key, shape, deviation, bound, cuts=(), kind=jnp.bfloat16):
    level = level_of(key, shape, cuts, -0.22, 0.18) if cuts else 1.0
    values = jax.random.normal(key, shape, jnp.float32) * deviation * level
    return jnp.minimum(jnp.maximum(values, -bound), bound).astype(kind)


def setup_inputs(seed: int = 0) -> dict:
    key_list = jax.random.split(jax.random.key(seed), 16)
    return {
        "tokens": bell_draw(key_list[0], (MB, N_GROUP, TREE, D), 1.0, 6.0, ((1, 8), (2, 4))),
        "cond": bell_draw(key_list[1], (MB, N_GROUP, C), 1.0, 6.0, ((1, 8),), jnp.float32),
        "seg_ids": draw_seg_ids(jax.random.fold_in(key_list[15], 71), 0),
        "parents": draw_parents(jax.random.fold_in(key_list[15], 71), 0),
        "cotangent": bell_draw(key_list[4], (MB, N_GROUP, TREE, D), 1.0, 6.0, ((1, 8), (2, 4))),
        "w_qkv": bell_draw(key_list[5], (D, 3 * D), D ** -0.5, 0.21875, ((0, 4),)),
        "w_out": bell_draw(key_list[6], (D, D), (max(D // 64, 1)) ** -0.5, 1.75, ((0, 4),)),
        "w_fc1": bell_draw(key_list[7], (D, FF), D ** -0.5, 0.21875, ((0, 4),)),
        "b_fc1": bell_draw(key_list[8], (FF,), 0.5, 3.0, ((0, 4),)),
        "w_fc2": bell_draw(key_list[9], (FF, D), FF ** -0.5, 0.109375, ((0, 4),)),
        "b_fc2": bell_draw(key_list[10], (D,), 0.5, 3.0, ((0, 4),)),
        "w_ada": bell_draw(key_list[11], (C, 6 * D), C ** -0.5, 0.5, ((1, 4),)),
        "b_ada": bell_draw(key_list[12], (6 * D,), 0.5, 3.0, ((0, 4),)),
        "gain1": jnp.clip(1.0 + 0.15 * jax.random.normal(key_list[13], (D,), jnp.float32), 0.25, 1.75).astype(jnp.bfloat16),
        "gain2": jnp.clip(1.0 + 0.15 * jax.random.normal(key_list[14], (D,), jnp.float32), 0.25, 1.75).astype(jnp.bfloat16),
    }


EPS = 1e-05
GELU_C = 0.7978845608028654
GELU_K = 0.044715
HIGH = lax.Precision.HIGHEST

@jax.custom_vjp
def low(v):
    return lax.optimization_barrier(v.astype(jnp.bfloat16)).astype(jnp.float32)

@jax.custom_vjp
def low_back(v):
    return v

def low_keep(v):
    return (low(v), None)

def low_pass(kept, grad):
    return (grad,)

def back_keep(v):
    return (v, None)

def back_low(kept, grad):
    return (low(grad),)
low.defvjp(low_keep, low_pass)
low_back.defvjp(back_keep, back_low)

def path_mask(query_seg, key_seg, parent_row):
    segments = parent_row.shape[0]
    labels = jnp.arange(segments, dtype=jnp.int32)
    first_up = lax.optimization_barrier(jnp.sum(jnp.where(query_seg[:, None] == labels[None, :], parent_row[None, :], 0), axis=1)).astype(jnp.int32)
    second_up = lax.optimization_barrier(jnp.sum(jnp.where(first_up[:, None] == labels[None, :], parent_row[None, :], 0), axis=1)).astype(jnp.int32)
    key_segs = key_seg[None, :]
    return (key_segs == query_seg[:, None]) | (key_segs == first_up[:, None]) | (key_segs == second_up[:, None])

def layer_norm(values, gain):
    centred = values - lax.optimization_barrier(jnp.mean(values, axis=-1, keepdims=True))
    return centred * lax.rsqrt(lax.optimization_barrier(jnp.mean(centred * centred, axis=-1, keepdims=True)) + EPS) * gain

def forward(tok_in, cond_row, params, allowed):
    qkv_w, out_w, fc1_w, fc1_b, fc2_w, fc2_b, ada_w, ada_b, gain_one, gain_two = params
    tree_len, model_width = tok_in.shape
    head_dim = model_width // HEADS
    score_scale = 1.0 / math.sqrt(head_dim)
    ada = jnp.dot(cond_row[None, :], ada_w, precision=HIGH)[0] + ada_b
    shift_one, scale_one, gate_one, shift_two, scale_two, gate_two = jnp.split(ada, 6)
    act_one = low(layer_norm(tok_in, gain_one) * (1.0 + scale_one) + shift_one)
    qkv = low(low_back(jnp.dot(act_one, qkv_w, precision=HIGH)))
    query = qkv[:, :model_width].reshape(tree_len, HEADS, head_dim)
    key_part = qkv[:, model_width:2 * model_width].reshape(tree_len, HEADS, head_dim)
    val_part = qkv[:, 2 * model_width:].reshape(tree_len, HEADS, head_dim)
    scores = low_back(jnp.einsum('qhd,khd->hqk', query, key_part, precision=HIGH) * score_scale)
    masked = jnp.where(allowed[None], scores, -1000000000.0)
    top_val = lax.optimization_barrier(jnp.max(masked, axis=-1, keepdims=True))
    expo = jnp.exp(masked - top_val)
    probs = low(expo / lax.optimization_barrier(jnp.sum(expo, axis=-1, keepdims=True)))
    attn = low(low_back(jnp.einsum('hqk,khd->qhd', probs, val_part, precision=HIGH))).reshape(tree_len, model_width)
    branch_one = low_back(jnp.dot(attn, out_w, precision=HIGH))
    middle = tok_in + gate_one * branch_one
    act_two = low(layer_norm(middle, gain_two) * (1.0 + scale_two) + shift_two)
    pre_act = low_back(jnp.dot(act_two, fc1_w, precision=HIGH) + fc1_b)
    hidden = low(0.5 * pre_act * (1.0 + jnp.tanh(GELU_C * (pre_act + GELU_K * pre_act * pre_act * pre_act))))
    branch_two = low_back(jnp.dot(hidden, fc2_w, precision=HIGH) + fc2_b)
    return middle + gate_two * branch_two

def reference(tokens, cond, seg_ids, parents, cotangent, w_qkv, w_out, w_fc1, b_fc1, w_fc2, b_fc2, w_ada, b_ada, gain1, gain2):
    params = tuple((weight.astype(jnp.float32) for weight in (w_qkv, w_out, w_fc1, b_fc1, w_fc2, b_fc2, w_ada, b_ada, gain1, gain2)))
    batches, groups, tree_len, model_width = tokens.shape
    tree_count = batches * groups
    tok_all = tokens.reshape(tree_count, tree_len, model_width)
    cot_all = cotangent.reshape(tree_count, tree_len, model_width)
    cond_all = cond.reshape(tree_count, cond.shape[2])
    seg_all = seg_ids.reshape(tree_count, tree_len)
    par_all = parents.reshape(tree_count, parents.shape[2])

    def one_tree(carry, item):
        tok_in, cond_row, tree_seg, parent_row, grad_out = item
        allowed = path_mask(tree_seg, tree_seg, parent_row)

        def run(tok_val, cond_val, *param_vals):
            return forward(tok_val, cond_val, param_vals, allowed)
        result, pull = jax.vjp(run, tok_in.astype(jnp.float32), cond_row, *params)
        grads = pull(grad_out.astype(jnp.float32))
        new_carry = tuple((total + grad for total, grad in zip(carry, grads[2:])))
        return (new_carry, (result.astype(jnp.bfloat16), grads[0].astype(jnp.bfloat16), grads[1]))
    start_carry = tuple((jnp.zeros_like(param) for param in params))
    totals, (outs, grads_x, grads_c) = lax.scan(one_tree, start_carry, (tok_all, cond_all, seg_all, par_all, cot_all))
    return (outs.reshape(batches, groups, tree_len, model_width), grads_x.reshape(batches, groups, tree_len, model_width), grads_c.reshape(batches, groups, cond.shape[2]), totals[0], totals[1], totals[2], totals[3], totals[4], totals[5], totals[6], totals[7], totals[8], totals[9])
```

```python
import math

import jax
import jax.numpy as jnp
from jax import lax
from jax.sharding import PartitionSpec as P

HEADS = 12
EPS = 1e-05
GELU_C = 0.7978845608028654
GELU_K = 0.044715
HIGH = lax.Precision.HIGHEST
BF = jnp.bfloat16
F32 = jnp.float32


def layer_norm(values):
    centred = values - jnp.mean(values, axis=-1, keepdims=True)
    inv_std = lax.rsqrt(jnp.mean(centred * centred, axis=-1, keepdims=True) + EPS)
    return centred * inv_std, inv_std


def norm_back(grad_normed, normed, inv_std):
    first_mean = jnp.mean(grad_normed, axis=-1, keepdims=True)
    second = jnp.mean(grad_normed * normed, axis=-1, keepdims=True)
    return (grad_normed - first_mean - normed * second) * inv_std


def gelu_parts(pre_act):
    inner_arg = GELU_C * (pre_act + GELU_K * pre_act * pre_act * pre_act)
    tangent = jnp.tanh(inner_arg)
    gelu_value = 0.5 * pre_act * (1.0 + tangent)
    gelu_slope = 0.5 * (1.0 + tangent) + 0.5 * pre_act * (1.0 - tangent * tangent) * GELU_C * (
        1.0 + 3.0 * GELU_K * pre_act * pre_act
    )
    return gelu_value, gelu_slope


def mm(left, right):
    return jnp.dot(left, right, preferred_element_type=F32)


def mm_t(left, right):
    return lax.dot_general(left, right, (((1,), (1,)), ((), ())), preferred_element_type=F32)


def t_mm(left, right):
    return lax.dot_general(left, right, (((0,), (0,)), ((), ())), preferred_element_type=F32)


class Links:
    def __init__(self, groups, shards):
        self.groups, self.shards, self.planes = groups, shards, groups // 2
        self.g = lax.axis_index("group")
        self.s = lax.axis_index("shard")
        self.c = self.g % 2
        self.plane = self.g // 2

    def swap(self, value):
        return lax.ppermute(value, "group", [(i, i ^ 1) for i in range(self.groups)])

    def turn(self, value, step):
        n = self.shards
        return lax.ppermute(value, "shard", [(i, (i + step) % n) for i in range(n)])

    def across(self, value, step):
        return lax.ppermute(value, "group", [(i, i ^ (2 * step)) for i in range(self.groups)])

    def round_perm(self, k):
        n, perm = self.shards, []
        for g in range(self.groups):
            for s in range(n):
                d = (s + k) % n
                goal = ((g // 2) * 2 + d % 2, 2 * (d // 2) + g % 2)
                perm.append((g * n + s, goal[0] * n + goal[1]))
        return perm

    def to_trees(self, value):
        batches, rows, width = value.shape
        pieces = value.reshape(batches * 2, rows // 2, width)
        got = []
        for k in range(self.shards):
            piece = lax.dynamic_index_in_dim(pieces, (self.s + k) % self.shards, 0, False)
            got.append(lax.ppermute(piece, ("group", "shard"), self.round_perm(k)))
        return jnp.concatenate(got, axis=0)

    def from_trees(self, value, batches):
        total, width = value.shape
        rows = total // self.shards
        out = jnp.zeros((self.shards, rows, width), value.dtype)
        for k in range(self.shards):
            back = [(b, a) for a, b in self.round_perm(k)]
            piece = lax.ppermute(value[k * rows : (k + 1) * rows], ("group", "shard"), back)
            out = lax.dynamic_update_index_in_dim(out, piece, (self.s + k) % self.shards, 0)
        return out.reshape(batches, 1, 2 * rows, width)

    def line_order(self, parts):
        stacked = jnp.stack(parts)
        return jnp.stack(
            [
                lax.dynamic_index_in_dim(stacked, (self.s - j) % self.shards, 0, False)
                for j in range(self.shards)
            ]
        )

    def line_gather(self, value):
        return self.line_order([value] + [self.turn(value, k) for k in range(1, self.shards)])

    def gather_weight(self, weight):
        rows = weight.shape[0] // self.groups
        part = lax.dynamic_slice_in_dim(weight, self.g * rows, rows, 0)
        return lax.all_gather(part, ("shard", "group"), axis=0, tiled=True)

    def plane_sum(self, value):
        if self.planes != 4:
            groups = [[2 * p + c for p in range(self.planes)] for c in range(2)]
            return lax.psum_scatter(
                value, "group", scatter_dimension=1, axis_index_groups=groups
            ).astype(F32)
        total = lax.dynamic_index_in_dim(value, self.plane, 1, False).astype(F32)
        for k in range(1, 4):
            piece = lax.dynamic_index_in_dim(value, self.plane ^ k, 1, False)
            total = total + self.across(piece, k).astype(F32)
        return total

    def plane_gather(self, value):
        if self.planes != 4:
            groups = [[2 * p + c for p in range(self.planes)] for c in range(2)]
            return lax.all_gather(value, "group", axis_index_groups=groups)
        parts = jnp.stack([value] + [self.across(value, k) for k in range(1, 4)])
        return jnp.stack(
            [lax.dynamic_index_in_dim(parts, self.plane ^ j, 0, False) for j in range(4)]
        )

    def reduce_grad(self, grad):
        width = grad.shape[1]
        rows = grad.shape[0] // self.shards
        halves = grad.reshape(self.shards, 2, rows // 2, width)
        mine = lax.dynamic_index_in_dim(halves, self.c, 1, False)
        yours = lax.dynamic_index_in_dim(halves, 1 - self.c, 1, False)
        pair = (mine.astype(F32) + self.swap(yours).astype(F32)).astype(BF)
        fine = rows // 2 // self.planes
        plane = self.plane_sum(pair.reshape(self.shards, self.planes, fine, width)).astype(BF)
        total = lax.dynamic_index_in_dim(plane, self.s, 0, False).astype(F32)
        for k in range(1, self.shards):
            piece = lax.dynamic_index_in_dim(plane, (self.s + k) % self.shards, 0, False)
            total = total + self.turn(piece, k).astype(F32)
        half = self.plane_gather(total.astype(BF)).reshape(rows // 2, width)
        other = self.swap(half)
        out = jnp.where(
            self.c == 0, jnp.concatenate([half, other]), jnp.concatenate([other, half])
        )
        return out.astype(F32)

    def tree_sums(self, vec):
        line = self.line_gather(vec)
        return line + self.swap(line)


def on_device(
    tokens,
    cond,
    seg_ids,
    parents,
    cotangent,
    w_qkv,
    w_out,
    w_fc1,
    b_fc1,
    w_fc2,
    b_fc2,
    w_ada,
    b_ada,
    gain1,
    gain2,
    groups,
):
    batches, _, row_count, width = tokens.shape
    shards = lax.axis_size("shard")
    assert shards == 2 * batches and groups % 2 == 0
    head_dim = width // HEADS
    scale = 1.0 / math.sqrt(head_dim)
    net = Links(groups, shards)
    rows = row_count // 2
    mine = shards * rows
    tree_len = seg_ids.shape[2]
    labels = parents.shape[2]
    cond_dim = cond.shape[2]

    qkv_w = net.gather_weight(w_qkv)
    tok = net.to_trees(tokens[:, 0])
    out_w = net.gather_weight(w_out)
    fc1_w = net.gather_weight(w_fc1)
    fc2_w = net.gather_weight(w_fc2)
    grad_out = net.to_trees(cotangent[:, 0])

    packed = jnp.concatenate(
        [seg_ids[:, 0].astype(F32), parents[:, 0].astype(F32), cond[:, 0]], axis=1
    )
    other = net.swap(packed)
    trees = jnp.where(
        net.c == 0, jnp.stack([packed, other], axis=1), jnp.stack([other, packed], axis=1)
    ).reshape(shards, packed.shape[1])
    conds = trees[:, tree_len + labels :]
    my_tree = lax.dynamic_index_in_dim(trees, net.s, 0, False)
    tree_seg = my_tree[:tree_len]
    parent_row = my_tree[tree_len : tree_len + labels]
    ada_rows = jnp.dot(conds, w_ada.astype(F32), precision=HIGH) + b_ada.astype(F32)
    small = jnp.concatenate([b_fc1, b_fc2, gain1, gain2]).astype(F32)
    pieces = jnp.concatenate(
        [ada_rows, jnp.broadcast_to(small[None], (shards, small.shape[0]))], axis=1
    )
    got = [lax.dynamic_index_in_dim(pieces, net.s, 0, False)]
    for k in range(1, shards):
        piece = lax.dynamic_index_in_dim(pieces, (net.s + k) % shards, 0, False)
        got.append(net.turn(piece, k))
    line = net.line_order(got)
    cut = ada_rows.shape[1]
    ada = line[:, :cut].reshape(-1)
    ends = [cut]
    for vec in (b_fc1, b_fc2, gain1, gain2):
        ends.append(ends[-1] + vec.shape[0])
    fc1_b, fc2_b, gain_a, gain_b = (
        line[:, ends[i] : ends[i + 1]].reshape(-1) for i in range(4)
    )
    shift_one, scale_one, gate_one, shift_two, scale_two, gate_two = jnp.split(ada, 6)

    half_seg = tree_seg.reshape(shards, 2, rows)
    base = 2 * (net.s // 2)

    def row_segs(place):
        take = lax.dynamic_index_in_dim(half_seg, place, 1, False)
        return jnp.concatenate(
            [
                lax.dynamic_index_in_dim(take, (base + place - k) % shards, 0, False)
                for k in range(shards)
            ]
        )

    query_seg = row_segs(net.c)
    key_seg = jnp.concatenate([query_seg, row_segs(1 - net.c)])
    label_row = jnp.arange(labels, dtype=F32)

    def parent_of(seg):
        return jnp.sum(
            jnp.where(seg[:, None] == label_row[None, :], parent_row[None, :], 0.0), axis=1
        )

    first_up = parent_of(query_seg)
    second_up = parent_of(first_up)
    allowed = (
        (key_seg[None, :] == query_seg[:, None])
        | (key_seg[None, :] == first_up[:, None])
        | (key_seg[None, :] == second_up[:, None])
    )

    tok_f = tok.astype(F32)
    normed_one, inv_one = layer_norm(tok_f)
    lifted_one = normed_one * gain_a
    act_one = (lifted_one * (1.0 + scale_one) + shift_one).astype(BF)
    qkv = mm(act_one, qkv_w).astype(BF)
    kv = qkv[:, width:]
    whole_kv = jnp.concatenate([kv, net.swap(kv)], axis=0)

    def heads_of(x):
        return x.reshape(x.shape[0], HEADS, head_dim).transpose(1, 0, 2)

    query_heads = heads_of(qkv[:, :width])
    key_heads = heads_of(whole_kv[:, :width])
    val_heads = heads_of(whole_kv[:, width:])

    def head_forward(unused, items):
        q_h, k_h, v_h = items
        masked = jnp.where(allowed, mm_t(q_h, k_h) * scale, -1000000000.0)
        top_val = jnp.max(masked, axis=-1, keepdims=True)
        expo = jnp.exp(masked - top_val)
        row_total = jnp.sum(expo, axis=-1, keepdims=True)
        probs = expo / row_total
        head_out = mm(probs.astype(BF), v_h)
        return unused, (head_out.astype(BF), top_val + jnp.log(row_total))

    _, (attn_heads, log_totals) = lax.scan(head_forward, 0, (query_heads, key_heads, val_heads))
    attn = attn_heads.transpose(1, 0, 2).reshape(mine, width)
    branch_one = mm(attn, out_w)
    middle = tok_f + gate_one * branch_one
    normed_two, inv_two = layer_norm(middle)
    lifted_two = normed_two * gain_b
    act_two = (lifted_two * (1.0 + scale_two) + shift_two).astype(BF)
    pre_act = mm(act_two, fc1_w) + fc1_b
    gelu_value, gelu_slope = gelu_parts(pre_act)
    hidden = gelu_value.astype(BF)
    branch_two = mm(hidden, fc2_w) + fc2_b
    out = net.from_trees((middle + gate_two * branch_two).astype(BF), batches)

    grad_f = grad_out.astype(F32)
    grad_y2 = (grad_f * gate_two).astype(BF)
    d_gate_two = jnp.sum(grad_f * branch_two, axis=0)
    t_fc2 = net.reduce_grad(t_mm(hidden, grad_y2).astype(BF))
    g_b2 = jnp.sum(grad_y2.astype(F32), axis=0)
    grad_pre = (mm_t(grad_y2, fc2_w) * gelu_slope).astype(BF)
    t_fc1 = net.reduce_grad(t_mm(act_two, grad_pre).astype(BF))
    g_b1 = jnp.sum(grad_pre.astype(F32), axis=0)
    grad_a2 = mm_t(grad_pre, fc1_w)
    d_shift_two = jnp.sum(grad_a2, axis=0)
    d_scale_two = jnp.sum(grad_a2 * lifted_two, axis=0)
    grad_h2 = grad_a2 * (1.0 + scale_two)
    g_gain2 = jnp.sum(grad_h2 * normed_two, axis=0)
    grad_mid = grad_f + norm_back(grad_h2 * gain_b, normed_two, inv_two)
    grad_y1 = (grad_mid * gate_one).astype(BF)
    d_gate_one = jnp.sum(grad_mid * branch_one, axis=0)
    t_out = net.reduce_grad(t_mm(attn, grad_y1).astype(BF))
    grad_attn = heads_of(mm_t(grad_y1, out_w).astype(BF))

    def head_backward(unused, items):
        q_h, k_h, v_h, lse_h, da_h = items
        masked = jnp.where(allowed, mm_t(q_h, k_h) * scale, -1000000000.0)
        again = jnp.exp(masked - lse_h)
        grad_prob = mm_t(da_h, v_h)
        delta_row = jnp.sum(again * grad_prob, axis=-1, keepdims=True)
        grad_score = (again * (grad_prob - delta_row)).astype(BF)
        grad_q = mm(grad_score, k_h) * scale
        grad_k = t_mm(grad_score, q_h) * scale
        grad_v = t_mm(again.astype(BF), da_h)
        return unused, (grad_q.astype(BF), grad_k, grad_v)

    _, (q_grads, k_grads, v_grads) = lax.scan(
        head_backward, 0, (query_heads, key_heads, val_heads, log_totals, grad_attn)
    )

    def rows_of(x):
        return x.transpose(1, 0, 2).reshape(x.shape[1], width)

    tree_kv = jnp.concatenate([rows_of(k_grads), rows_of(v_grads)], axis=1)
    local_kv = tree_kv[:mine] + net.swap(tree_kv[mine:].astype(BF)).astype(F32)
    grad_qkv = jnp.concatenate([rows_of(q_grads), local_kv.astype(BF)], axis=1)
    t_qkv = net.reduce_grad(t_mm(act_one, grad_qkv).astype(BF))
    grad_a1 = mm_t(grad_qkv, qkv_w)
    d_shift_one = jnp.sum(grad_a1, axis=0)
    d_scale_one = jnp.sum(grad_a1 * lifted_one, axis=0)
    grad_h1 = grad_a1 * (1.0 + scale_one)
    g_gain1 = jnp.sum(grad_h1 * normed_one, axis=0)
    grad_in = grad_mid + norm_back(grad_h1 * gain_a, normed_one, inv_one)
    grads_x = net.from_trees(grad_in.astype(BF), batches)

    early = net.tree_sums(
        jnp.concatenate([d_gate_one, d_shift_two, d_scale_two, d_gate_two, g_gain2, g_b2, g_b1])
    )
    late = net.tree_sums(jnp.concatenate([d_shift_one, d_scale_one, g_gain1]))
    dada = jnp.concatenate([late[:, : 2 * width], early[:, : 4 * width]], axis=1)
    bias = jnp.concatenate([early[:, 4 * width :], late[:, 2 * width :]], axis=1)
    everyone = net.plane_gather(
        jnp.concatenate([dada, conds, jnp.broadcast_to(jnp.sum(bias, axis=0), bias.shape)], axis=1)
    )
    every_dada = everyone[:, :, : 6 * width].reshape(-1, 6 * width)
    every_cond = everyone[:, :, 6 * width : 6 * width + cond_dim].reshape(-1, cond_dim)
    sums = jnp.sum(everyone[:, 0, 6 * width + cond_dim :], axis=0)

    def place(vec):
        n = vec.shape[-1] // shards
        return lax.dynamic_slice_in_dim(vec, net.s * n, n, vec.ndim - 1)

    dada_here = place(every_dada)
    t_ada = lax.dot_general(
        every_cond, dada_here, (((0,), (0,)), ((), ())), precision=HIGH
    )
    t_bada = jnp.sum(dada_here, axis=0)
    g_two, g_bias2, g_bias1, g_one = jnp.split(
        sums, [width, 2 * width, 2 * width + 4 * width]
    )
    own = lax.dynamic_index_in_dim(
        place(dada).reshape(batches, 2, -1), net.c, 1, False
    )
    cond_part = lax.dot_general(
        own, w_ada.astype(F32), (((1,), (1,)), ((), ())), precision=HIGH
    )
    cond_total = cond_part
    for k in range(1, shards):
        cond_total = cond_total + net.turn(cond_part, k)
    return (
        out,
        grads_x,
        cond_total[:, None, :],
        t_qkv,
        t_out,
        t_fc1,
        place(g_bias1),
        t_fc2,
        place(g_bias2),
        t_ada,
        t_bada,
        place(g_one),
        place(g_two),
    )


def solution(mesh):
    in_specs = (
        P(None, "group", "shard", None),
        P(None, "group", None),
        P(None, "group", None),
        P(None, "group", None),
        P(None, "group", "shard", None),
        P("shard", None),
        P("shard", None),
        P("shard", None),
        P("shard"),
        P("shard", None),
        P("shard"),
        P(None, "shard"),
        P("shard"),
        P("shard"),
        P("shard"),
    )
    out_specs = (
        P(None, "group", "shard", None),
        P(None, "group", "shard", None),
        P(None, "group", None),
        P("shard", None),
        P("shard", None),
        P("shard", None),
        P("shard"),
        P("shard", None),
        P("shard"),
        P(None, "shard"),
        P("shard"),
        P("shard"),
        P("shard"),
    )
    groups = mesh.shape["group"]

    def run(*args):
        return on_device(*args, groups)

    return jax.shard_map(
        run, mesh=mesh, in_specs=in_specs, out_specs=out_specs, check_vma=False
    )
```

```python
import functools
import math

import jax
import jax.numpy as jnp
from jax import lax
from jax.experimental import pallas as pl
from jax.experimental.pallas import tpu as pltpu
from jax.sharding import PartitionSpec as P

HEADS = 12
EPS = 1e-05
GELU_C = 0.7978845608028654
GELU_K = 0.044715
HIGH = lax.Precision.HIGHEST
BF = jnp.bfloat16
F32 = jnp.float32
BLOCK = 256
LANES = 128
BIG = -float(2**30)
MASKED = -1000000000.0
PAIRS = 6


def layer_norm(values):
    centred = values - jnp.mean(values, axis=-1, keepdims=True)
    inv_std = lax.rsqrt(jnp.mean(centred * centred, axis=-1, keepdims=True) + EPS)
    return centred * inv_std, inv_std


def norm_back(grad_normed, normed, inv_std):
    first_mean = jnp.mean(grad_normed, axis=-1, keepdims=True)
    second = jnp.mean(grad_normed * normed, axis=-1, keepdims=True)
    return (grad_normed - first_mean - normed * second) * inv_std


def gelu_parts(pre_act):
    inner_arg = GELU_C * (pre_act + GELU_K * pre_act * pre_act * pre_act)
    tangent = jnp.tanh(inner_arg)
    gelu_value = 0.5 * pre_act * (1.0 + tangent)
    gelu_slope = 0.5 * (1.0 + tangent) + 0.5 * pre_act * (1.0 - tangent * tangent) * GELU_C * (
        1.0 + 3.0 * GELU_K * pre_act * pre_act
    )
    return gelu_value, gelu_slope


def mm(left, right):
    return jnp.dot(left, right, preferred_element_type=F32)


def mm_t(left, right):
    return lax.dot_general(left, right, (((1,), (1,)), ((), ())), preferred_element_type=F32)


def t_mm(left, right):
    return lax.dot_general(left, right, (((0,), (0,)), ((), ())), preferred_element_type=F32)


def split_heads(pair):
    first = lax.broadcasted_iota(jnp.int32, pair.shape, 1) < LANES // 2
    zero = jnp.zeros_like(pair)
    return jnp.concatenate([jnp.where(first, pair, zero), jnp.where(first, zero, pair)], axis=0)

def side_by_side(stack):
    n = stack.shape[0] // 2
    return jnp.concatenate([stack[:n], stack[n:]], axis=1)

def lanes_sum(x): return jnp.sum(x, axis=1, keepdims=True)

def fwd_kernel(near, pp, scale, flags, q_ref, kn_ref, vn_ref, kf_ref, vf_ref, feat_ref, hot_ref, o_ref, lse_ref,
               s_ref, m_ref, l_ref, acc_ref, k_all, v_all):
    qb = pl.program_id(1)
    nk = hot_ref.shape[0] // BLOCK
    safe = flags[flags.shape[0] - 1] == 1
    @pl.when(qb == 0)
    def _():
        k_all[:near] = kn_ref[...]; k_all[near:] = kf_ref[...]
        v_all[:near] = vn_ref[...]; v_all[near:] = vf_ref[...]
    feat = feat_ref[...]
    feat2 = jnp.concatenate([feat, feat], axis=0)
    qs = [split_heads(q_ref[:, p*LANES:(p+1)*LANES] * scale) for p in range(pp)]
    m_ref[...] = jnp.full(m_ref.shape, -jnp.inf, F32)
    def scan_scores(exact):
        def step(j, _):
            @pl.when(flags[qb * nk + j] == 1)
            def _():
                rows = pl.ds(pl.multiple_of(j * BLOCK, BLOCK), BLOCK)
                hot = hot_ref[rows, :]
                for p in range(pp):
                    k = k_all[rows, p*LANES:(p+1)*LANES]
                    if exact:
                        ok = mm_t(feat2, hot) > -1.0
                        s = jnp.where(ok, mm_t(qs[p], k), MASKED)
                    else:
                        s = mm_t(jnp.concatenate([qs[p], feat2], axis=1), jnp.concatenate([k, hot], axis=1))
                    s_ref[p, j] = s
                    m_ref[p] = jnp.maximum(m_ref[p], jnp.maximum(s[:, :LANES], s[:, LANES:]))
            return 0
        lax.fori_loop(0, nk, step, 0)
    @pl.when(safe)
    def _(): scan_scores(False)
    @pl.when(jnp.logical_not(safe))
    def _(): scan_scores(True)
    tops = [jnp.max(m_ref[p], axis=1, keepdims=True) for p in range(pp)]
    l_ref[...] = jnp.zeros(l_ref.shape, F32)
    acc_ref[...] = jnp.zeros(acc_ref.shape, F32)
    def step(j, _):
        @pl.when(flags[qb * nk + j] == 1)
        def _():
            rows = pl.ds(pl.multiple_of(j * BLOCK, BLOCK), BLOCK)
            for p in range(pp):
                e = jnp.exp(s_ref[p, j] - tops[p])
                l_ref[p] += e[:, :LANES] + e[:, LANES:]
                v = split_heads(v_all[rows, p*LANES:(p+1)*LANES])
                acc_ref[p] += mm(side_by_side(e.astype(BF)), v)
        return 0
    lax.fori_loop(0, nk, step, 0)
    for p in range(pp):
        total = lanes_sum(l_ref[p])
        lse_ref[p, 0] = tops[p] + jnp.log(total)
        first = lax.broadcasted_iota(jnp.int32, (BLOCK, LANES), 1) < LANES // 2
        o_ref[:, p*LANES:(p+1)*LANES] = (acc_ref[p] / jnp.where(first, total[:BLOCK], total[BLOCK:])).astype(BF)

def attn_fwd(q, kv, far, feat, hot, flags, scale, pp):
    near, width = q.shape
    total = hot.shape[0]
    steps = width // LANES // pp
    nq = near // BLOCK
    col = lambda c: (lambda h, i, f: (0, c * steps + h))
    return pl.pallas_call(
        functools.partial(fwd_kernel, near, pp, scale),
        grid_spec=pltpu.PrefetchScalarGridSpec(
            num_scalar_prefetch=1, grid=(steps, nq),
            in_specs=[
                pl.BlockSpec((BLOCK, pp*LANES), lambda h, i, f: (i, h)),
                pl.BlockSpec((near, pp*LANES), col(0)),
                pl.BlockSpec((near, pp*LANES), col(1)),
                pl.BlockSpec((near, pp*LANES), col(0)),
                pl.BlockSpec((near, pp*LANES), col(1)),
                pl.BlockSpec((BLOCK, LANES), lambda h, i, f: (i, 0)),
                pl.BlockSpec((total, LANES), lambda h, i, f: (0, 0)),
            ],
            out_specs=[
                pl.BlockSpec((BLOCK, pp*LANES), lambda h, i, f: (i, h)),
                pl.BlockSpec((pp, 1, 2*BLOCK, 1), lambda h, i, f: (h, i, 0, 0)),
            ],
            scratch_shapes=[
                pltpu.VMEM((pp, total // BLOCK, 2*BLOCK, BLOCK), F32),
                pltpu.VMEM((pp, 2*BLOCK, LANES), F32),
                pltpu.VMEM((pp, 2*BLOCK, LANES), F32),
                pltpu.VMEM((pp, BLOCK, LANES), F32),
                pltpu.VMEM((total, pp*LANES), BF),
                pltpu.VMEM((total, pp*LANES), BF),
            ]),
        out_shape=[jax.ShapeDtypeStruct((near, width), BF), jax.ShapeDtypeStruct((width // LANES, nq, 2*BLOCK, 1), F32)],
        compiler_params=pltpu.CompilerParams(vmem_limit_bytes=56<<20),
        cost_estimate=pl.CostEstimate(flops=4*near*total*width, bytes_accessed=8*near*width*2, transcendentals=near*total*width//64),
        name="attn_forward",
    )(flags, q, kv, kv, far, far, feat, hot)

def bwd_kernel(near, pp, scale, flags, q_ref, kn_ref, vn_ref, kf_ref, vf_ref, feat_ref, hot_ref, o_ref, do_ref, lse_ref,
               dq_ref, near_ref, far_ref, k_all, v_all, dk_acc, dv_acc, dq_acc):
    qb = pl.program_id(1)
    nk = hot_ref.shape[0] // BLOCK
    safe = flags[flags.shape[0] - 1] == 1
    @pl.when(qb == 0)
    def _():
        k_all[:near] = kn_ref[...]; k_all[near:] = kf_ref[...]
        v_all[:near] = vn_ref[...]; v_all[near:] = vf_ref[...]
        dk_acc[...] = jnp.zeros(dk_acc.shape, F32)
        dv_acc[...] = jnp.zeros(dv_acc.shape, F32)
    feat = feat_ref[...]
    feat2 = jnp.concatenate([feat, feat], axis=0)
    dq_acc[...] = jnp.zeros(dq_acc.shape, F32)
    qs, dos, deltas, lses = [], [], [], []
    for p in range(pp):
        cols = slice(p*LANES, (p+1)*LANES)
        qs.append(split_heads(q_ref[:, cols] * scale))
        do2 = split_heads(do_ref[:, cols])
        dos.append(do2)
        o = o_ref[:, cols].astype(F32)
        deltas.append(lanes_sum(do2.astype(F32) * jnp.concatenate([o, o], axis=0)))
        lses.append(lse_ref[p, 0])
    def sweep(exact):
        def step(j, _):
            @pl.when(flags[qb * nk + j] == 1)
            def _():
                rows = pl.ds(pl.multiple_of(j * BLOCK, BLOCK), BLOCK)
                hot = hot_ref[rows, :]
                for p in range(pp):
                    cols = slice(p*LANES, (p+1)*LANES)
                    k = k_all[rows, cols]; v = v_all[rows, cols]
                    if exact:
                        ok = mm_t(feat2, hot) > -1.0
                        s = jnp.where(ok, mm_t(qs[p], k), MASKED)
                    else:
                        s = mm_t(jnp.concatenate([qs[p], feat2], axis=1), jnp.concatenate([k, hot], axis=1))
                    prob = jnp.exp(s - lses[p])
                    dprob = mm_t(dos[p], v)
                    ds = prob * (dprob - deltas[p])
                    if exact:
                        ds = jnp.where(ok, ds, 0.0)
                    ds = ds.astype(BF)
                    dv_acc[rows, cols] += t_mm(prob.astype(BF), dos[p])
                    dk_acc[rows, cols] += t_mm(ds, qs[p])
                    dq_acc[p] += mm(side_by_side(ds), split_heads(k))
            return 0
        lax.fori_loop(0, nk, step, 0)
    @pl.when(safe)
    def _(): sweep(False)
    @pl.when(jnp.logical_not(safe))
    def _(): sweep(True)
    for p in range(pp):
        dq_ref[:, p*LANES:(p+1)*LANES] = (dq_acc[p] * scale).astype(BF)
    @pl.when(qb == pl.num_programs(1) - 1)
    def _():
        near_ref[0] = dk_acc[:near]
        near_ref[1] = dv_acc[:near]
        far_ref[0] = dk_acc[near:].astype(BF)
        far_ref[1] = dv_acc[near:].astype(BF)

def attn_bwd(q, kv, far, feat, hot, flags, attn, dattn, lse, scale, pp):
    near, width = q.shape
    total = hot.shape[0]
    steps = width // LANES // pp
    nq = near // BLOCK
    col = lambda c: (lambda h, i, f: (0, c * steps + h))
    rowblk = pl.BlockSpec((BLOCK, pp*LANES), lambda h, i, f: (i, h))
    whole = pl.BlockSpec((near, pp*LANES), col(0))
    both = pl.BlockSpec((2, near, pp*LANES), lambda h, i, f: (0, 0, h))
    return pl.pallas_call(
        functools.partial(bwd_kernel, near, pp, scale),
        grid_spec=pltpu.PrefetchScalarGridSpec(
            num_scalar_prefetch=1, grid=(steps, nq),
            in_specs=[
                rowblk,
                pl.BlockSpec((near, pp*LANES), col(0)),
                pl.BlockSpec((near, pp*LANES), col(1)),
                whole,
                pl.BlockSpec((near, pp*LANES), col(1)),
                pl.BlockSpec((BLOCK, LANES), lambda h, i, f: (i, 0)),
                pl.BlockSpec((total, LANES), lambda h, i, f: (0, 0)),
                rowblk, rowblk,
                pl.BlockSpec((pp, 1, 2*BLOCK, 1), lambda h, i, f: (h, i, 0, 0)),
            ],
            out_specs=[rowblk, both, both],
            scratch_shapes=[
                pltpu.VMEM((total, pp*LANES), BF),
                pltpu.VMEM((total, pp*LANES), BF),
                pltpu.VMEM((total, pp*LANES), F32),
                pltpu.VMEM((total, pp*LANES), F32),
                pltpu.VMEM((pp, BLOCK, LANES), F32),
            ]),
        out_shape=[
            jax.ShapeDtypeStruct((near, width), BF),
            jax.ShapeDtypeStruct((2, near, width), F32),
            jax.ShapeDtypeStruct((2, near, width), BF),
        ],
        compiler_params=pltpu.CompilerParams(vmem_limit_bytes=56<<20),
        cost_estimate=pl.CostEstimate(flops=10*near*total*width, bytes_accessed=16*near*width*2, transcendentals=near*total*width//64),
        name="attn_backward",
    )(flags, q, kv, kv, far, far, feat, hot, attn, dattn, lse)


class Links:
    def __init__(self, groups, shards):
        self.groups, self.shards, self.planes = groups, shards, groups // 2
        self.g = lax.axis_index("group")
        self.s = lax.axis_index("shard")
        self.c = self.g % 2
        self.plane = self.g // 2

    def swap(self, value):
        return lax.ppermute(value, "group", [(i, i ^ 1) for i in range(self.groups)])

    def turn(self, value, step):
        n = self.shards
        return lax.ppermute(value, "shard", [(i, (i + step) % n) for i in range(n)])

    def across(self, value, step):
        return lax.ppermute(value, "group", [(i, i ^ (2 * step)) for i in range(self.groups)])

    def round_perm(self, k):
        n, perm = self.shards, []
        for g in range(self.groups):
            for s in range(n):
                d = (s + k) % n
                goal = ((g // 2) * 2 + d % 2, 2 * (d // 2) + g % 2)
                perm.append((g * n + s, goal[0] * n + goal[1]))
        return perm

    def to_trees(self, value):
        batches, rows, width = value.shape
        pieces = value.reshape(batches * 2, rows // 2, width)
        got = []
        for k in range(self.shards):
            piece = lax.dynamic_index_in_dim(pieces, (self.s + k) % self.shards, 0, False)
            got.append(lax.ppermute(piece, ("group", "shard"), self.round_perm(k)))
        return jnp.concatenate(got, axis=0)

    def from_trees(self, value, batches):
        total, width = value.shape
        rows = total // self.shards
        out = jnp.zeros((self.shards, rows, width), value.dtype)
        for k in range(self.shards):
            back = [(b, a) for a, b in self.round_perm(k)]
            piece = lax.ppermute(value[k * rows : (k + 1) * rows], ("group", "shard"), back)
            out = lax.dynamic_update_index_in_dim(out, piece, (self.s + k) % self.shards, 0)
        return out.reshape(batches, 1, 2 * rows, width)

    def line_order(self, parts):
        stacked = jnp.stack(parts)
        return jnp.stack(
            [
                lax.dynamic_index_in_dim(stacked, (self.s - j) % self.shards, 0, False)
                for j in range(self.shards)
            ]
        )

    def line_gather(self, value):
        return self.line_order([value] + [self.turn(value, k) for k in range(1, self.shards)])

    def gather_weight(self, weight):
        rows = weight.shape[0] // self.groups
        part = lax.dynamic_slice_in_dim(weight, self.g * rows, rows, 0)
        return lax.all_gather(part, ("shard", "group"), axis=0, tiled=True)

    def plane_sum(self, value):
        if self.planes != 4:
            groups = [[2 * p + c for p in range(self.planes)] for c in range(2)]
            return lax.psum_scatter(
                value, "group", scatter_dimension=1, axis_index_groups=groups
            ).astype(F32)
        total = lax.dynamic_index_in_dim(value, self.plane, 1, False).astype(F32)
        for k in range(1, 4):
            piece = lax.dynamic_index_in_dim(value, self.plane ^ k, 1, False)
            total = total + self.across(piece, k).astype(F32)
        return total

    def plane_gather(self, value):
        if self.planes != 4:
            groups = [[2 * p + c for p in range(self.planes)] for c in range(2)]
            return lax.all_gather(value, "group", axis_index_groups=groups)
        parts = jnp.stack([value] + [self.across(value, k) for k in range(1, 4)])
        return jnp.stack(
            [lax.dynamic_index_in_dim(parts, self.plane ^ j, 0, False) for j in range(4)]
        )

    def reduce_grad(self, grad):
        width = grad.shape[1]
        rows = grad.shape[0] // self.shards
        halves = grad.reshape(self.shards, 2, rows // 2, width)
        mine = lax.dynamic_index_in_dim(halves, self.c, 1, False)
        yours = lax.dynamic_index_in_dim(halves, 1 - self.c, 1, False)
        pair = (mine.astype(F32) + self.swap(yours).astype(F32)).astype(BF)
        fine = rows // 2 // self.planes
        plane = self.plane_sum(pair.reshape(self.shards, self.planes, fine, width)).astype(BF)
        total = lax.dynamic_index_in_dim(plane, self.s, 0, False).astype(F32)
        for k in range(1, self.shards):
            piece = lax.dynamic_index_in_dim(plane, (self.s + k) % self.shards, 0, False)
            total = total + self.turn(piece, k).astype(F32)
        half = self.plane_gather(total.astype(BF)).reshape(rows // 2, width)
        other = self.swap(half)
        out = jnp.where(
            self.c == 0, jnp.concatenate([half, other]), jnp.concatenate([other, half])
        )
        return out.astype(F32)

    def tree_sums(self, vec):
        line = self.line_gather(vec)
        return line + self.swap(line)


def on_device(
    tokens,
    cond,
    seg_ids,
    parents,
    cotangent,
    w_qkv,
    w_out,
    w_fc1,
    b_fc1,
    w_fc2,
    b_fc2,
    w_ada,
    b_ada,
    gain1,
    gain2,
    groups,
):
    batches, _, row_count, width = tokens.shape
    shards = lax.axis_size("shard")
    assert shards == 2 * batches and groups % 2 == 0
    head_dim = width // HEADS
    scale = 1.0 / math.sqrt(head_dim)
    net = Links(groups, shards)
    rows = row_count // 2
    mine = shards * rows
    tree_len = seg_ids.shape[2]
    labels = parents.shape[2]
    cond_dim = cond.shape[2]

    qkv_w = net.gather_weight(w_qkv)
    tok = net.to_trees(tokens[:, 0])
    out_w = net.gather_weight(w_out)
    fc1_w = net.gather_weight(w_fc1)
    fc2_w = net.gather_weight(w_fc2)
    grad_out = net.to_trees(cotangent[:, 0])

    packed = jnp.concatenate(
        [seg_ids[:, 0].astype(F32), parents[:, 0].astype(F32), cond[:, 0]], axis=1
    )
    other = net.swap(packed)
    trees = jnp.where(
        net.c == 0, jnp.stack([packed, other], axis=1), jnp.stack([other, packed], axis=1)
    ).reshape(shards, packed.shape[1])
    conds = trees[:, tree_len + labels :]
    my_tree = lax.dynamic_index_in_dim(trees, net.s, 0, False)
    tree_seg = my_tree[:tree_len]
    parent_row = my_tree[tree_len : tree_len + labels]
    ada_rows = jnp.dot(conds, w_ada.astype(F32), precision=HIGH) + b_ada.astype(F32)
    small = jnp.concatenate([b_fc1, b_fc2, gain1, gain2]).astype(F32)
    pieces = jnp.concatenate(
        [ada_rows, jnp.broadcast_to(small[None], (shards, small.shape[0]))], axis=1
    )
    got = [lax.dynamic_index_in_dim(pieces, net.s, 0, False)]
    for k in range(1, shards):
        piece = lax.dynamic_index_in_dim(pieces, (net.s + k) % shards, 0, False)
        got.append(net.turn(piece, k))
    line = net.line_order(got)
    cut = ada_rows.shape[1]
    ada = line[:, :cut].reshape(-1)
    ends = [cut]
    for vec in (b_fc1, b_fc2, gain1, gain2):
        ends.append(ends[-1] + vec.shape[0])
    fc1_b, fc2_b, gain_a, gain_b = (
        line[:, ends[i] : ends[i + 1]].reshape(-1) for i in range(4)
    )
    shift_one, scale_one, gate_one, shift_two, scale_two, gate_two = jnp.split(ada, 6)

    half_seg = tree_seg.reshape(shards, 2, rows)
    base = 2 * (net.s // 2)

    def row_segs(place):
        take = lax.dynamic_index_in_dim(half_seg, place, 1, False)
        return jnp.concatenate(
            [
                lax.dynamic_index_in_dim(take, (base + place - k) % shards, 0, False)
                for k in range(shards)
            ]
        )

    query_seg = row_segs(net.c)
    key_seg = jnp.concatenate([query_seg, row_segs(1 - net.c)])
    lanes = jnp.arange(LANES, dtype=F32)
    table = jnp.zeros((LANES,), F32).at[:labels].set(parent_row)
    up_two = jnp.sum(jnp.where(table[:, None] == lanes[None, :], table[None, :], 0.0), axis=1)
    reach = (
        (lanes[:, None] == lanes[None, :])
        | (table[:, None] == lanes[None, :])
        | (up_two[:, None] == lanes[None, :])
    )
    hot = (key_seg[:, None] == lanes[None, :]).astype(BF)
    feat = mm(hot[:mine], jnp.where(reach, 0.0, BIG).astype(BF)).astype(BF)
    held = jnp.max(hot.reshape(-1, BLOCK, LANES), axis=1)
    wanted = mm(held[: mine // BLOCK], reach.astype(BF)).astype(BF)
    active = mm_t(wanted, held) > 0.5

    tok_f = tok.astype(F32)
    normed_one, inv_one = layer_norm(tok_f)
    lifted_one = normed_one * gain_a
    act_one = (lifted_one * (1.0 + scale_one) + shift_one).astype(BF)
    kv = mm(act_one, qkv_w[:, width:]).astype(BF)
    far = net.swap(kv)
    query = mm(act_one, qkv_w[:, :width]).astype(BF)
    bound = jnp.maximum(jnp.max(jnp.abs(query)), jnp.max(jnp.abs(kv))).astype(F32)
    other_bound = jnp.maximum(bound, jnp.max(jnp.abs(far)).astype(F32))
    safe = bound * other_bound * (head_dim * scale) < 2.0**27
    flags = jnp.concatenate(
        [(active | ~safe).reshape(-1), safe[None]]
    ).astype(jnp.int32)
    attn, log_totals = attn_fwd(query, kv, far, feat, hot, flags, scale, PAIRS)
    branch_one = mm(attn, out_w)
    middle = tok_f + gate_one * branch_one
    normed_two, inv_two = layer_norm(middle)
    lifted_two = normed_two * gain_b
    act_two = (lifted_two * (1.0 + scale_two) + shift_two).astype(BF)
    pre_act = mm(act_two, fc1_w) + fc1_b
    gelu_value, gelu_slope = gelu_parts(pre_act)
    hidden = gelu_value.astype(BF)
    branch_two = mm(hidden, fc2_w) + fc2_b
    out = net.from_trees((middle + gate_two * branch_two).astype(BF), batches)

    grad_f = grad_out.astype(F32)
    grad_y2 = (grad_f * gate_two).astype(BF)
    d_gate_two = jnp.sum(grad_f * branch_two, axis=0)
    t_fc2 = net.reduce_grad(t_mm(hidden, grad_y2).astype(BF))
    g_b2 = jnp.sum(grad_y2.astype(F32), axis=0)
    grad_pre = (mm_t(grad_y2, fc2_w) * gelu_slope).astype(BF)
    t_fc1 = net.reduce_grad(t_mm(act_two, grad_pre).astype(BF))
    g_b1 = jnp.sum(grad_pre.astype(F32), axis=0)
    grad_a2 = mm_t(grad_pre, fc1_w)
    d_shift_two = jnp.sum(grad_a2, axis=0)
    d_scale_two = jnp.sum(grad_a2 * lifted_two, axis=0)
    grad_h2 = grad_a2 * (1.0 + scale_two)
    g_gain2 = jnp.sum(grad_h2 * normed_two, axis=0)
    grad_mid = grad_f + norm_back(grad_h2 * gain_b, normed_two, inv_two)
    grad_y1 = (grad_mid * gate_one).astype(BF)
    d_gate_one = jnp.sum(grad_mid * branch_one, axis=0)
    t_out = net.reduce_grad(t_mm(attn, grad_y1).astype(BF))
    grad_attn = mm_t(grad_y1, out_w).astype(BF)
    q_grads, near_grads, far_grads = attn_bwd(
        query, kv, far, feat, hot, flags, attn, grad_attn, log_totals, scale, PAIRS
    )
    kv_grads = (near_grads + net.swap(far_grads).astype(F32)).astype(BF)
    grad_qkv = jnp.concatenate([q_grads, kv_grads[0], kv_grads[1]], axis=1)
    t_qkv = net.reduce_grad(t_mm(act_one, grad_qkv).astype(BF))
    grad_a1 = mm_t(grad_qkv, qkv_w)
    d_shift_one = jnp.sum(grad_a1, axis=0)
    d_scale_one = jnp.sum(grad_a1 * lifted_one, axis=0)
    grad_h1 = grad_a1 * (1.0 + scale_one)
    g_gain1 = jnp.sum(grad_h1 * normed_one, axis=0)
    grad_in = grad_mid + norm_back(grad_h1 * gain_a, normed_one, inv_one)
    grads_x = net.from_trees(grad_in.astype(BF), batches)

    early = net.tree_sums(
        jnp.concatenate([d_gate_one, d_shift_two, d_scale_two, d_gate_two, g_gain2, g_b2, g_b1])
    )
    late = net.tree_sums(jnp.concatenate([d_shift_one, d_scale_one, g_gain1]))
    dada = jnp.concatenate([late[:, : 2 * width], early[:, : 4 * width]], axis=1)
    bias = jnp.concatenate([early[:, 4 * width :], late[:, 2 * width :]], axis=1)
    everyone = net.plane_gather(
        jnp.concatenate([dada, conds, jnp.broadcast_to(jnp.sum(bias, axis=0), bias.shape)], axis=1)
    )
    every_dada = everyone[:, :, : 6 * width].reshape(-1, 6 * width)
    every_cond = everyone[:, :, 6 * width : 6 * width + cond_dim].reshape(-1, cond_dim)
    sums = jnp.sum(everyone[:, 0, 6 * width + cond_dim :], axis=0)

    def place(vec):
        n = vec.shape[-1] // shards
        return lax.dynamic_slice_in_dim(vec, net.s * n, n, vec.ndim - 1)

    dada_here = place(every_dada)
    t_ada = lax.dot_general(
        every_cond, dada_here, (((0,), (0,)), ((), ())), precision=HIGH
    )
    t_bada = jnp.sum(dada_here, axis=0)
    g_two, g_bias2, g_bias1, g_one = jnp.split(
        sums, [width, 2 * width, 2 * width + 4 * width]
    )
    own = lax.dynamic_index_in_dim(
        place(dada).reshape(batches, 2, -1), net.c, 1, False
    )
    cond_part = lax.dot_general(
        own, w_ada.astype(F32), (((1,), (1,)), ((), ())), precision=HIGH
    )
    cond_total = cond_part
    for k in range(1, shards):
        cond_total = cond_total + net.turn(cond_part, k)
    return (
        out,
        grads_x,
        cond_total[:, None, :],
        t_qkv,
        t_out,
        t_fc1,
        place(g_bias1),
        t_fc2,
        place(g_bias2),
        t_ada,
        t_bada,
        place(g_one),
        place(g_two),
    )


def solution(mesh):
    in_specs = (
        P(None, "group", "shard", None),
        P(None, "group", None),
        P(None, "group", None),
        P(None, "group", None),
        P(None, "group", "shard", None),
        P("shard", None),
        P("shard", None),
        P("shard", None),
        P("shard"),
        P("shard", None),
        P("shard"),
        P(None, "shard"),
        P("shard"),
        P("shard"),
        P("shard"),
    )
    out_specs = (
        P(None, "group", "shard", None),
        P(None, "group", "shard", None),
        P(None, "group", None),
        P("shard", None),
        P("shard", None),
        P("shard", None),
        P("shard"),
        P("shard", None),
        P("shard"),
        P(None, "shard"),
        P("shard"),
        P("shard"),
        P("shard"),
    )
    groups = mesh.shape["group"]

    def run(*args):
        return on_device(*args, groups)

    return jax.shard_map(
        run, mesh=mesh, in_specs=in_specs, out_specs=out_specs, check_vma=False
    )
```

```python
import functools
import math

import jax
import jax.numpy as jnp
from jax import lax
from jax.experimental import pallas as pl
from jax.experimental.pallas import tpu as pltpu
from jax.sharding import PartitionSpec as P

HEADS = 12
EPS = 1e-05
GELU_C = 0.7978845608028654
GELU_K = 0.044715
HIGH = lax.Precision.HIGHEST
BF = jnp.bfloat16
F32 = jnp.float32
BLOCK = 256
LANES = 128
BIG = -float(2**30)
MASKED = -1000000000.0
PAIRS = 6


def layer_norm(values):
    centred = values - jnp.mean(values, axis=-1, keepdims=True)
    inv_std = lax.rsqrt(jnp.mean(centred * centred, axis=-1, keepdims=True) + EPS)
    return centred * inv_std, inv_std


def norm_back(grad_normed, normed, inv_std):
    first_mean = jnp.mean(grad_normed, axis=-1, keepdims=True)
    second = jnp.mean(grad_normed * normed, axis=-1, keepdims=True)
    return (grad_normed - first_mean - normed * second) * inv_std


def gelu_parts(pre_act):
    inner_arg = GELU_C * (pre_act + GELU_K * pre_act * pre_act * pre_act)
    tangent = jnp.tanh(inner_arg)
    gelu_value = 0.5 * pre_act * (1.0 + tangent)
    gelu_slope = 0.5 * (1.0 + tangent) + 0.5 * pre_act * (1.0 - tangent * tangent) * GELU_C * (
        1.0 + 3.0 * GELU_K * pre_act * pre_act
    )
    return gelu_value, gelu_slope


def mm(left, right):
    return jnp.dot(left, right, preferred_element_type=F32)


def mm_t(left, right):
    return lax.dot_general(left, right, (((1,), (1,)), ((), ())), preferred_element_type=F32)


def t_mm(left, right):
    return lax.dot_general(left, right, (((0,), (0,)), ((), ())), preferred_element_type=F32)


def split_heads(pair):
    first = lax.broadcasted_iota(jnp.int32, pair.shape, 1) < LANES // 2
    zero = jnp.zeros_like(pair)
    return jnp.concatenate([jnp.where(first, pair, zero), jnp.where(first, zero, pair)], axis=0)

def side_by_side(stack):
    n = stack.shape[0] // 2
    return jnp.concatenate([stack[:n], stack[n:]], axis=1)

def lanes_sum(x): return jnp.sum(x, axis=1, keepdims=True)

def fwd_kernel(near, pp, scale, flags, q_ref, kn_ref, vn_ref, kf_ref, vf_ref, feat_ref, hot_ref, o_ref, lse_ref,
               s_ref, m_ref, l_ref, acc_ref, k_all, v_all):
    qb = pl.program_id(1)
    nk = hot_ref.shape[0] // BLOCK
    safe = flags[flags.shape[0] - 1] == 1
    @pl.when(qb == 0)
    def _():
        k_all[:near] = kn_ref[...]; k_all[near:] = kf_ref[...]
        v_all[:near] = vn_ref[...]; v_all[near:] = vf_ref[...]
    feat = feat_ref[...]
    feat2 = jnp.concatenate([feat, feat], axis=0)
    qs = [split_heads(q_ref[:, p*LANES:(p+1)*LANES] * scale) for p in range(pp)]
    m_ref[...] = jnp.full(m_ref.shape, -jnp.inf, F32)
    def scan_scores(exact):
        def step(j, _):
            @pl.when(flags[qb * nk + j] == 1)
            def _():
                rows = pl.ds(pl.multiple_of(j * BLOCK, BLOCK), BLOCK)
                hot = hot_ref[rows, :]
                for p in range(pp):
                    k = k_all[rows, p*LANES:(p+1)*LANES]
                    if exact:
                        ok = mm_t(feat2, hot) > -1.0
                        s = jnp.where(ok, mm_t(qs[p], k), MASKED)
                    else:
                        s = mm_t(jnp.concatenate([qs[p], feat2], axis=1), jnp.concatenate([k, hot], axis=1))
                    s_ref[p, j] = s
                    m_ref[p] = jnp.maximum(m_ref[p], jnp.maximum(s[:, :LANES], s[:, LANES:]))
            return 0
        lax.fori_loop(0, nk, step, 0)
    @pl.when(safe)
    def _(): scan_scores(False)
    @pl.when(jnp.logical_not(safe))
    def _(): scan_scores(True)
    tops = [jnp.max(m_ref[p], axis=1, keepdims=True) for p in range(pp)]
    l_ref[...] = jnp.zeros(l_ref.shape, F32)
    acc_ref[...] = jnp.zeros(acc_ref.shape, F32)
    def step(j, _):
        @pl.when(flags[qb * nk + j] == 1)
        def _():
            rows = pl.ds(pl.multiple_of(j * BLOCK, BLOCK), BLOCK)
            for p in range(pp):
                e = jnp.exp(s_ref[p, j] - tops[p])
                l_ref[p] += e[:, :LANES] + e[:, LANES:]
                v = split_heads(v_all[rows, p*LANES:(p+1)*LANES])
                acc_ref[p] += mm(side_by_side(e.astype(BF)), v)
        return 0
    lax.fori_loop(0, nk, step, 0)
    for p in range(pp):
        total = lanes_sum(l_ref[p])
        lse_ref[p, 0] = tops[p] + jnp.log(total)
        first = lax.broadcasted_iota(jnp.int32, (BLOCK, LANES), 1) < LANES // 2
        o_ref[:, p*LANES:(p+1)*LANES] = (acc_ref[p] / jnp.where(first, total[:BLOCK], total[BLOCK:])).astype(BF)

def attn_fwd(q, kv, far, feat, hot, flags, scale, pp):
    near, width = q.shape
    total = hot.shape[0]
    steps = width // LANES // pp
    nq = near // BLOCK
    col = lambda c: (lambda h, i, f: (0, c * steps + h))
    return pl.pallas_call(
        functools.partial(fwd_kernel, near, pp, scale),
        grid_spec=pltpu.PrefetchScalarGridSpec(
            num_scalar_prefetch=1, grid=(steps, nq),
            in_specs=[
                pl.BlockSpec((BLOCK, pp*LANES), lambda h, i, f: (i, h)),
                pl.BlockSpec((near, pp*LANES), col(0)),
                pl.BlockSpec((near, pp*LANES), col(1)),
                pl.BlockSpec((near, pp*LANES), col(0)),
                pl.BlockSpec((near, pp*LANES), col(1)),
                pl.BlockSpec((BLOCK, LANES), lambda h, i, f: (i, 0)),
                pl.BlockSpec((total, LANES), lambda h, i, f: (0, 0)),
            ],
            out_specs=[
                pl.BlockSpec((BLOCK, pp*LANES), lambda h, i, f: (i, h)),
                pl.BlockSpec((pp, 1, 2*BLOCK, 1), lambda h, i, f: (h, i, 0, 0)),
            ],
            scratch_shapes=[
                pltpu.VMEM((pp, total // BLOCK, 2*BLOCK, BLOCK), F32),
                pltpu.VMEM((pp, 2*BLOCK, LANES), F32),
                pltpu.VMEM((pp, 2*BLOCK, LANES), F32),
                pltpu.VMEM((pp, BLOCK, LANES), F32),
                pltpu.VMEM((total, pp*LANES), BF),
                pltpu.VMEM((total, pp*LANES), BF),
            ]),
        out_shape=[jax.ShapeDtypeStruct((near, width), BF), jax.ShapeDtypeStruct((width // LANES, nq, 2*BLOCK, 1), F32)],
        compiler_params=pltpu.CompilerParams(vmem_limit_bytes=56<<20),
        cost_estimate=cost(41),
        name="attn_forward",
    )(flags, q, kv, kv, far, far, feat, hot)

def bwd_kernel(near, pp, scale, flags, q_ref, kn_ref, vn_ref, kf_ref, vf_ref, feat_ref, hot_ref, o_ref, do_ref, lse_ref,
               dq_ref, near_ref, far_ref, k_all, v_all, dk_acc, dv_acc, dq_acc):
    qb = pl.program_id(1)
    nk = hot_ref.shape[0] // BLOCK
    safe = flags[flags.shape[0] - 1] == 1
    @pl.when(qb == 0)
    def _():
        k_all[:near] = kn_ref[...]; k_all[near:] = kf_ref[...]
        v_all[:near] = vn_ref[...]; v_all[near:] = vf_ref[...]
        dk_acc[...] = jnp.zeros(dk_acc.shape, F32)
        dv_acc[...] = jnp.zeros(dv_acc.shape, F32)
    feat = feat_ref[...]
    feat2 = jnp.concatenate([feat, feat], axis=0)
    dq_acc[...] = jnp.zeros(dq_acc.shape, F32)
    qs, dos, deltas, lses = [], [], [], []
    for p in range(pp):
        cols = slice(p*LANES, (p+1)*LANES)
        qs.append(split_heads(q_ref[:, cols] * scale))
        do2 = split_heads(do_ref[:, cols])
        dos.append(do2)
        o = o_ref[:, cols].astype(F32)
        deltas.append(lanes_sum(do2.astype(F32) * jnp.concatenate([o, o], axis=0)))
        lses.append(lse_ref[p, 0])
    def sweep(exact):
        def step(j, _):
            @pl.when(flags[qb * nk + j] == 1)
            def _():
                rows = pl.ds(pl.multiple_of(j * BLOCK, BLOCK), BLOCK)
                hot = hot_ref[rows, :]
                for p in range(pp):
                    cols = slice(p*LANES, (p+1)*LANES)
                    k = k_all[rows, cols]; v = v_all[rows, cols]
                    if exact:
                        ok = mm_t(feat2, hot) > -1.0
                        s = jnp.where(ok, mm_t(qs[p], k), MASKED)
                    else:
                        s = mm_t(jnp.concatenate([qs[p], feat2], axis=1), jnp.concatenate([k, hot], axis=1))
                    prob = jnp.exp(s - lses[p])
                    dprob = mm_t(dos[p], v)
                    ds = prob * (dprob - deltas[p])
                    if exact:
                        ds = jnp.where(ok, ds, 0.0)
                    ds = ds.astype(BF)
                    dv_acc[rows, cols] += t_mm(prob.astype(BF), dos[p])
                    dk_acc[rows, cols] += t_mm(ds, qs[p])
                    dq_acc[p] += mm(side_by_side(ds), split_heads(k))
            return 0
        lax.fori_loop(0, nk, step, 0)
    @pl.when(safe)
    def _(): sweep(False)
    @pl.when(jnp.logical_not(safe))
    def _(): sweep(True)
    for p in range(pp):
        dq_ref[:, p*LANES:(p+1)*LANES] = (dq_acc[p] * scale).astype(BF)
    @pl.when(qb == pl.num_programs(1) - 1)
    def _():
        near_ref[0] = dk_acc[:near]
        near_ref[1] = dv_acc[:near]
        far_ref[0] = dk_acc[near:].astype(BF)
        far_ref[1] = dv_acc[near:].astype(BF)

def attn_bwd(q, kv, far, feat, hot, flags, attn, dattn, lse, scale, pp):
    near, width = q.shape
    total = hot.shape[0]
    steps = width // LANES // pp
    nq = near // BLOCK
    col = lambda c: (lambda h, i, f: (0, c * steps + h))
    rowblk = pl.BlockSpec((BLOCK, pp*LANES), lambda h, i, f: (i, h))
    whole = pl.BlockSpec((near, pp*LANES), col(0))
    both = pl.BlockSpec((2, near, pp*LANES), lambda h, i, f: (0, 0, h))
    return pl.pallas_call(
        functools.partial(bwd_kernel, near, pp, scale),
        grid_spec=pltpu.PrefetchScalarGridSpec(
            num_scalar_prefetch=1, grid=(steps, nq),
            in_specs=[
                rowblk,
                pl.BlockSpec((near, pp*LANES), col(0)),
                pl.BlockSpec((near, pp*LANES), col(1)),
                whole,
                pl.BlockSpec((near, pp*LANES), col(1)),
                pl.BlockSpec((BLOCK, LANES), lambda h, i, f: (i, 0)),
                pl.BlockSpec((total, LANES), lambda h, i, f: (0, 0)),
                rowblk, rowblk,
                pl.BlockSpec((pp, 1, 2*BLOCK, 1), lambda h, i, f: (h, i, 0, 0)),
            ],
            out_specs=[rowblk, both, both],
            scratch_shapes=[
                pltpu.VMEM((total, pp*LANES), BF),
                pltpu.VMEM((total, pp*LANES), BF),
                pltpu.VMEM((total, pp*LANES), F32),
                pltpu.VMEM((total, pp*LANES), F32),
                pltpu.VMEM((pp, BLOCK, LANES), F32),
            ]),
        out_shape=[
            jax.ShapeDtypeStruct((near, width), BF),
            jax.ShapeDtypeStruct((2, near, width), F32),
            jax.ShapeDtypeStruct((2, near, width), BF),
        ],
        compiler_params=pltpu.CompilerParams(vmem_limit_bytes=56<<20),
        cost_estimate=cost(81),
        name="attn_backward",
    )(flags, q, kv, kv, far, far, feat, hot, attn, dattn, lse)


def assemble_kernel(shards, where, own_ref, half_ref, other_ref, out_ref):
    s, c, plane = where[0], where[1], where[2]
    out_ref[pl.ds(s * 8, 8)] = own_ref[...]
    for side, source in ((c, half_ref), (1 - c, other_ref)):
        for j in range(4):
            for k in range(1, shards):
                place = lax.rem(s + shards - k, shards)
                out_ref[place * 8 + side * 4 + (plane ^ j)] = source[j, k - 1]


def assemble(where, own, half, other, shards):
    rows, width = own.shape
    fine = rows // 8
    full = lambda *shape: pl.BlockSpec(shape, lambda i, w: (0,) * len(shape))
    out = pl.pallas_call(
        functools.partial(assemble_kernel, shards),
        grid_spec=pltpu.PrefetchScalarGridSpec(
            num_scalar_prefetch=1,
            grid=(1,),
            in_specs=[full(8, fine, width), full(*half.shape), full(*half.shape)],
            out_specs=full(8 * shards, fine, width),
        ),
        out_shape=jax.ShapeDtypeStruct((8 * shards, fine, width), own.dtype),
        compiler_params=pltpu.CompilerParams(vmem_limit_bytes=40 << 20),
        name="assemble",
    )(where, own.reshape(8, fine, width), half, other)
    return out.reshape(shards * rows, width)


def entry_kernel(pieces, *refs):
    parts, (vec_ref, w_ref, tok_ref, act_ref, q_ref, kv_ref, peak_ref) = refs[:pieces], refs[pieces:]
    step = pl.program_id(0)
    rows = parts[0].shape[0]

    @pl.when(step == 0)
    def _():
        gain, lift, shift = (vec_ref[i : i + 1, :] for i in range(3))
        for i, part in enumerate(parts):
            at = slice(i * rows, (i + 1) * rows)
            tok_ref[at, :] = part[...]
            normed, _unused = layer_norm(part[...].astype(F32))
            act_ref[at, :] = (normed * gain * lift + shift).astype(BF)
        peak_ref[...] = jnp.zeros_like(peak_ref)

    top = jnp.zeros((1, w_ref.shape[1]), F32)
    for i in range(pieces):
        at = slice(i * rows, (i + 1) * rows)
        value = mm(act_ref[at, :], w_ref[...])
        low = value.astype(BF)
        top = jnp.maximum(top, jnp.max(jnp.abs(low.astype(F32)), axis=0, keepdims=True))

        @pl.when(step < 2)
        def _():
            kv_ref[at, :] = low

        @pl.when(step == 2)
        def _():
            q_ref[at, :] = low

    peak_ref[0:1, :] = jnp.maximum(peak_ref[0:1, :], top)


def entry(parts, vec, qkv_w):
    rows, width = parts[0].shape
    total = rows * len(parts)
    fixed = lambda *shape: pl.BlockSpec(shape, lambda j: (0,) * len(shape))
    return pl.pallas_call(
        functools.partial(entry_kernel, len(parts)),
        grid=(3,),
        in_specs=[fixed(rows, width)] * len(parts)
        + [fixed(8, width), pl.BlockSpec((width, width), lambda j: (0, lax.rem(j + 1, 3)))],
        out_specs=[
            fixed(total, width), fixed(total, width), fixed(total, width),
            pl.BlockSpec((total, width), lambda j: (0, jnp.minimum(j, 1))),
            fixed(8, width),
        ],
        out_shape=[
            jax.ShapeDtypeStruct((total, width), BF),
            jax.ShapeDtypeStruct((total, width), BF),
            jax.ShapeDtypeStruct((total, width), BF),
            jax.ShapeDtypeStruct((total, 2 * width), BF),
            jax.ShapeDtypeStruct((8, width), F32),
        ],
        compiler_params=pltpu.CompilerParams(vmem_limit_bytes=48 << 20),
        cost_estimate=cost(9),
        name="entry",
    )(*parts, vec, qkv_w)


def leave_kernel(spots, where, dq_ref, near_ref, far_ref, act_ref, w_ref, tok_ref, dmid_ref, vec_ref,
                 grad_ref, g_ref, sums_ref, d_all, da):
    step = pl.program_id(0)
    total = dq_ref.shape[0]
    sides, planes, places, fine = spots

    @pl.when(step == 0)
    def _():
        d_all[...] = dq_ref[...]
        da[...] = jnp.zeros_like(da)

    @pl.when(step > 0)
    def _():
        d_all[...] = (near_ref[0] + far_ref[0].astype(F32)).astype(BF)

    grad = t_mm(act_ref[...], d_all[...])
    for place in range(places):
        turned = lax.rem(place + places - where[0], places)
        for side in range(sides):
            for plane in range(planes):
                start = ((place * sides + side) * planes + plane) * fine
                g_ref[side ^ where[1], plane ^ where[2], turned] = grad[start : start + fine].astype(BF)

    def add(r, _):
        rows = pl.ds(pl.multiple_of(r * BLOCK, BLOCK), BLOCK)
        da[rows, :] += mm_t(d_all[rows, :], w_ref[...])
        return 0

    lax.fori_loop(0, total // BLOCK, add, 0)

    @pl.when(step == 2)
    def _():
        gain, lift, shift = (vec_ref[i : i + 1, :] for i in range(3))
        sums_ref[...] = jnp.zeros_like(sums_ref)

        def finish(r, _):
            rows = pl.ds(pl.multiple_of(r * BLOCK, BLOCK), BLOCK)
            normed, inv = layer_norm(tok_ref[rows, :].astype(F32))
            part = da[rows, :]
            grad_h = part * lift
            back = norm_back(grad_h * gain, normed, inv)
            grad_ref[rows, :] = (dmid_ref[rows, :] + back).astype(BF)
            for i, term in enumerate((part, part * (normed * gain), grad_h * normed)):
                sums_ref[i : i + 1, :] += jnp.sum(term, axis=0, keepdims=True)
            return 0

        lax.fori_loop(0, total // BLOCK, finish, 0)


def leave(where, q_grads, near, far, act, qkv_w, tok, dmid, vec, spots):
    total, width = q_grads.shape
    keep = pl.Buffered(1)
    whole = pl.BlockSpec((total, width), lambda j, w: (0, 0), pipeline_mode=keep)
    both = pl.BlockSpec((1, total, width), lambda j, w: (jnp.maximum(j - 1, 0), 0, 0))
    small = pl.BlockSpec((8, width), lambda j, w: (0, 0))
    return pl.pallas_call(
        functools.partial(leave_kernel, spots),
        grid_spec=pltpu.PrefetchScalarGridSpec(
            num_scalar_prefetch=1,
            grid=(3,),
            in_specs=[
                whole, both, both, whole,
                pl.BlockSpec((width, width), lambda j, w: (0, j)),
                whole, whole, small,
            ],
            out_specs=[
                whole,
                pl.BlockSpec(tuple(spots) + (width,), lambda j, w: (0, 0, 0, 0, j)),
                small,
            ],
            scratch_shapes=[pltpu.VMEM((total, width), BF), pltpu.VMEM((total, width), F32)],
        ),
        out_shape=[
            jax.ShapeDtypeStruct((total, width), BF),
            jax.ShapeDtypeStruct(tuple(spots) + (3 * width,), BF),
            jax.ShapeDtypeStruct((8, width), F32),
        ],
        compiler_params=pltpu.CompilerParams(vmem_limit_bytes=56 << 20),
        cost_estimate=cost(14),
        name="leave",
    )(where, q_grads, near, far, act, qkv_w, tok, dmid, vec)


def settle_kernel(where, half_ref, other_ref, out_ref):
    c, plane = where[1], where[2]
    for side, source in ((c, half_ref), (1 - c, other_ref)):
        for j in range(half_ref.shape[0]):
            out_ref[side * half_ref.shape[0] + (plane ^ j)] = source[j].astype(F32)


def settle(where, half, other):
    planes, fine, width = half.shape
    full = lambda *shape: pl.BlockSpec(shape, lambda i, w: (0,) * len(shape))
    return pl.pallas_call(
        settle_kernel,
        grid_spec=pltpu.PrefetchScalarGridSpec(
            num_scalar_prefetch=1,
            grid=(1,),
            in_specs=[full(planes, fine, width)] * 2,
            out_specs=full(2 * planes, fine, width),
        ),
        out_shape=jax.ShapeDtypeStruct((2 * planes, fine, width), F32),
        compiler_params=pltpu.CompilerParams(vmem_limit_bytes=40 << 20),
        name="settle",
    )(where, half, other)


def unpack_kernel(count, in_ref, *outs):
    step = pl.program_id(0)
    out_ref, fc1_ref, fc2_ref = outs

    @pl.when(step == 0)
    def _():
        out_ref[...] = in_ref[...].astype(F32)

    @pl.when((step > 0) & (step <= count))
    def _():
        fc1_ref[...] = in_ref[...].astype(F32)

    @pl.when(step > count)
    def _():
        rows = fc2_ref.shape[2]
        for g in range(fc2_ref.shape[0]):
            fc2_ref[g, 0] = in_ref[g * rows : (g + 1) * rows, :].astype(F32)


def unpack(sums, groups, width):
    rows = sums.shape[0]
    count = sums.shape[1] // width // 2
    fine = rows // groups
    out, fc1, fc2 = pl.pallas_call(
        functools.partial(unpack_kernel, count),
        grid=(1 + 2 * count,),
        in_specs=[pl.BlockSpec((rows, width), lambda i: (0, i))],
        out_specs=[
            pl.BlockSpec((rows, width), lambda i: (0, 0)),
            pl.BlockSpec((rows, width), lambda i: (0, jnp.clip(i - 1, 0, count - 1))),
            pl.BlockSpec(
                (groups, 1, fine, width), lambda i: (0, jnp.clip(i - 1 - count, 0, count - 1), 0, 0)
            ),
        ],
        out_shape=[
            jax.ShapeDtypeStruct((rows, width), F32),
            jax.ShapeDtypeStruct((rows, count * width), F32),
            jax.ShapeDtypeStruct((groups, count, fine, width), F32),
        ],
        name="unpack",
    )(sums)
    return out, fc1, fc2.reshape(-1, width)


def cost(microseconds):
    return pl.CostEstimate(
        flops=int(microseconds * 1.15e9), bytes_accessed=1 << 20, transcendentals=0
    )


def middle_kernel(chunks, pieces, attn_ref, tok_ref, vec_ref, b1_ref, wo_ref, w1_ref, *rest):
    w2_refs, rest = rest[:chunks], rest[chunks:]
    cot_parts, rest = rest[:pieces], rest[pieces:]
    (out_ref, dattn_ref, dmid_ref, grads_ref, sums_ref, gb1_ref) = rest[:6]
    (mid, branch, act, dy, two, da, hid, dpre, w2, cot_ref, wide, tall, sems) = rest[6:]
    width = attn_ref.shape[1]

    def send_wide(column):
        cols = pl.ds(pl.multiple_of(column * width, LANES), width)
        return pltpu.make_async_copy(wide, grads_ref.at[:, :, :, cols], sems.at[0])

    def send_tall(place):
        cols = pl.ds((1 + chunks) * width, chunks * width)
        return pltpu.make_async_copy(tall, grads_ref.at[:, place, :, cols], sems.at[1])

    step = pl.program_id(0)
    total = attn_ref.shape[0]
    blocks = total // BLOCK
    gate_one, gain, lift, shift, gate_two, fc2_b = (vec_ref[i : i + 1, :] for i in range(6))

    def rows_of(r):
        return pl.ds(pl.multiple_of(r * BLOCK, BLOCK), BLOCK)

    @pl.when(step == 0)
    def _():
        sums_ref[...] = jnp.zeros_like(sums_ref)
        for i, part in enumerate(cot_parts):
            cot_ref[i * part.shape[0] : (i + 1) * part.shape[0], :] = part[...]

        def start(r, _):
            rows = rows_of(r)
            one = mm(attn_ref[rows, :], wo_ref[...])
            middle = tok_ref[rows, :].astype(F32) + gate_one * one
            normed, _unused = layer_norm(middle)
            branch[rows, :] = one
            mid[rows, :] = middle
            act[rows, :] = (normed * gain * lift + shift).astype(BF)
            dy[rows, :] = (cot_ref[rows, :].astype(F32) * gate_two).astype(BF)
            two[rows, :] = jnp.zeros((BLOCK, two.shape[1]), F32)
            da[rows, :] = jnp.zeros((BLOCK, da.shape[1]), F32)
            return 0

        lax.fori_loop(0, blocks, start, 0)

    @pl.when(step < chunks)
    def _():
        height = w2_refs[0].shape[0]
        for b in range(chunks):
            w2[b * height : (b + 1) * height, :] = w2_refs[b][...]
        gb1_ref[...] = jnp.zeros_like(gb1_ref)

        def chunk(r, _):
            rows = rows_of(r)
            value, slope = gelu_parts(mm(act[rows, :], w1_ref[...]) + b1_ref[...])
            hidden = value.astype(BF)
            hid[rows, :] = hidden
            two[rows, :] += mm(hidden, w2[...])
            grad = (mm_t(dy[rows, :], w2[...]) * slope).astype(BF)
            dpre[rows, :] = grad
            gb1_ref[...] += jnp.sum(grad.astype(F32), axis=0, keepdims=True)
            da[rows, :] += mm_t(grad, w1_ref[...])
            return 0

        lax.fori_loop(0, blocks, chunk, 0)
        grad_two = t_mm(hid[...], dy[...])
        grad_one = t_mm(act[...], dpre[...])

        @pl.when(step > 0)
        def _():
            send_wide(step).wait()
            send_tall(step - 1).wait()

        groups, fine = tall.shape[:2]
        for g in range(groups):
            for b in range(chunks):
                start = (g * chunks + b) * fine
                tall[g, :, b * width : (b + 1) * width] = grad_two[start : start + fine].astype(BF)
        put_blocks(wide, grad_one)
        send_wide(step + 1).start()
        send_tall(step).start()

    @pl.when(step == chunks)
    def _():
        def finish(r, _):
            rows = rows_of(r)
            cot = cot_ref[rows, :].astype(F32)
            middle = mid[rows, :]
            second = two[rows, :] + fc2_b
            out_ref[rows, :] = (middle + gate_two * second).astype(BF)
            normed, inv = layer_norm(middle)
            lifted = normed * gain
            grad = da[rows, :]
            grad_h = grad * lift
            dmid = cot + norm_back(grad_h * gain, normed, inv)
            dmid_ref[rows, :] = dmid
            dy_one = (dmid * gate_one).astype(BF)
            dpre[rows, :] = dy_one
            dattn_ref[rows, :] = mm_t(dy_one, wo_ref[...]).astype(BF)
            parts = (
                dmid * branch[rows, :], grad, grad * lifted, cot * second,
                grad_h * normed, dy[rows, :].astype(F32),
            )
            for i, part in enumerate(parts):
                sums_ref[i : i + 1, :] += jnp.sum(part, axis=0, keepdims=True)
            return 0

        lax.fori_loop(0, blocks, finish, 0)
        grad_out = t_mm(attn_ref[...], dpre[...])
        send_wide(step).wait()
        send_tall(step - 1).wait()
        put_blocks(wide, grad_out)
        send_wide(0).start()
        send_wide(0).wait()


def put_blocks(ref, grad):
    groups, places, rows = ref.shape[:3]
    for s in range(places):
        for g in range(groups):
            start = (s * groups + g) * rows
            ref[g, s] = grad[start : start + rows].astype(BF)


def middle(attn, tok, cot, vec, fc1_b, pack, groups):
    total, width = attn.shape
    shards = pack.shape[1] // width - 6
    fine = width // shards // groups
    keep = pl.Buffered(1)
    whole = pl.BlockSpec((total, width), lambda i: (0, 0), pipeline_mode=keep)
    last = shards - 1
    low = lambda i: jnp.minimum(i, last)
    w2_spec = lambda b: pl.BlockSpec((width // shards, width), lambda i: (low(i), 5 + b))
    return pl.pallas_call(
        functools.partial(middle_kernel, shards, len(cot)),
        grid=(shards + 1,),
        in_specs=[
            whole, whole,
            pl.BlockSpec((8, width), lambda i: (0, 0)),
            pl.BlockSpec((1, width), lambda i: (0, low(i))),
            pl.BlockSpec((width, width), lambda i: (0, 0), pipeline_mode=keep),
            pl.BlockSpec((width, width), lambda i: (0, 1 + low(i))),
        ] + [w2_spec(b) for b in range(shards)]
        + [pl.BlockSpec(cot[0].shape, lambda i: (0, 0), pipeline_mode=keep)] * len(cot),
        out_specs=[
            whole, whole, whole,
            pl.BlockSpec(memory_space=pl.ANY),
            pl.BlockSpec((8, width), lambda i: (0, 0)),
            pl.BlockSpec((1, width), lambda i: (0, low(i))),
        ],
        out_shape=[
            jax.ShapeDtypeStruct((total, width), BF),
            jax.ShapeDtypeStruct((total, width), BF),
            jax.ShapeDtypeStruct((total, width), F32),
            jax.ShapeDtypeStruct((groups, shards, fine, 9 * width), BF),
            jax.ShapeDtypeStruct((8, width), F32),
            jax.ShapeDtypeStruct((1, 4 * width), F32),
        ],
        scratch_shapes=[
            pltpu.VMEM((total, width), F32),
            pltpu.VMEM((total, width), F32),
            pltpu.VMEM((total, width), BF),
            pltpu.VMEM((total, width), BF),
            pltpu.VMEM((total, width), F32),
            pltpu.VMEM((total, width), F32),
            pltpu.VMEM((total, width), BF),
            pltpu.VMEM((total, width), BF),
            pltpu.VMEM((width, width), BF),
            pltpu.VMEM((total, width), BF),
            pltpu.VMEM((groups, shards, fine, width), BF),
            pltpu.VMEM((groups, fine, shards * width), BF),
            pltpu.SemaphoreType.DMA((2,)),
        ],
        compiler_params=pltpu.CompilerParams(vmem_limit_bytes=60 << 20),
        cost_estimate=cost(55),
        name="middle",
    )(attn, tok, vec, fc1_b, pack, pack, *([pack] * shards), *cot)


class Links:
    def __init__(self, groups, shards):
        self.groups, self.shards, self.planes = groups, shards, groups // 2
        self.g = lax.axis_index("group")
        self.s = lax.axis_index("shard")
        self.c = self.g % 2
        self.plane = self.g // 2
        tilt = self.plane if self.planes == 4 else 0 * self.plane
        self.where = jnp.stack([self.s, self.c, tilt]).astype(jnp.int32)

    def swap(self, value):
        return lax.ppermute(value, "group", [(i, i ^ 1) for i in range(self.groups)])

    def turn(self, value, step):
        n = self.shards
        return lax.ppermute(value, "shard", [(i, (i + step) % n) for i in range(n)])

    def across(self, value, step):
        return lax.ppermute(value, "group", [(i, i ^ (2 * step)) for i in range(self.groups)])

    def round_perm(self, k):
        n, perm = self.shards, []
        for g in range(self.groups):
            for s in range(n):
                d = (s + k) % n
                goal = ((g // 2) * 2 + d % 2, 2 * (d // 2) + g % 2)
                perm.append((g * n + s, goal[0] * n + goal[1]))
        return perm

    def cut(self, value):
        batches, rows, width = value.shape
        pieces = value.reshape(batches * 2, rows // 2, width)
        return [
            lax.dynamic_index_in_dim(pieces, (self.s + k) % self.shards, 0, False)
            for k in range(self.shards)
        ]

    def to_trees(self, pieces):
        return [
            lax.ppermute(piece, ("group", "shard"), self.round_perm(k))
            for k, piece in enumerate(pieces)
        ]

    def from_trees(self, value):
        rows = value.shape[0] // self.shards
        got = []
        for k in range(self.shards):
            back = [(b, a) for a, b in self.round_perm(k)]
            got.append(
                lax.ppermute(value[k * rows : (k + 1) * rows], ("group", "shard"), back)
            )
        return got

    def lay_out(self, got, batches):
        rows, width = got[0].shape
        out = jnp.zeros((self.shards, rows, width), got[0].dtype)
        for k, piece in enumerate(got):
            out = lax.dynamic_update_index_in_dim(out, piece, (self.s + k) % self.shards, 0)
        return out.reshape(batches, 1, 2 * rows, width)

    def line_order(self, parts):
        stacked = jnp.stack(parts)
        return jnp.stack(
            [
                lax.dynamic_index_in_dim(stacked, (self.s - j) % self.shards, 0, False)
                for j in range(self.shards)
            ]
        )

    def line_gather(self, value):
        return self.line_order([value] + [self.turn(value, k) for k in range(1, self.shards)])

    def gather_all(self, part):
        return lax.all_gather(part, ("shard", "group"), axis=0, tiled=True)

    def tree_sums(self, vec):
        line = self.line_gather(vec)
        return line + self.swap(line)

    def my_rows(self, weight):
        rows = weight.shape[-2] // self.groups
        return lax.dynamic_slice_in_dim(weight, self.g * rows, rows, weight.ndim - 2)

    def gather_fast(self, weight):
        if self.planes != 4:
            return self.gather_all(self.my_rows(weight))
        rows, width = weight.shape
        fine = rows // 8
        pieces = weight.reshape(2, 4, fine, width)
        piece = lax.dynamic_index_in_dim(
            pieces.reshape(8, fine, width), self.c * 4 + self.plane, 0, False
        )
        line = jnp.stack([self.turn(piece, k) for k in range(1, self.shards)])
        half = jnp.stack([line] + [self.across(line, k) for k in range(1, 4)])
        return assemble(self.where, weight, half, self.swap(half), self.shards)

    def group_sum(self, blocks):
        out = lax.psum_scatter(blocks, "group", scatter_dimension=0, tiled=True)
        return out

    def plane_sum(self, value):
        if self.planes != 4:
            groups = [[2 * p + c for p in range(self.planes)] for c in range(2)]
            return lax.psum_scatter(
                value, "group", scatter_dimension=1, axis_index_groups=groups
            ).astype(F32)
        total = lax.dynamic_index_in_dim(value, self.plane, 1, False).astype(F32)
        for k in range(1, 4):
            piece = lax.dynamic_index_in_dim(value, self.plane ^ k, 1, False)
            total = total + self.across(piece, k).astype(F32)
        return total

    def plane_gather(self, value):
        if self.planes != 4:
            groups = [[2 * p + c for p in range(self.planes)] for c in range(2)]
            return lax.all_gather(value, "group", axis_index_groups=groups)
        parts = jnp.stack([value] + [self.across(value, k) for k in range(1, 4)])
        return jnp.stack(
            [lax.dynamic_index_in_dim(parts, self.plane ^ j, 0, False) for j in range(4)]
        )

    def reduce_fast(self, grad):
        pair = (grad[0].astype(F32) + self.swap(grad[1]).astype(F32)).astype(BF)
        if self.planes != 4:
            line = self.plane_sum(pair.transpose(1, 0, 2, 3)).astype(BF)
        else:
            line = pair[0].astype(F32)
            for k in range(1, 4):
                line = line + self.across(pair[k], k).astype(F32)
            line = line.astype(BF)
        total = line[0].astype(F32)
        for k in range(1, self.shards):
            total = total + self.turn(line[k], k).astype(F32)
        total = total.astype(BF)
        if self.planes != 4:
            half = self.plane_gather(total)
        else:
            half = jnp.stack([total] + [self.across(total, k) for k in range(1, 4)])
        return settle(self.where, half, self.swap(half)).reshape(-1, total.shape[1])


def on_device(
    tokens,
    cond,
    seg_ids,
    parents,
    cotangent,
    w_qkv,
    w_out,
    w_fc1,
    b_fc1,
    w_fc2,
    b_fc2,
    w_ada,
    b_ada,
    gain1,
    gain2,
    groups,
):
    batches, _, row_count, width = tokens.shape
    shards = lax.axis_size("shard")
    assert shards == 2 * batches and groups % 2 == 0
    head_dim = width // HEADS
    scale = 1.0 / math.sqrt(head_dim)
    net = Links(groups, shards)
    rows = row_count // 2
    mine = shards * rows
    tree_len = seg_ids.shape[2]
    labels = parents.shape[2]
    cond_dim = cond.shape[2]

    qkv_w = net.gather_fast(w_qkv)
    tok_parts = net.to_trees(net.cut(tokens[:, 0]))
    fc2_blocks = net.my_rows(w_fc2.reshape(shards, -1, width))
    share = jnp.concatenate(
        [net.my_rows(w_out), net.my_rows(w_fc1)] + [fc2_blocks[b] for b in range(shards)]
        + [net.my_rows(w_ada.reshape(-1, width))],
        axis=1,
    )
    pack = net.gather_all(share)

    packed = jnp.concatenate(
        [seg_ids[:, 0].astype(F32), parents[:, 0].astype(F32), cond[:, 0]], axis=1
    )
    other = net.swap(packed)
    trees = jnp.where(
        net.c == 0, jnp.stack([packed, other], axis=1), jnp.stack([other, packed], axis=1)
    ).reshape(shards, packed.shape[1])
    conds = trees[:, tree_len + labels :]
    my_tree = lax.dynamic_index_in_dim(trees, net.s, 0, False)
    tree_seg = my_tree[:tree_len]
    parent_row = my_tree[tree_len : tree_len + labels]
    ada_rows = jnp.dot(conds, w_ada.astype(F32), precision=HIGH) + b_ada.astype(F32)
    small = jnp.concatenate([b_fc1, b_fc2, gain1, gain2]).astype(F32)
    pieces = jnp.concatenate(
        [ada_rows, jnp.broadcast_to(small[None], (shards, small.shape[0]))], axis=1
    )
    got = [lax.dynamic_index_in_dim(pieces, net.s, 0, False)]
    for k in range(1, shards):
        piece = lax.dynamic_index_in_dim(pieces, (net.s + k) % shards, 0, False)
        got.append(net.turn(piece, k))
    line = net.line_order(got)
    cut = ada_rows.shape[1]
    ada = line[:, :cut].reshape(-1)
    ends = [cut]
    for vec in (b_fc1, b_fc2, gain1, gain2):
        ends.append(ends[-1] + vec.shape[0])
    fc1_b, fc2_b, gain_a, gain_b = (
        line[:, ends[i] : ends[i + 1]].reshape(-1) for i in range(4)
    )
    shift_one, scale_one, gate_one, shift_two, scale_two, gate_two = jnp.split(ada, 6)

    half_seg = tree_seg.reshape(shards, 2, rows)
    base = 2 * (net.s // 2)

    def row_segs(place):
        take = lax.dynamic_index_in_dim(half_seg, place, 1, False)
        return jnp.concatenate(
            [
                lax.dynamic_index_in_dim(take, (base + place - k) % shards, 0, False)
                for k in range(shards)
            ]
        )

    query_seg = row_segs(net.c)
    key_seg = jnp.concatenate([query_seg, row_segs(1 - net.c)])
    lanes = jnp.arange(LANES, dtype=F32)
    table = jnp.zeros((LANES,), F32).at[:labels].set(parent_row)
    up_two = jnp.sum(jnp.where(table[:, None] == lanes[None, :], table[None, :], 0.0), axis=1)
    reach = (
        (lanes[:, None] == lanes[None, :])
        | (table[:, None] == lanes[None, :])
        | (up_two[:, None] == lanes[None, :])
    )
    hot = (key_seg[:, None] == lanes[None, :]).astype(BF)
    feat = mm(hot[:mine], jnp.where(reach, 0.0, BIG).astype(BF)).astype(BF)
    held = jnp.max(hot.reshape(-1, BLOCK, LANES), axis=1)
    wanted = mm(held[: mine // BLOCK], reach.astype(BF)).astype(BF)
    active = mm_t(wanted, held) > 0.5

    tok_parts, cot_pieces = lax.optimization_barrier((tok_parts, net.cut(cotangent[:, 0])))
    vec_one = jnp.stack([gain_a, 1.0 + scale_one, shift_one] + [gain_a] * 5)
    tok, act_one, query, kv, peak = entry(tok_parts, vec_one, qkv_w)
    far = net.swap(kv)
    grad_out = net.to_trees(cot_pieces)
    bound = jnp.max(peak[0])
    other_bound = jnp.maximum(bound, jnp.max(jnp.abs(far)).astype(F32))
    safe = bound * other_bound * (head_dim * scale) < 2.0**27
    flags = jnp.concatenate(
        [(active | ~safe).reshape(-1), safe[None]]
    ).astype(jnp.int32)
    attn, log_totals = attn_fwd(query, kv, far, feat, hot, flags, scale, PAIRS)
    vec = jnp.stack(
        [gate_one, gain_b, 1.0 + scale_two, shift_two, gate_two, fc2_b, fc2_b, fc2_b]
    )
    result, grad_attn, grad_mid, blocks, sums, g_b1 = middle(
        attn, tok, grad_out, vec, fc1_b[None], pack, groups
    )
    out_parts = net.from_trees(result)

    parts = net.group_sum(blocks.reshape(-1, 9 * width))
    q_grads, near_grads, far_grads = attn_bwd(
        query, kv, far, feat, hot, flags, attn, grad_attn, log_totals, scale, PAIRS
    )
    spots = (2, groups // 2, shards, w_qkv.shape[0] // groups)
    grad_in, g_qkv, late_sums = leave(
        net.where, q_grads, near_grads, net.swap(far_grads), act_one, qkv_w, tok, grad_mid, vec_one, spots
    )
    out_parts, grad_in, g_qkv = lax.optimization_barrier((out_parts, grad_in, g_qkv))
    t_qkv = net.reduce_fast(g_qkv)
    grads_parts = net.from_trees(grad_in)
    out = net.lay_out(out_parts, batches)
    grads_x = net.lay_out(grads_parts, batches)
    line_sum = lax.psum_scatter(
        parts, "shard", scatter_dimension=0, tiled=True
    )
    sums_here = lax.all_gather(line_sum, "group", axis=0, tiled=True)
    t_out, t_fc1, t_fc2 = unpack(sums_here, groups, width)

    trees_here = net.tree_sums(
        jnp.concatenate([late_sums[:3].reshape(-1), sums[:6].reshape(-1), g_b1[0]])
    )
    ada_cols = [0, 1, 3, 4, 5, 6]
    dada = jnp.concatenate(
        [trees_here[:, i * width : (i + 1) * width] for i in ada_cols], axis=1
    )
    biases = jnp.sum(
        jnp.concatenate([trees_here[:, 2 * width : 3 * width], trees_here[:, 7 * width :]], axis=1),
        axis=0,
        keepdims=True,
    )
    everyone = net.plane_gather(
        jnp.concatenate([dada, conds, jnp.broadcast_to(biases, (shards, 7 * width))], axis=1)
    )
    every_dada = everyone[:, :, : 6 * width].reshape(-1, 6 * width)
    every_cond = everyone[:, :, 6 * width : 6 * width + cond_dim].reshape(-1, cond_dim)
    g_one, g_two, g_bias2, g_bias1 = jnp.split(
        jnp.sum(everyone[:, 0, 6 * width + cond_dim :], axis=0), [width, 2 * width, 3 * width]
    )

    def place(vec):
        n = vec.shape[-1] // shards
        return lax.dynamic_slice_in_dim(vec, net.s * n, n, vec.ndim - 1)

    dada_here = place(every_dada)
    t_ada = lax.dot_general(
        every_cond, dada_here, (((0,), (0,)), ((), ())), precision=HIGH
    )
    t_bada = jnp.sum(dada_here, axis=0)
    own = lax.dynamic_index_in_dim(dada.reshape(batches, 2, -1), net.c, 1, False)
    ada_w = pack[:, 9 * width :].reshape(shards, cond_dim, -1).astype(F32)
    cond_total = jnp.einsum(
        "bsn,scn->bc", own.reshape(batches, shards, -1), ada_w, precision=HIGH
    )
    return (
        out,
        grads_x,
        cond_total[:, None, :],
        t_qkv,
        t_out,
        t_fc1,
        place(g_bias1),
        t_fc2,
        place(g_bias2),
        t_ada,
        t_bada,
        place(g_one),
        place(g_two),
    )


def solution(mesh):
    in_specs = (
        P(None, "group", "shard", None),
        P(None, "group", None),
        P(None, "group", None),
        P(None, "group", None),
        P(None, "group", "shard", None),
        P("shard", None),
        P("shard", None),
        P("shard", None),
        P("shard"),
        P("shard", None),
        P("shard"),
        P(None, "shard"),
        P("shard"),
        P("shard"),
        P("shard"),
    )
    out_specs = (
        P(None, "group", "shard", None),
        P(None, "group", "shard", None),
        P(None, "group", None),
        P("shard", None),
        P("shard", None),
        P("shard", None),
        P("shard"),
        P("shard", None),
        P("shard"),
        P(None, "shard"),
        P("shard"),
        P("shard"),
        P("shard"),
    )
    groups = mesh.shape["group"]

    def run(*args):
        return on_device(*args, groups)

    return jax.shard_map(
        run, mesh=mesh, in_specs=in_specs, out_specs=out_specs, check_vma=False
    )
```

```python
import functools
import math

import jax
import jax.numpy as jnp
from jax import lax
from jax.experimental import pallas as pl
from jax.experimental.pallas import tpu as pltpu
from jax.sharding import PartitionSpec as P

HEADS = 12
EPS = 1e-05
GELU_C = 0.7978845608028654
GELU_K = 0.044715
HIGH = lax.Precision.HIGHEST
BF = jnp.bfloat16
F32 = jnp.float32
BLOCK = 256
SPAN = 512
LANES = 128
BIG = -float(2**30)
MASKED = -1000000000.0
PAIRS = 6


def layer_norm(values):
    centred = values - jnp.mean(values, axis=-1, keepdims=True)
    inv_std = lax.rsqrt(jnp.mean(centred * centred, axis=-1, keepdims=True) + EPS)
    return centred * inv_std, inv_std


def norm_back(grad_normed, normed, inv_std):
    first_mean = jnp.mean(grad_normed, axis=-1, keepdims=True)
    second = jnp.mean(grad_normed * normed, axis=-1, keepdims=True)
    return (grad_normed - first_mean - normed * second) * inv_std


def gelu_parts(pre_act):
    inner_arg = GELU_C * (pre_act + GELU_K * pre_act * pre_act * pre_act)
    tangent = jnp.tanh(inner_arg)
    gelu_value = 0.5 * pre_act * (1.0 + tangent)
    gelu_slope = 0.5 * (1.0 + tangent) + 0.5 * pre_act * (1.0 - tangent * tangent) * GELU_C * (
        1.0 + 3.0 * GELU_K * pre_act * pre_act
    )
    return gelu_value, gelu_slope


def mm(left, right):
    return jnp.dot(left, right, preferred_element_type=F32)


def mm_t(left, right):
    return lax.dot_general(left, right, (((1,), (1,)), ((), ())), preferred_element_type=F32)


def t_mm(left, right):
    return lax.dot_general(left, right, (((0,), (0,)), ((), ())), preferred_element_type=F32)


def split_heads(pair):
    first = lax.broadcasted_iota(jnp.int32, pair.shape, 1) < LANES // 2
    zero = jnp.zeros_like(pair)
    return jnp.concatenate([jnp.where(first, pair, zero), jnp.where(first, zero, pair)], axis=0)

def side_by_side(stack):
    n = stack.shape[0] // 2
    return jnp.concatenate([stack[:n], stack[n:]], axis=1)

def as_row(column):
    return jnp.transpose(jnp.broadcast_to(column, (column.shape[0], LANES)))[:1]

def interleave(into, near_ref, far_ref):
    for i in range(near_ref.shape[0] // BLOCK):
        rows = slice(i * BLOCK, (i + 1) * BLOCK)
        into[2 * i * BLOCK : (2 * i + 1) * BLOCK, :] = near_ref[rows, :]
        into[(2 * i + 1) * BLOCK : (2 * i + 2) * BLOCK, :] = far_ref[rows, :]

def lane_groups(x):
    return [x[:, i : i + LANES] for i in range(0, x.shape[1], LANES)]

def is_safe(peak, far_keys, scale):
    top = jnp.maximum(peak, jnp.max(jnp.abs(far_keys.astype(F32))))
    return (peak * top * (scale * (LANES // 2)) < 2.0**27).astype(jnp.int32)

def lanes_sum(x): return jnp.sum(x, axis=1, keepdims=True)

def fwd_kernel(near, pp, scale, flags, peak_ref, q_ref, kn_ref, vn_ref, kf_ref, vf_ref, feat_ref, hot_ref, o_ref, lse_ref,
               s_ref, m_ref, l_ref, acc_ref, k_all, v_all, safe_ref):
    qb = pl.program_id(1)
    nk = hot_ref.shape[0] // SPAN
    @pl.when(qb == 0)
    def _():
        interleave(k_all, kn_ref, kf_ref)
        interleave(v_all, vn_ref, vf_ref)
        safe_ref[0] = is_safe(peak_ref[0], kf_ref[...], scale)
    safe = safe_ref[0] == 1
    feat = feat_ref[...]
    feat2 = jnp.concatenate([feat, feat], axis=0)
    qs = [split_heads(q_ref[:, p*LANES:(p+1)*LANES] * scale) for p in range(pp)]
    m_ref[...] = jnp.full(m_ref.shape, -jnp.inf, F32)
    def scan_scores(exact):
        def step(j, _):
            @pl.when((flags[qb * nk + j] == 1) | jnp.logical_not(safe))
            def _():
                rows = pl.ds(pl.multiple_of(j * SPAN, SPAN), SPAN)
                hot = hot_ref[rows, :]
                for p in range(pp):
                    k = k_all[rows, p*LANES:(p+1)*LANES]
                    if exact:
                        ok = mm_t(feat2, hot) > -1.0
                        s = jnp.where(ok, mm_t(qs[p], k), MASKED)
                    else:
                        s = mm_t(jnp.concatenate([qs[p], feat2], axis=1), jnp.concatenate([k, hot], axis=1))
                    s_ref[p, j] = s
                    m_ref[p] = functools.reduce(jnp.maximum, lane_groups(s), m_ref[p])
            return 0
        lax.fori_loop(0, nk, step, 0)
    @pl.when(safe)
    def _(): scan_scores(False)
    @pl.when(jnp.logical_not(safe))
    def _(): scan_scores(True)
    tops = [jnp.max(m_ref[p], axis=1, keepdims=True) for p in range(pp)]
    l_ref[...] = jnp.zeros(l_ref.shape, F32)
    acc_ref[...] = jnp.zeros(acc_ref.shape, F32)
    def step(j, _):
        @pl.when((flags[qb * nk + j] == 1) | jnp.logical_not(safe))
        def _():
            rows = pl.ds(pl.multiple_of(j * SPAN, SPAN), SPAN)
            for p in range(pp):
                e = jnp.exp(s_ref[p, j] - tops[p])
                l_ref[p] += sum(lane_groups(e))
                v = split_heads(v_all[rows, p*LANES:(p+1)*LANES])
                acc_ref[p] += mm(side_by_side(e.astype(BF)), v)
        return 0
    lax.fori_loop(0, nk, step, 0)
    for p in range(pp):
        total = lanes_sum(l_ref[p])
        lse_ref[p, 0] = as_row(tops[p] + jnp.log(total))
        first = lax.broadcasted_iota(jnp.int32, (BLOCK, LANES), 1) < LANES // 2
        o_ref[:, p*LANES:(p+1)*LANES] = (acc_ref[p] / jnp.where(first, total[:BLOCK], total[BLOCK:])).astype(BF)

def attn_fwd(q, kv, far, feat, hot, flags, peak, scale, pp):
    near, width = q.shape
    total = hot.shape[0]
    steps = width // LANES // pp
    nq = near // BLOCK
    col = lambda c: (lambda h, i, f: (0, c * steps + h))
    return pl.pallas_call(
        functools.partial(fwd_kernel, near, pp, scale),
        grid_spec=pltpu.PrefetchScalarGridSpec(
            num_scalar_prefetch=1, grid=(steps, nq),
            in_specs=[
                pl.BlockSpec(memory_space=pltpu.SMEM),
                pl.BlockSpec((BLOCK, pp*LANES), lambda h, i, f: (i, h)),
                pl.BlockSpec((near, pp*LANES), col(0)),
                pl.BlockSpec((near, pp*LANES), col(1)),
                pl.BlockSpec((near, pp*LANES), col(0)),
                pl.BlockSpec((near, pp*LANES), col(1)),
                pl.BlockSpec((BLOCK, LANES), lambda h, i, f: (i, 0)),
                pl.BlockSpec((total, LANES), lambda h, i, f: (0, 0)),
            ],
            out_specs=[
                pl.BlockSpec((BLOCK, pp*LANES), lambda h, i, f: (i, h)),
                pl.BlockSpec((pp, 1, 1, 2*BLOCK), lambda h, i, f: (h, i, 0, 0)),
            ],
            scratch_shapes=[
                pltpu.VMEM((pp, total // SPAN, 2*BLOCK, SPAN), F32),
                pltpu.VMEM((pp, 2*BLOCK, LANES), F32),
                pltpu.VMEM((pp, 2*BLOCK, LANES), F32),
                pltpu.VMEM((pp, BLOCK, LANES), F32),
                pltpu.VMEM((total, pp*LANES), BF),
                pltpu.VMEM((total, pp*LANES), BF),
                pltpu.SMEM((1,), jnp.int32),
            ]),
        out_shape=[jax.ShapeDtypeStruct((near, width), BF), jax.ShapeDtypeStruct((width // LANES, nq, 1, 2*BLOCK), F32)],
        compiler_params=pltpu.CompilerParams(vmem_limit_bytes=56<<20),
        cost_estimate=cost(38),
        name="attn_forward",
    )(flags, peak, q, kv, kv, far, far, feat, hot)

def bwd_kernel(near, pp, scale, flags, peak_ref, q_ref, kn_ref, vn_ref, kf_ref, vf_ref, feat_ref, hot_ref, o_ref, do_ref, lse_ref,
               dq_ref, near_ref, far_ref, k_all, v_all, k_turned, dk_acc, dv_acc, dq_acc, safe_ref):
    half = LANES // 2
    qb = pl.program_id(1)
    nk = hot_ref.shape[0] // SPAN
    @pl.when(qb == 0)
    def _():
        interleave(k_all, kn_ref, kf_ref)
        interleave(v_all, vn_ref, vf_ref)
        safe_ref[0] = is_safe(peak_ref[0], kf_ref[...], scale)
        k_turned[...] = jnp.transpose(k_all[...])
        dk_acc[...] = jnp.zeros(dk_acc.shape, F32)
        dv_acc[...] = jnp.zeros(dv_acc.shape, F32)
    safe = safe_ref[0] == 1
    feat = feat_ref[...]
    feat2 = jnp.concatenate([feat, feat], axis=0)
    dq_acc[...] = jnp.zeros(dq_acc.shape, F32)
    qs, dos, deltas, lses = [], [], [], []
    for p in range(pp):
        cols = slice(p*LANES, (p+1)*LANES)
        qs.append(split_heads(q_ref[:, cols] * scale))
        do2 = split_heads(do_ref[:, cols])
        dos.append(do2)
        o = o_ref[:, cols].astype(F32)
        deltas.append(as_row(lanes_sum(do2.astype(F32) * jnp.concatenate([o, o], axis=0))))
        lses.append(lse_ref[p, 0])
    def sweep(exact):
        def step(j, _):
            @pl.when((flags[qb * nk + j] == 1) | jnp.logical_not(safe))
            def _():
                rows = pl.ds(pl.multiple_of(j * SPAN, SPAN), SPAN)
                hot = hot_ref[rows, :]
                for p in range(pp):
                    cols = slice(p*LANES, (p+1)*LANES)
                    k = k_all[rows, cols]; v = v_all[rows, cols]
                    if exact:
                        ok = mm_t(hot, feat2) > -1.0
                        s = jnp.where(ok, mm_t(k, qs[p]), MASKED)
                    else:
                        s = mm_t(jnp.concatenate([k, hot], axis=1), jnp.concatenate([qs[p], feat2], axis=1))
                    prob = jnp.exp(s - lses[p])
                    dprob = mm_t(v, dos[p])
                    ds = prob * (dprob - deltas[p])
                    if exact:
                        ds = jnp.where(ok, ds, 0.0)
                    ds = ds.astype(BF)
                    dv_acc[rows, cols] += mm(prob.astype(BF), dos[p])
                    dk_acc[rows, cols] += mm(ds, qs[p])
                    for h in range(2):
                        kt = k_turned[p*LANES + h*half : p*LANES + (h+1)*half, rows]
                        dq_acc[p, h*half:(h+1)*half] += mm(kt, ds[:, h*BLOCK:(h+1)*BLOCK])
            return 0
        lax.fori_loop(0, nk, step, 0)
    @pl.when(safe)
    def _(): sweep(False)
    @pl.when(jnp.logical_not(safe))
    def _(): sweep(True)
    for p in range(pp):
        dq_ref[:, p*LANES:(p+1)*LANES] = jnp.transpose(dq_acc[p] * scale).astype(BF)
    @pl.when(qb == pl.num_programs(1) - 1)
    def _():
        for i in range(near // BLOCK):
            rows = slice(i * BLOCK, (i + 1) * BLOCK)
            for side, acc in enumerate((dk_acc, dv_acc)):
                near_ref[side, rows] = acc[2 * i * BLOCK : (2 * i + 1) * BLOCK]
                far_ref[side, rows] = acc[(2 * i + 1) * BLOCK : (2 * i + 2) * BLOCK].astype(BF)

def attn_bwd(q, kv, far, feat, hot, flags, peak, attn, dattn, lse, scale, pp):
    near, width = q.shape
    total = hot.shape[0]
    steps = width // LANES // pp
    nq = near // BLOCK
    col = lambda c: (lambda h, i, f: (0, c * steps + h))
    rowblk = pl.BlockSpec((BLOCK, pp*LANES), lambda h, i, f: (i, h))
    whole = pl.BlockSpec((near, pp*LANES), col(0))
    both = pl.BlockSpec((2, near, pp*LANES), lambda h, i, f: (0, 0, h))
    return pl.pallas_call(
        functools.partial(bwd_kernel, near, pp, scale),
        grid_spec=pltpu.PrefetchScalarGridSpec(
            num_scalar_prefetch=1, grid=(steps, nq),
            in_specs=[
                pl.BlockSpec(memory_space=pltpu.SMEM),
                rowblk,
                pl.BlockSpec((near, pp*LANES), col(0)),
                pl.BlockSpec((near, pp*LANES), col(1)),
                whole,
                pl.BlockSpec((near, pp*LANES), col(1)),
                pl.BlockSpec((BLOCK, LANES), lambda h, i, f: (i, 0)),
                pl.BlockSpec((total, LANES), lambda h, i, f: (0, 0)),
                rowblk, rowblk,
                pl.BlockSpec((pp, 1, 1, 2*BLOCK), lambda h, i, f: (h, i, 0, 0)),
            ],
            out_specs=[rowblk, both, both],
            scratch_shapes=[
                pltpu.VMEM((total, pp*LANES), BF),
                pltpu.VMEM((total, pp*LANES), BF),
                pltpu.VMEM((pp*LANES, total), BF),
                pltpu.VMEM((total, pp*LANES), F32),
                pltpu.VMEM((total, pp*LANES), F32),
                pltpu.VMEM((pp, LANES, BLOCK), F32),
                pltpu.SMEM((1,), jnp.int32),
            ]),
        out_shape=[
            jax.ShapeDtypeStruct((near, width), BF),
            jax.ShapeDtypeStruct((2, near, width), F32),
            jax.ShapeDtypeStruct((2, near, width), BF),
        ],
        compiler_params=pltpu.CompilerParams(vmem_limit_bytes=56<<20),
        cost_estimate=cost(63),
        name="attn_backward",
    )(flags, peak, q, kv, kv, far, far, feat, hot, attn, dattn, lse)


def assemble_kernel(shards, where, own_ref, half_ref, other_ref, out_ref):
    s, c, plane = where[0], where[1], where[2]
    groups, planes = own_ref.shape[0], half_ref.shape[0]
    out_ref[pl.ds(s * groups, groups)] = own_ref[...]
    for side, source in ((c, half_ref), (1 - c, other_ref)):
        for j in range(planes):
            for k in range(1, shards):
                place = lax.rem(s + shards - k, shards)
                out_ref[place * groups + side * planes + (plane ^ j)] = source[j, k - 1]


def assemble(where, own, half, other, shards):
    rows, width = own.shape
    fine = half.shape[2]
    groups = rows // fine
    full = lambda *shape: pl.BlockSpec(shape, lambda i, w: (0,) * len(shape))
    out = pl.pallas_call(
        functools.partial(assemble_kernel, shards),
        grid_spec=pltpu.PrefetchScalarGridSpec(
            num_scalar_prefetch=1,
            grid=(1,),
            in_specs=[full(groups, fine, width), full(*half.shape), full(*half.shape)],
            out_specs=full(groups * shards, fine, width),
        ),
        out_shape=jax.ShapeDtypeStruct((groups * shards, fine, width), own.dtype),
        compiler_params=pltpu.CompilerParams(vmem_limit_bytes=60 << 20),
        name="assemble",
    )(where, own.reshape(groups, fine, width), half, other)
    return out.reshape(shards * rows, width)


def entry_kernel(tok_ref, vec_ref, w_ref, act_ref, q_ref, kv_ref, peak_ref):
    step = pl.program_id(0)
    rows, pieces = BLOCK, tok_ref.shape[0] // BLOCK

    @pl.when(step == 0)
    def _():
        gain, lift, shift = (vec_ref[i : i + 1, :] for i in range(3))
        for i in range(pieces):
            at = slice(i * rows, (i + 1) * rows)
            normed, _unused = layer_norm(tok_ref[at, :].astype(F32))
            act_ref[at, :] = (normed * gain * lift + shift).astype(BF)
        peak_ref[...] = jnp.zeros_like(peak_ref)

    top = jnp.zeros((1, w_ref.shape[1]), F32)
    for i in range(pieces):
        at = slice(i * rows, (i + 1) * rows)
        value = mm(act_ref[at, :], w_ref[...])
        low = value.astype(BF)
        top = jnp.maximum(top, jnp.max(jnp.abs(low.astype(F32)), axis=0, keepdims=True))

        @pl.when(step < 2)
        def _():
            kv_ref[at, :] = low

        @pl.when(step == 2)
        def _():
            q_ref[at, :] = low

    peak_ref[0:1, :] = jnp.maximum(peak_ref[0:1, :], top)


def entry(tok, vec, qkv_w):
    total, width = tok.shape
    fixed = lambda *shape: pl.BlockSpec(shape, lambda j: (0,) * len(shape))
    return pl.pallas_call(
        entry_kernel,
        grid=(3,),
        in_specs=[
            fixed(total, width), fixed(8, width),
            pl.BlockSpec((width, width), lambda j: (0, lax.rem(j + 1, 3))),
        ],
        out_specs=[
            fixed(total, width), fixed(total, width),
            pl.BlockSpec((total, width), lambda j: (0, jnp.minimum(j, 1))),
            fixed(8, width),
        ],
        out_shape=[
            jax.ShapeDtypeStruct((total, width), BF),
            jax.ShapeDtypeStruct((total, width), BF),
            jax.ShapeDtypeStruct((total, 2 * width), BF),
            jax.ShapeDtypeStruct((8, width), F32),
        ],
        compiler_params=pltpu.CompilerParams(vmem_limit_bytes=48 << 20),
        cost_estimate=cost(9),
        name="entry",
    )(tok, vec, qkv_w)


def leave_kernel(spots, where, dq_ref, near_ref, far_ref, act_ref, w_ref, tok_ref, dmid_ref, vec_ref,
                 grad_ref, mine_ref, yours_ref, sums_ref, d_all, da):
    step = pl.program_id(0)
    total = dq_ref.shape[0]
    sides, planes, places, fine = spots

    @pl.when(step == 0)
    def _():
        d_all[...] = dq_ref[...]
        da[...] = jnp.zeros_like(da)

    @pl.when(step > 0)
    def _():
        d_all[...] = (near_ref[0] + far_ref[0].astype(F32)).astype(BF)

    grad = t_mm(act_ref[...], d_all[...])

    def put(ref, side):
        for place in range(places):
            turned = lax.rem(place + places - where[0], places)
            for plane in range(planes):
                start = ((place * sides + side) * planes + plane) * fine
                ref[plane ^ where[2], turned] = grad[start : start + fine].astype(BF)

    for side in range(sides):
        pl.when(where[1] == side)(functools.partial(put, mine_ref, side))
        pl.when(where[1] != side)(functools.partial(put, yours_ref, side))

    def add(r, _):
        rows = pl.ds(pl.multiple_of(r * BLOCK, BLOCK), BLOCK)
        da[rows, :] += mm_t(d_all[rows, :], w_ref[...])
        return 0

    lax.fori_loop(0, total // BLOCK, add, 0)

    @pl.when(step == 2)
    def _():
        gain, lift, shift = (vec_ref[i : i + 1, :] for i in range(3))
        sums_ref[...] = jnp.zeros_like(sums_ref)

        def finish(r, _):
            rows = pl.ds(pl.multiple_of(r * BLOCK, BLOCK), BLOCK)
            normed, inv = layer_norm(tok_ref[rows, :].astype(F32))
            part = da[rows, :]
            grad_h = part * lift
            back = norm_back(grad_h * gain, normed, inv)
            grad_ref[rows, :] = (dmid_ref[rows, :] + back).astype(BF)
            for i, term in enumerate((part, part * (normed * gain), grad_h * normed)):
                sums_ref[i : i + 1, :] += jnp.sum(term, axis=0, keepdims=True)
            return 0

        lax.fori_loop(0, total // BLOCK, finish, 0)


def leave(where, q_grads, near, far, act, qkv_w, tok, dmid, vec, spots):
    total, width = q_grads.shape
    keep = pl.Buffered(1)
    whole = pl.BlockSpec((total, width), lambda j, w: (0, 0), pipeline_mode=keep)
    both = pl.BlockSpec((1, total, width), lambda j, w: (jnp.maximum(j - 1, 0), 0, 0))
    small = pl.BlockSpec((8, width), lambda j, w: (0, 0))
    part = pl.BlockSpec(tuple(spots[1:]) + (width,), lambda j, w: (0, 0, 0, j))
    return pl.pallas_call(
        functools.partial(leave_kernel, spots),
        grid_spec=pltpu.PrefetchScalarGridSpec(
            num_scalar_prefetch=1,
            grid=(3,),
            in_specs=[
                whole, both, both, whole,
                pl.BlockSpec((width, width), lambda j, w: (0, j)),
                whole, whole, small,
            ],
            out_specs=[
                whole,
                part, part,
                small,
            ],
            scratch_shapes=[pltpu.VMEM((total, width), BF), pltpu.VMEM((total, width), F32)],
        ),
        out_shape=[
            jax.ShapeDtypeStruct((total, width), BF),
            jax.ShapeDtypeStruct(tuple(spots[1:]) + (3 * width,), BF),
            jax.ShapeDtypeStruct(tuple(spots[1:]) + (3 * width,), BF),
            jax.ShapeDtypeStruct((8, width), F32),
        ],
        compiler_params=pltpu.CompilerParams(vmem_limit_bytes=56 << 20),
        cost_estimate=cost(14),
        name="leave",
    )(where, q_grads, near, far, act, qkv_w, tok, dmid, vec)


def settle_kernel(where, half_ref, other_ref, out_ref):
    c, plane = where[1], where[2]
    for side, source in ((c, half_ref), (1 - c, other_ref)):
        for j in range(half_ref.shape[0]):
            out_ref[side * half_ref.shape[0] + (plane ^ j)] = source[j].astype(F32)


def settle(where, half, other):
    planes, fine, width = half.shape
    full = lambda *shape: pl.BlockSpec(shape, lambda i, w: (0,) * len(shape))
    return pl.pallas_call(
        settle_kernel,
        grid_spec=pltpu.PrefetchScalarGridSpec(
            num_scalar_prefetch=1,
            grid=(1,),
            in_specs=[full(planes, fine, width)] * 2,
            out_specs=full(2 * planes, fine, width),
        ),
        out_shape=jax.ShapeDtypeStruct((2 * planes, fine, width), F32),
        compiler_params=pltpu.CompilerParams(vmem_limit_bytes=40 << 20),
        name="settle",
    )(where, half, other)


def unpack_kernel(count, where, half_ref, other_ref, out_ref, fc1_ref, fc2_ref):
    step = pl.program_id(0)
    c, plane = where[1], where[2]

    def fill(ref):
        for side, source in ((c, half_ref), (1 - c, other_ref)):
            for j in range(source.shape[0]):
                ref[2 * (plane ^ j) + side] = source[j].astype(F32).reshape(ref.shape[1:])

    @pl.when(step == 0)
    def _():
        fill(out_ref)

    @pl.when((step > 0) & (step <= count))
    def _():
        fill(fc1_ref)

    @pl.when(step > count)
    def _():
        fill(fc2_ref)


def unpack(where, half, other, width):
    planes, fine, total = half.shape
    groups, count = 2 * planes, total // width // 2
    block = pl.BlockSpec((planes, fine, width), lambda i, w: (0, 0, i))
    low = lambda i: jnp.clip(i, 0, count - 1)
    out, fc1, fc2 = pl.pallas_call(
        functools.partial(unpack_kernel, count),
        grid_spec=pltpu.PrefetchScalarGridSpec(
            num_scalar_prefetch=1,
            grid=(1 + 2 * count,),
            in_specs=[block, block],
            out_specs=[
                pl.BlockSpec((groups, fine, width), lambda i, w: (0, 0, 0)),
                pl.BlockSpec((groups, fine, width), lambda i, w: (0, 0, low(i - 1))),
                pl.BlockSpec((groups, 1, fine, width), lambda i, w: (0, low(i - 1 - count), 0, 0)),
            ],
        ),
        out_shape=[
            jax.ShapeDtypeStruct((groups, fine, width), F32),
            jax.ShapeDtypeStruct((groups, fine, count * width), F32),
            jax.ShapeDtypeStruct((groups, count, fine, width), F32),
        ],
        compiler_params=pltpu.CompilerParams(vmem_limit_bytes=40 << 20),
        cost_estimate=cost(4),
        name="unpack",
    )(where, half, other)
    return out.reshape(-1, width), fc1.reshape(-1, count * width), fc2.reshape(-1, width)


def cost(microseconds):
    return pl.CostEstimate(
        flops=int(microseconds * 1.15e9), bytes_accessed=1 << 20, transcendentals=0
    )


def middle_kernel(chunks, where, attn_ref, tok_ref, cot_ref, vec_ref, b1_ref, wo_ref, w1_ref, *rest):
    w2_refs, rest = rest[:chunks], rest[chunks:]
    (out_ref, dattn_ref, dmid_ref, grads_ref, sums_ref, gb1_ref) = rest[:6]
    (mid, branch, act, dy, two, da, hid, dpre, w2, wide, tall, sems) = rest[6:]
    width = attn_ref.shape[1]

    def send_wide(column):
        cols = pl.ds(pl.multiple_of(column * width, LANES), width)
        return pltpu.make_async_copy(wide, grads_ref.at[:, :, :, cols], sems.at[0])

    def turned(place):
        return lax.rem(place + chunks - where[0], chunks)

    def send_tall(place):
        cols = pl.ds((1 + chunks) * width, chunks * width)
        return pltpu.make_async_copy(tall, grads_ref.at[:, turned(place), :, cols], sems.at[1])

    step = pl.program_id(0)
    total = attn_ref.shape[0]
    blocks = total // BLOCK
    gate_one, gain, lift, shift, gate_two, fc2_b = (vec_ref[i : i + 1, :] for i in range(6))

    def rows_of(r):
        return pl.ds(pl.multiple_of(r * BLOCK, BLOCK), BLOCK)

    @pl.when(step == 0)
    def _():
        sums_ref[...] = jnp.zeros_like(sums_ref)

        def start(r, _):
            rows = rows_of(r)
            one = mm(attn_ref[rows, :], wo_ref[...])
            middle = tok_ref[rows, :].astype(F32) + gate_one * one
            normed, _unused = layer_norm(middle)
            branch[rows, :] = one
            mid[rows, :] = middle
            act[rows, :] = (normed * gain * lift + shift).astype(BF)
            dy[rows, :] = (cot_ref[rows, :].astype(F32) * gate_two).astype(BF)
            two[rows, :] = jnp.zeros((BLOCK, two.shape[1]), F32)
            da[rows, :] = jnp.zeros((BLOCK, da.shape[1]), F32)
            return 0

        lax.fori_loop(0, blocks, start, 0)

    @pl.when(step < chunks)
    def _():
        height = w2_refs[0].shape[0]
        for b in range(chunks):
            w2[b * height : (b + 1) * height, :] = w2_refs[b][...]
        gb1_ref[...] = jnp.zeros_like(gb1_ref)

        def chunk(r, _):
            rows = rows_of(r)
            value, slope = gelu_parts(mm(act[rows, :], w1_ref[...]) + b1_ref[...])
            hidden = value.astype(BF)
            hid[rows, :] = hidden
            two[rows, :] += mm(hidden, w2[...])
            grad = (mm_t(dy[rows, :], w2[...]) * slope).astype(BF)
            dpre[rows, :] = grad
            gb1_ref[...] += jnp.sum(grad.astype(F32), axis=0, keepdims=True)
            da[rows, :] += mm_t(grad, w1_ref[...])
            return 0

        lax.fori_loop(0, blocks, chunk, 0)
        grad_two = t_mm(hid[...], dy[...])
        grad_one = t_mm(act[...], dpre[...])

        @pl.when(step > 0)
        def _():
            send_wide(step).wait()
            send_tall(step - 1).wait()

        groups, fine = tall.shape[:2]
        for g in range(groups):
            for b in range(chunks):
                start = (g * chunks + b) * fine
                tall[g, :, b * width : (b + 1) * width] = grad_two[start : start + fine].astype(BF)
        put_blocks(wide, grad_one, turned)
        send_wide(step + 1).start()
        send_tall(step).start()

    @pl.when(step == chunks)
    def _():
        def finish(r, _):
            rows = rows_of(r)
            cot = cot_ref[rows, :].astype(F32)
            middle = mid[rows, :]
            second = two[rows, :] + fc2_b
            out_ref[rows, :] = (middle + gate_two * second).astype(BF)
            normed, inv = layer_norm(middle)
            lifted = normed * gain
            grad = da[rows, :]
            grad_h = grad * lift
            dmid = cot + norm_back(grad_h * gain, normed, inv)
            dmid_ref[rows, :] = dmid
            dy_one = (dmid * gate_one).astype(BF)
            dpre[rows, :] = dy_one
            dattn_ref[rows, :] = mm_t(dy_one, wo_ref[...]).astype(BF)
            parts = (
                dmid * branch[rows, :], grad, grad * lifted, cot * second,
                grad_h * normed, dy[rows, :].astype(F32),
            )
            for i, part in enumerate(parts):
                sums_ref[i : i + 1, :] += jnp.sum(part, axis=0, keepdims=True)
            return 0

        lax.fori_loop(0, blocks, finish, 0)
        grad_out = t_mm(attn_ref[...], dpre[...])
        send_wide(step).wait()
        send_tall(step - 1).wait()
        put_blocks(wide, grad_out, turned)
        send_wide(0).start()
        send_wide(0).wait()


def put_blocks(ref, grad, turned):
    groups, places, rows = ref.shape[:3]
    for s in range(places):
        for g in range(groups):
            start = (s * groups + g) * rows
            ref[g, turned(s)] = grad[start : start + rows].astype(BF)


def middle(where, attn, tok, cot, vec, fc1_b, pack, groups):
    total, width = attn.shape
    shards = pack.shape[1] // width - 5
    fine = width // shards // groups
    keep = pl.Buffered(1)
    whole = pl.BlockSpec((total, width), lambda i, w: (0, 0), pipeline_mode=keep)
    last = shards - 1
    low = lambda i: jnp.minimum(i, last)
    w2_spec = lambda b: pl.BlockSpec((width // shards, width), lambda i, w: (low(i), 5 + b))
    return pl.pallas_call(
        functools.partial(middle_kernel, shards),
        grid_spec=pltpu.PrefetchScalarGridSpec(
            num_scalar_prefetch=1,
            grid=(shards + 1,),
            in_specs=[
            whole, whole, whole,
            pl.BlockSpec((8, width), lambda i, w: (0, 0)),
            pl.BlockSpec((1, width), lambda i, w: (0, low(i))),
            pl.BlockSpec((width, width), lambda i, w: (0, 0), pipeline_mode=keep),
            pl.BlockSpec((width, width), lambda i, w: (0, 1 + low(i))),
        ] + [w2_spec(b) for b in range(shards)],
        out_specs=[
            whole, whole, whole,
            pl.BlockSpec(memory_space=pl.ANY),
            pl.BlockSpec((8, width), lambda i, w: (0, 0)),
            pl.BlockSpec((1, width), lambda i, w: (0, low(i))),
        ],
        scratch_shapes=[
            pltpu.VMEM((total, width), F32),
            pltpu.VMEM((total, width), F32),
            pltpu.VMEM((total, width), BF),
            pltpu.VMEM((total, width), BF),
            pltpu.VMEM((total, width), F32),
            pltpu.VMEM((total, width), F32),
            pltpu.VMEM((total, width), BF),
            pltpu.VMEM((total, width), BF),
            pltpu.VMEM((width, width), BF),
            pltpu.VMEM((groups, shards, fine, width), BF),
            pltpu.VMEM((groups, fine, shards * width), BF),
            pltpu.SemaphoreType.DMA((2,)),
        ],
        ),
        out_shape=[
            jax.ShapeDtypeStruct((total, width), BF),
            jax.ShapeDtypeStruct((total, width), BF),
            jax.ShapeDtypeStruct((total, width), F32),
            jax.ShapeDtypeStruct((groups, shards, fine, 9 * width), BF),
            jax.ShapeDtypeStruct((8, width), F32),
            jax.ShapeDtypeStruct((1, 4 * width), F32),
        ],
        compiler_params=pltpu.CompilerParams(vmem_limit_bytes=60 << 20),
        cost_estimate=cost(55),
        name="middle",
    )(where, attn, tok, cot, vec, fc1_b, pack, pack, *([pack] * shards))


class Links:
    def __init__(self, groups, shards):
        self.groups, self.shards, self.planes = groups, shards, groups // 2
        self.g = lax.axis_index("group")
        self.s = lax.axis_index("shard")
        self.c = self.g % 2
        self.plane = self.g // 2
        tilt = self.plane if self.planes == 4 else 0 * self.plane
        self.where = jnp.stack([self.s, self.c, tilt]).astype(jnp.int32)

    def swap(self, value):
        return lax.ppermute(value, "group", [(i, i ^ 1) for i in range(self.groups)])

    def turn(self, value, step):
        n = self.shards
        return lax.ppermute(value, "shard", [(i, (i + step) % n) for i in range(n)])

    def across(self, value, step):
        return lax.ppermute(value, "group", [(i, i ^ (2 * step)) for i in range(self.groups)])

    def give(self, value):
        batches, rows, width = value.shape
        halves = value.reshape(batches, 2, rows // 2, width)
        keep = lax.dynamic_index_in_dim(halves, self.c, 1, False)
        return keep, lax.dynamic_index_in_dim(halves, 1 - self.c, 1, False)

    def to_trees(self, keep, got):
        return self.exchange(self.by_core(keep, got).reshape(-1, *keep.shape[1:]))

    def exchange(self, by_tree):
        return lax.all_to_all(by_tree, "shard", 0, 0).reshape(-1, by_tree.shape[-1])

    def by_core(self, mine, other):
        return jnp.where(
            self.c == 0, jnp.stack([mine, other], axis=1), jnp.stack([other, mine], axis=1)
        )

    def from_trees(self, value):
        return lax.all_to_all(
            value.reshape(self.shards, -1, value.shape[1]), "shard", 0, 0
        )

    def back(self, value, batches):
        by_core = value.reshape(batches, 2, *value.shape[1:])
        keep = lax.dynamic_index_in_dim(by_core, self.c, 1, False)
        return keep, lax.dynamic_index_in_dim(by_core, 1 - self.c, 1, False)

    def lay_out(self, keep, got):
        return self.by_core(keep, got).reshape(keep.shape[0], 1, -1, keep.shape[-1])

    def plane_order(self, parts):
        stacked = jnp.stack(parts)
        if self.planes != 4:
            return stacked
        return jnp.stack(
            [lax.dynamic_index_in_dim(stacked, self.plane ^ j, 0, False) for j in range(4)]
        )

    def line_order(self, parts):
        stacked = jnp.stack(parts)
        return jnp.stack(
            [
                lax.dynamic_index_in_dim(stacked, (self.s - j) % self.shards, 0, False)
                for j in range(self.shards)
            ]
        )

    def gather_all(self, part):
        return lax.all_gather(part, ("shard", "group"), axis=0, tiled=True)

    def my_rows(self, weight):
        rows = weight.shape[-2] // self.groups
        return lax.dynamic_slice_in_dim(weight, self.g * rows, rows, weight.ndim - 2)

    def group_sum(self, blocks):
        out = lax.psum_scatter(blocks, "group", scatter_dimension=0, tiled=True)
        return out

    def plane_sum(self, value):
        if self.planes != 4:
            groups = [[2 * p + c for p in range(self.planes)] for c in range(2)]
            return lax.psum_scatter(
                value, "group", scatter_dimension=1, axis_index_groups=groups
            ).astype(F32)
        total = lax.dynamic_index_in_dim(value, self.plane, 1, False).astype(F32)
        for k in range(1, 4):
            piece = lax.dynamic_index_in_dim(value, self.plane ^ k, 1, False)
            total = total + self.across(piece, k).astype(F32)
        return total

    def plane_gather(self, value):
        if self.planes != 4:
            groups = [[2 * p + c for p in range(self.planes)] for c in range(2)]
            return lax.all_gather(value, "group", axis_index_groups=groups)
        parts = jnp.stack([value] + [self.across(value, k) for k in range(1, 4)])
        return jnp.stack(
            [lax.dynamic_index_in_dim(parts, self.plane ^ j, 0, False) for j in range(4)]
        )

    def turns(self, values):
        return [self.turn(values[k], k) for k in range(1, self.shards)]

    def spread(self, value):
        if self.planes != 4:
            every = self.plane_gather(value)
            return [every[j] for j in range(self.planes)]
        return [value] + [self.across(value, k) for k in range(1, 4)]


def total(terms):
    result = terms[0].astype(F32)
    for term in terms[1:]:
        result = result + term.astype(F32)
    return result


def on_device(
    tokens,
    cond,
    seg_ids,
    parents,
    cotangent,
    w_qkv,
    w_out,
    w_fc1,
    b_fc1,
    w_fc2,
    b_fc2,
    w_ada,
    b_ada,
    gain1,
    gain2,
    groups,
):
    batches, _, row_count, width = tokens.shape
    shards = lax.axis_size("shard")
    assert shards == 2 * batches and groups % 2 == 0
    head_dim = width // HEADS
    scale = 1.0 / math.sqrt(head_dim)
    net = Links(groups, shards)
    rows = row_count // 2
    mine = shards * rows
    tree_len = seg_ids.shape[2]
    labels = parents.shape[2]
    cond_dim = cond.shape[2]

    fc2_blocks = net.my_rows(w_fc2.reshape(shards, -1, width))
    share = jnp.concatenate(
        [net.my_rows(w_out), net.my_rows(w_fc1)] + [fc2_blocks[b] for b in range(shards)],
        axis=1,
    )

    packed = jnp.concatenate(
        [seg_ids[:, 0].astype(F32), parents[:, 0].astype(F32), cond[:, 0]], axis=1
    )
    part_rows = w_qkv.shape[0] // groups
    early_w = jnp.concatenate([w_qkv, w_ada.reshape(-1, width)], axis=1)
    own_part = lax.dynamic_index_in_dim(
        early_w.reshape(groups, part_rows, -1), net.c * (groups // 2) + net.plane, 0, False
    )
    tok_keep, tok_give = net.give(tokens[:, 0])
    other = net.swap(packed)
    line_w = net.turns([own_part] * shards)
    tok_got = net.swap(tok_give)
    other, line_w, tok_got = lax.optimization_barrier((other, line_w, tok_got))
    tok = net.to_trees(tok_keep, tok_got)
    plane_w = net.spread(jnp.stack(line_w))
    cot_keep, cot_give = net.give(cotangent[:, 0])
    trees = jnp.where(
        net.c == 0, jnp.stack([packed, other], axis=1), jnp.stack([other, packed], axis=1)
    ).reshape(shards, packed.shape[1])
    conds = trees[:, tree_len + labels :]
    my_tree = lax.dynamic_index_in_dim(trees, net.s, 0, False)
    tree_seg = my_tree[:tree_len]
    parent_row = my_tree[tree_len : tree_len + labels]
    ada_rows = jnp.dot(conds, w_ada.astype(F32), precision=HIGH) + b_ada.astype(F32)
    small = jnp.concatenate([b_fc1, b_fc2, gain1, gain2]).astype(F32)
    pieces = jnp.concatenate(
        [ada_rows, jnp.broadcast_to(small[None], (shards, small.shape[0]))], axis=1
    )
    plane_w, tok, pieces, share, cot_give = lax.optimization_barrier(
        (plane_w, tok, pieces, share, cot_give)
    )
    cot_got = net.swap(cot_give)
    got = [lax.dynamic_index_in_dim(pieces, net.s, 0, False)]
    for k in range(1, shards):
        piece = lax.dynamic_index_in_dim(pieces, (net.s + k) % shards, 0, False)
        got.append(net.turn(piece, k))
    pack = net.gather_all(share)
    half_w = jnp.stack(plane_w)
    qkv_w = assemble(net.where, early_w, half_w, net.swap(half_w), shards)
    line = net.line_order(got)
    cut = ada_rows.shape[1]
    ada = line[:, :cut].reshape(-1)
    ends = [cut]
    for vec in (b_fc1, b_fc2, gain1, gain2):
        ends.append(ends[-1] + vec.shape[0])
    fc1_b, fc2_b, gain_a, gain_b = (
        line[:, ends[i] : ends[i + 1]].reshape(-1) for i in range(4)
    )
    shift_one, scale_one, gate_one, shift_two, scale_two, gate_two = jnp.split(ada, 6)

    half_seg = tree_seg.reshape(shards, 2, rows)

    def row_segs(half):
        return lax.dynamic_index_in_dim(half_seg, half, 1, False).reshape(-1)

    query_seg = row_segs(net.c)
    key_seg = jnp.stack(
        [query_seg.reshape(shards, rows), row_segs(1 - net.c).reshape(shards, rows)], axis=1
    ).reshape(-1)
    lanes = jnp.arange(LANES, dtype=F32)
    table = jnp.zeros((LANES,), F32).at[:labels].set(parent_row)
    up_two = jnp.sum(jnp.where(table[:, None] == lanes[None, :], table[None, :], 0.0), axis=1)
    reach = (
        (lanes[:, None] == lanes[None, :])
        | (table[:, None] == lanes[None, :])
        | (up_two[:, None] == lanes[None, :])
    )
    hot = (key_seg[:, None] == lanes[None, :]).astype(BF)
    hot_mine = hot.reshape(shards, 2, rows, LANES)[:, 0].reshape(mine, LANES)
    feat = mm(hot_mine, jnp.where(reach, 0.0, BIG).astype(BF)).astype(BF)
    held = jnp.max(hot.reshape(-1, SPAN, LANES), axis=1)
    asking = jnp.max(hot_mine.reshape(-1, BLOCK, LANES), axis=1)
    wanted = mm(asking, reach.astype(BF)).astype(BF)
    flags = (mm_t(wanted, held) > 0.5).reshape(-1).astype(jnp.int32)

    vec_one = jnp.stack([gain_a, 1.0 + scale_one, shift_one] + [gain_a] * 5)
    cot_both = net.by_core(cot_keep, cot_got).reshape(shards, rows, width)
    act_one, query, kv, peak = entry(tok, vec_one, qkv_w)
    kv, cot_both = lax.optimization_barrier((kv, cot_both))
    far = net.swap(kv)
    grad_out = net.exchange(cot_both)
    bound = jnp.max(peak[:1]).reshape(1)
    attn, log_totals = attn_fwd(query, kv, far, feat, hot, flags, bound, scale, PAIRS)
    vec = jnp.stack(
        [gate_one, gain_b, 1.0 + scale_two, shift_two, gate_two, fc2_b, fc2_b, fc2_b]
    )
    result, grad_attn, grad_mid, blocks, sums, g_b1 = middle(
        net.where, attn, tok, grad_out, vec, fc1_b[None], pack, groups
    )
    out_rows = net.from_trees(result)

    parts = net.group_sum(blocks.reshape(-1, 9 * width)).reshape(shards, -1, 9 * width)
    q_grads, near_grads, far_grads = attn_bwd(
        query, kv, far, feat, hot, flags, bound, attn, grad_attn, log_totals, scale, PAIRS
    )
    near_grads, parts, out_rows = lax.optimization_barrier((near_grads, parts, out_rows))
    out_keep, out_give = net.back(out_rows, batches)
    out_got = net.swap(out_give)
    turned = net.turns(parts)
    grad_in, g_mine, g_yours, late_sums = leave(
        net.where, q_grads, near_grads, net.swap(far_grads), act_one, qkv_w, tok, grad_mid,
        vec_one, (2, groups // 2, shards, part_rows),
    )

    turned, out_got, grad_in, g_mine, g_yours, late_sums = lax.optimization_barrier(
        (turned, out_got, grad_in, g_mine, g_yours, late_sums)
    )
    span = g_mine.shape[-1]
    g_got = net.swap(g_yours)
    grads_rows = net.from_trees(grad_in)
    small = jnp.concatenate(
        [late_sums[:2], sums[:4], late_sums[2:3], sums[4:6], g_b1.reshape(-1, width)]
    ).astype(BF)
    n_ada = 6 * width
    small_got = net.swap(small)
    rest_line = total([parts[0]] + turned).astype(BF)
    my_cond = lax.dynamic_index_in_dim(conds, net.s, 0, False)
    cond_top = my_cond.astype(BF)
    tree_extra = jnp.concatenate([cond_top, (my_cond - cond_top.astype(F32)).astype(BF)])
    g_got, small_got, rest_line, tree_extra = lax.optimization_barrier(
        (g_got, small_got, rest_line, tree_extra)
    )
    pairs = [
        total([g_mine[k], g_got[k]]).astype(BF).reshape(-1, span) for k in range(groups // 2)
    ]
    pair_small = total([small, small_got]).astype(BF).reshape(-1)
    per_tree = jnp.concatenate([pair_small[:n_ada], tree_extra, pair_small[n_ada:]])
    n_tree = per_tree.shape[0]
    if groups == 8:
        plane_terms = [pairs[0]] + [net.across(pairs[k], k) for k in range(1, 4)]
    else:
        plane_terms = [net.plane_sum(jnp.stack(pairs)[None])[0]]
    plane_small = net.spread(per_tree)
    plane_terms, plane_small, grads_rows, rest_line = lax.optimization_barrier(
        (plane_terms, plane_small, grads_rows, rest_line)
    )

    line_terms = total(plane_terms).astype(BF).reshape(shards, -1, span)
    every_plane = net.plane_order(plane_small)
    mid_part = n_ada + 2 * cond_dim
    bias_sum = jnp.sum(every_plane[:, mid_part:].astype(F32), axis=0).astype(BF)
    line_small = jnp.concatenate([every_plane[:, :mid_part].reshape(-1), bias_sum])
    n_line = line_small.shape[0]
    more = -(-n_line // (8 * span)) * 8
    line_small = jnp.pad(line_small, (0, more * span - n_line)).reshape(more, span)
    line_sent = jnp.concatenate(
        [line_terms, jnp.broadcast_to(line_small[None], (shards, more, span))], axis=1
    )
    line_got = net.turns(line_sent)
    rest_plane = net.spread(rest_line)
    grads_keep, grads_give = net.back(grads_rows, batches)
    grads_got = net.swap(grads_give)
    line_got, rest_plane, grads_got = lax.optimization_barrier((line_got, rest_plane, grads_got))
    rest_half = jnp.stack(rest_plane)
    rest_other = net.swap(rest_half)

    fine = line_terms.shape[1]
    qkv_sum = total([line_terms[0]] + [got[:fine] for got in line_got]).astype(BF)
    qkv_plane = net.spread(qkv_sum)
    everyone = net.line_order([line_small] + [got[fine:] for got in line_got])
    everyone = everyone.reshape(shards, -1)[:, :n_line].astype(F32)
    by_tree = everyone[:, : (groups // 2) * mid_part].reshape(shards, groups // 2, mid_part)
    t_out, t_fc1, t_fc2 = unpack(net.where, rest_half, rest_other, width)
    out = net.lay_out(out_keep, out_got)
    grads_x = net.lay_out(grads_keep, grads_got)

    every_dada = by_tree[:, :, : 6 * width].reshape(-1, 6 * width)
    every_cond = (
        by_tree[:, :, 6 * width : 6 * width + cond_dim] + by_tree[:, :, 6 * width + cond_dim :]
    ).reshape(-1, cond_dim)
    dada = lax.dynamic_index_in_dim(by_tree[:, :, : 6 * width], net.plane, 1, False)
    g_one, g_two, g_bias2, g_bias1 = jnp.split(
        jnp.sum(everyone[:, (groups // 2) * mid_part :], axis=0), [width, 2 * width, 3 * width]
    )

    def place(vec):
        n = vec.shape[-1] // shards
        return lax.dynamic_slice_in_dim(vec, net.s * n, n, vec.ndim - 1)

    dada_here = place(every_dada)
    t_ada = lax.dot_general(
        every_cond, dada_here, (((0,), (0,)), ((), ())), precision=HIGH
    )
    t_bada = jnp.sum(dada_here, axis=0)
    own = lax.dynamic_index_in_dim(dada.reshape(batches, 2, -1), net.c, 1, False)
    ada_w = qkv_w[:, 3 * width :].reshape(shards, cond_dim, -1).astype(F32)
    cond_total = jnp.einsum(
        "bsn,scn->bc", own.reshape(batches, shards, -1), ada_w, precision=HIGH
    )
    qkv_half = jnp.stack(qkv_plane)
    t_qkv = settle(net.where, qkv_half, net.swap(qkv_half)).reshape(w_qkv.shape)
    return (
        out,
        grads_x,
        cond_total[:, None, :],
        t_qkv,
        t_out,
        t_fc1,
        place(g_bias1),
        t_fc2,
        place(g_bias2),
        t_ada,
        t_bada,
        place(g_one),
        place(g_two),
    )


def solution(mesh):
    in_specs = (
        P(None, "group", "shard", None),
        P(None, "group", None),
        P(None, "group", None),
        P(None, "group", None),
        P(None, "group", "shard", None),
        P("shard", None),
        P("shard", None),
        P("shard", None),
        P("shard"),
        P("shard", None),
        P("shard"),
        P(None, "shard"),
        P("shard"),
        P("shard"),
        P("shard"),
    )
    out_specs = (
        P(None, "group", "shard", None),
        P(None, "group", "shard", None),
        P(None, "group", None),
        P("shard", None),
        P("shard", None),
        P("shard", None),
        P("shard"),
        P("shard", None),
        P("shard"),
        P(None, "shard"),
        P("shard"),
        P("shard"),
        P("shard"),
    )
    groups = mesh.shape["group"]

    def run(*args):
        return on_device(*args, groups)

    return jax.shard_map(
        run, mesh=mesh, in_specs=in_specs, out_specs=out_specs, check_vma=False
    )
```

```python
import functools
import math

import jax
import jax.numpy as jnp
from jax import lax
from jax.experimental import pallas as pl
from jax.experimental.pallas import tpu as pltpu
from jax.sharding import PartitionSpec as P

HEADS = 12
EPS = 1e-05
GELU_C = 0.7978845608028654
GELU_K = 0.044715
HIGH = lax.Precision.HIGHEST
BF = jnp.bfloat16
F32 = jnp.float32
BLOCK = 256
SPAN = 512
LANES = 128
BIG = -float(2**30)
MASKED = -1000000000.0
PAIRS = 6


def layer_norm(values):
    centred = values - jnp.mean(values, axis=-1, keepdims=True)
    inv_std = lax.rsqrt(jnp.mean(centred * centred, axis=-1, keepdims=True) + EPS)
    return centred * inv_std, inv_std


def norm_back(grad_normed, normed, inv_std):
    first_mean = jnp.mean(grad_normed, axis=-1, keepdims=True)
    second = jnp.mean(grad_normed * normed, axis=-1, keepdims=True)
    return (grad_normed - first_mean - normed * second) * inv_std


def gelu_parts(pre_act):
    inner_arg = GELU_C * (pre_act + GELU_K * pre_act * pre_act * pre_act)
    tangent = jnp.tanh(inner_arg)
    gelu_value = 0.5 * pre_act * (1.0 + tangent)
    gelu_slope = 0.5 * (1.0 + tangent) + 0.5 * pre_act * (1.0 - tangent * tangent) * GELU_C * (
        1.0 + 3.0 * GELU_K * pre_act * pre_act
    )
    return gelu_value, gelu_slope


def mm(left, right):
    return jnp.dot(left, right, preferred_element_type=F32)


def mm_t(left, right):
    return lax.dot_general(left, right, (((1,), (1,)), ((), ())), preferred_element_type=F32)


def t_mm(left, right):
    return lax.dot_general(left, right, (((0,), (0,)), ((), ())), preferred_element_type=F32)


def split_heads(pair):
    first = lax.broadcasted_iota(jnp.int32, pair.shape, 1) < LANES // 2
    zero = jnp.zeros_like(pair)
    return jnp.concatenate([jnp.where(first, pair, zero), jnp.where(first, zero, pair)], axis=0)

def side_by_side(stack):
    n = stack.shape[0] // 2
    return jnp.concatenate([stack[:n], stack[n:]], axis=1)

def as_row(column):
    return jnp.transpose(jnp.broadcast_to(column, (column.shape[0], LANES)))[:1]

def interleave(into, near_ref, far_ref):
    for i in range(near_ref.shape[0] // BLOCK):
        rows = slice(i * BLOCK, (i + 1) * BLOCK)
        into[2 * i * BLOCK : (2 * i + 1) * BLOCK, :] = near_ref[rows, :]
        into[(2 * i + 1) * BLOCK : (2 * i + 2) * BLOCK, :] = far_ref[rows, :]

def lane_groups(x):
    return [x[:, i : i + LANES] for i in range(0, x.shape[1], LANES)]

def is_safe(peak, far_keys, scale):
    top = jnp.maximum(peak, jnp.max(jnp.abs(far_keys.astype(F32))))
    return (peak * top * (scale * (LANES // 2)) < 2.0**27).astype(jnp.int32)

def lanes_sum(x): return jnp.sum(x, axis=1, keepdims=True)

def fwd_kernel(near, pp, scale, flags, peak_ref, q_ref, kn_ref, vn_ref, kf_ref, vf_ref, feat_ref, hot_ref, o_ref, lse_ref,
               s_ref, m_ref, l_ref, acc_ref, k_all, v_all, safe_ref):
    qb = pl.program_id(1)
    nk = hot_ref.shape[0] // SPAN
    @pl.when(qb == 0)
    def _():
        interleave(k_all, kn_ref, kf_ref)
        interleave(v_all, vn_ref, vf_ref)
        safe_ref[0] = is_safe(peak_ref[0], kf_ref[...], scale)
    safe = safe_ref[0] == 1
    feat = feat_ref[...]
    feat2 = jnp.concatenate([feat, feat], axis=0)
    qs = [split_heads(q_ref[:, p*LANES:(p+1)*LANES] * scale) for p in range(pp)]
    m_ref[...] = jnp.full(m_ref.shape, -jnp.inf, F32)
    def scan_scores(exact):
        def step(j, _):
            @pl.when((flags[qb * nk + j] == 1) | jnp.logical_not(safe))
            def _():
                rows = pl.ds(pl.multiple_of(j * SPAN, SPAN), SPAN)
                hot = hot_ref[rows, :]
                for p in range(pp):
                    k = k_all[rows, p*LANES:(p+1)*LANES]
                    if exact:
                        ok = mm_t(feat2, hot) > -1.0
                        s = jnp.where(ok, mm_t(qs[p], k), MASKED)
                    else:
                        s = mm_t(jnp.concatenate([qs[p], feat2], axis=1), jnp.concatenate([k, hot], axis=1))
                    s_ref[p, j] = s
                    m_ref[p] = functools.reduce(jnp.maximum, lane_groups(s), m_ref[p])
            return 0
        lax.fori_loop(0, nk, step, 0)
    @pl.when(safe)
    def _(): scan_scores(False)
    @pl.when(jnp.logical_not(safe))
    def _(): scan_scores(True)
    tops = [jnp.max(m_ref[p], axis=1, keepdims=True) for p in range(pp)]
    l_ref[...] = jnp.zeros(l_ref.shape, F32)
    acc_ref[...] = jnp.zeros(acc_ref.shape, F32)
    def step(j, _):
        @pl.when((flags[qb * nk + j] == 1) | jnp.logical_not(safe))
        def _():
            rows = pl.ds(pl.multiple_of(j * SPAN, SPAN), SPAN)
            for p in range(pp):
                e = jnp.exp(s_ref[p, j] - tops[p])
                l_ref[p] += sum(lane_groups(e))
                v = split_heads(v_all[rows, p*LANES:(p+1)*LANES])
                acc_ref[p] += mm(side_by_side(e.astype(BF)), v)
        return 0
    lax.fori_loop(0, nk, step, 0)
    for p in range(pp):
        total = lanes_sum(l_ref[p])
        lse_ref[p, 0] = as_row(tops[p] + jnp.log(total))
        first = lax.broadcasted_iota(jnp.int32, (BLOCK, LANES), 1) < LANES // 2
        o_ref[:, p*LANES:(p+1)*LANES] = (acc_ref[p] / jnp.where(first, total[:BLOCK], total[BLOCK:])).astype(BF)

def attn_fwd(q, kv, far, feat, hot, flags, peak, scale, pp):
    near, width = q.shape
    total = hot.shape[0]
    steps = width // LANES // pp
    nq = near // BLOCK
    col = lambda c: (lambda h, i, f: (0, c * steps + h))
    return pl.pallas_call(
        functools.partial(fwd_kernel, near, pp, scale),
        grid_spec=pltpu.PrefetchScalarGridSpec(
            num_scalar_prefetch=1, grid=(steps, nq),
            in_specs=[
                pl.BlockSpec(memory_space=pltpu.SMEM),
                pl.BlockSpec((BLOCK, pp*LANES), lambda h, i, f: (i, h)),
                pl.BlockSpec((near, pp*LANES), col(0)),
                pl.BlockSpec((near, pp*LANES), col(1)),
                pl.BlockSpec((near, pp*LANES), col(0)),
                pl.BlockSpec((near, pp*LANES), col(1)),
                pl.BlockSpec((BLOCK, LANES), lambda h, i, f: (i, 0)),
                pl.BlockSpec((total, LANES), lambda h, i, f: (0, 0)),
            ],
            out_specs=[
                pl.BlockSpec((BLOCK, pp*LANES), lambda h, i, f: (i, h)),
                pl.BlockSpec((pp, 1, 1, 2*BLOCK), lambda h, i, f: (h, i, 0, 0)),
            ],
            scratch_shapes=[
                pltpu.VMEM((pp, total // SPAN, 2*BLOCK, SPAN), F32),
                pltpu.VMEM((pp, 2*BLOCK, LANES), F32),
                pltpu.VMEM((pp, 2*BLOCK, LANES), F32),
                pltpu.VMEM((pp, BLOCK, LANES), F32),
                pltpu.VMEM((total, pp*LANES), BF),
                pltpu.VMEM((total, pp*LANES), BF),
                pltpu.SMEM((1,), jnp.int32),
            ]),
        out_shape=[jax.ShapeDtypeStruct((near, width), BF), jax.ShapeDtypeStruct((width // LANES, nq, 1, 2*BLOCK), F32)],
        compiler_params=pltpu.CompilerParams(vmem_limit_bytes=56<<20),
        cost_estimate=cost(38),
        name="attn_forward",
    )(flags, peak, q, kv, kv, far, far, feat, hot)

def bwd_kernel(near, pp, scale, flags, peak_ref, q_ref, kn_ref, vn_ref, kf_ref, vf_ref, feat_ref, hot_ref, o_ref, do_ref, lse_ref,
               dq_ref, near_ref, far_ref, k_all, v_all, k_turned, dk_acc, dv_acc, dq_acc, safe_ref):
    half = LANES // 2
    qb = pl.program_id(1)
    nk = hot_ref.shape[0] // SPAN
    @pl.when(qb == 0)
    def _():
        interleave(k_all, kn_ref, kf_ref)
        interleave(v_all, vn_ref, vf_ref)
        safe_ref[0] = is_safe(peak_ref[0], kf_ref[...], scale)
        k_turned[...] = jnp.transpose(k_all[...])
        dk_acc[...] = jnp.zeros(dk_acc.shape, F32)
        dv_acc[...] = jnp.zeros(dv_acc.shape, F32)
    safe = safe_ref[0] == 1
    feat = feat_ref[...]
    feat2 = jnp.concatenate([feat, feat], axis=0)
    dq_acc[...] = jnp.zeros(dq_acc.shape, F32)
    qs, dos, deltas, lses = [], [], [], []
    for p in range(pp):
        cols = slice(p*LANES, (p+1)*LANES)
        qs.append(split_heads(q_ref[:, cols] * scale))
        do2 = split_heads(do_ref[:, cols])
        dos.append(do2)
        o = o_ref[:, cols].astype(F32)
        deltas.append(as_row(lanes_sum(do2.astype(F32) * jnp.concatenate([o, o], axis=0))))
        lses.append(lse_ref[p, 0])
    def sweep(exact):
        def step(j, _):
            @pl.when((flags[qb * nk + j] == 1) | jnp.logical_not(safe))
            def _():
                rows = pl.ds(pl.multiple_of(j * SPAN, SPAN), SPAN)
                hot = hot_ref[rows, :]
                for p in range(pp):
                    cols = slice(p*LANES, (p+1)*LANES)
                    k = k_all[rows, cols]; v = v_all[rows, cols]
                    if exact:
                        ok = mm_t(hot, feat2) > -1.0
                        s = jnp.where(ok, mm_t(k, qs[p]), MASKED)
                    else:
                        s = mm_t(jnp.concatenate([k, hot], axis=1), jnp.concatenate([qs[p], feat2], axis=1))
                    prob = jnp.exp(s - lses[p])
                    dprob = mm_t(v, dos[p])
                    ds = prob * (dprob - deltas[p])
                    if exact:
                        ds = jnp.where(ok, ds, 0.0)
                    ds = ds.astype(BF)
                    dv_acc[rows, cols] += mm(prob.astype(BF), dos[p])
                    dk_acc[rows, cols] += mm(ds, qs[p])
                    for h in range(2):
                        kt = k_turned[p*LANES + h*half : p*LANES + (h+1)*half, rows]
                        dq_acc[p, h*half:(h+1)*half] += mm(kt, ds[:, h*BLOCK:(h+1)*BLOCK])
            return 0
        lax.fori_loop(0, nk, step, 0)
    @pl.when(safe)
    def _(): sweep(False)
    @pl.when(jnp.logical_not(safe))
    def _(): sweep(True)
    for p in range(pp):
        dq_ref[:, p*LANES:(p+1)*LANES] = jnp.transpose(dq_acc[p] * scale).astype(BF)
    @pl.when(qb == pl.num_programs(1) - 1)
    def _():
        for i in range(near // BLOCK):
            rows = slice(i * BLOCK, (i + 1) * BLOCK)
            for side, acc in enumerate((dk_acc, dv_acc)):
                near_ref[side, rows] = acc[2 * i * BLOCK : (2 * i + 1) * BLOCK]
                far_ref[side, rows] = acc[(2 * i + 1) * BLOCK : (2 * i + 2) * BLOCK].astype(BF)

def attn_bwd(q, kv, far, feat, hot, flags, peak, attn, dattn, lse, scale, pp):
    near, width = q.shape
    total = hot.shape[0]
    steps = width // LANES // pp
    nq = near // BLOCK
    col = lambda c: (lambda h, i, f: (0, c * steps + h))
    rowblk = pl.BlockSpec((BLOCK, pp*LANES), lambda h, i, f: (i, h))
    whole = pl.BlockSpec((near, pp*LANES), col(0))
    both = pl.BlockSpec((2, near, pp*LANES), lambda h, i, f: (0, 0, h))
    return pl.pallas_call(
        functools.partial(bwd_kernel, near, pp, scale),
        grid_spec=pltpu.PrefetchScalarGridSpec(
            num_scalar_prefetch=1, grid=(steps, nq),
            in_specs=[
                pl.BlockSpec(memory_space=pltpu.SMEM),
                rowblk,
                pl.BlockSpec((near, pp*LANES), col(0)),
                pl.BlockSpec((near, pp*LANES), col(1)),
                whole,
                pl.BlockSpec((near, pp*LANES), col(1)),
                pl.BlockSpec((BLOCK, LANES), lambda h, i, f: (i, 0)),
                pl.BlockSpec((total, LANES), lambda h, i, f: (0, 0)),
                rowblk, rowblk,
                pl.BlockSpec((pp, 1, 1, 2*BLOCK), lambda h, i, f: (h, i, 0, 0)),
            ],
            out_specs=[rowblk, both, both],
            scratch_shapes=[
                pltpu.VMEM((total, pp*LANES), BF),
                pltpu.VMEM((total, pp*LANES), BF),
                pltpu.VMEM((pp*LANES, total), BF),
                pltpu.VMEM((total, pp*LANES), F32),
                pltpu.VMEM((total, pp*LANES), F32),
                pltpu.VMEM((pp, LANES, BLOCK), F32),
                pltpu.SMEM((1,), jnp.int32),
            ]),
        out_shape=[
            jax.ShapeDtypeStruct((near, width), BF),
            jax.ShapeDtypeStruct((2, near, width), F32),
            jax.ShapeDtypeStruct((2, near, width), BF),
        ],
        compiler_params=pltpu.CompilerParams(vmem_limit_bytes=56<<20),
        cost_estimate=cost(63),
        name="attn_backward",
    )(flags, peak, q, kv, kv, far, far, feat, hot, attn, dattn, lse)


def assemble_kernel(shards, where, own_ref, half_ref, other_ref, out_ref):
    s, c, plane = where[0], where[1], where[2]
    groups, planes = own_ref.shape[0], half_ref.shape[0]
    out_ref[pl.ds(s * groups, groups)] = own_ref[...]
    for side, source in ((c, half_ref), (1 - c, other_ref)):
        for j in range(planes):
            for k in range(1, shards):
                place = lax.rem(s + shards - k, shards)
                out_ref[place * groups + side * planes + (plane ^ j)] = source[j, k - 1]


def assemble(where, own, half, other, shards):
    rows, width = own.shape
    fine = half.shape[2]
    groups = rows // fine
    full = lambda *shape: pl.BlockSpec(shape, lambda i, w: (0,) * len(shape))
    out = pl.pallas_call(
        functools.partial(assemble_kernel, shards),
        grid_spec=pltpu.PrefetchScalarGridSpec(
            num_scalar_prefetch=1,
            grid=(1,),
            in_specs=[full(groups, fine, width), full(*half.shape), full(*half.shape)],
            out_specs=full(groups * shards, fine, width),
        ),
        out_shape=jax.ShapeDtypeStruct((groups * shards, fine, width), own.dtype),
        compiler_params=pltpu.CompilerParams(vmem_limit_bytes=60 << 20),
        name="assemble",
    )(where, own.reshape(groups, fine, width), half, other)
    return out.reshape(shards * rows, width)


def entry_kernel(tok_ref, vec_ref, w_ref, act_ref, q_ref, kv_ref, peak_ref):
    step = pl.program_id(0)
    rows, pieces = BLOCK, tok_ref.shape[0] // BLOCK

    @pl.when(step == 0)
    def _():
        gain, lift, shift = (vec_ref[i : i + 1, :] for i in range(3))
        for i in range(pieces):
            at = slice(i * rows, (i + 1) * rows)
            normed, _unused = layer_norm(tok_ref[at, :].astype(F32))
            act_ref[at, :] = (normed * gain * lift + shift).astype(BF)
        peak_ref[...] = jnp.zeros_like(peak_ref)

    top = jnp.zeros((1, w_ref.shape[1]), F32)
    for i in range(pieces):
        at = slice(i * rows, (i + 1) * rows)
        value = mm(act_ref[at, :], w_ref[...])
        low = value.astype(BF)
        top = jnp.maximum(top, jnp.max(jnp.abs(low.astype(F32)), axis=0, keepdims=True))

        @pl.when(step < 2)
        def _():
            kv_ref[at, :] = low

        @pl.when(step == 2)
        def _():
            q_ref[at, :] = low

    peak_ref[0:1, :] = jnp.maximum(peak_ref[0:1, :], top)


def entry(tok, vec, qkv_w):
    total, width = tok.shape
    fixed = lambda *shape: pl.BlockSpec(shape, lambda j: (0,) * len(shape))
    return pl.pallas_call(
        entry_kernel,
        grid=(3,),
        in_specs=[
            fixed(total, width), fixed(8, width),
            pl.BlockSpec((width, width), lambda j: (0, lax.rem(j + 1, 3))),
        ],
        out_specs=[
            fixed(total, width), fixed(total, width),
            pl.BlockSpec((total, width), lambda j: (0, jnp.minimum(j, 1))),
            fixed(8, width),
        ],
        out_shape=[
            jax.ShapeDtypeStruct((total, width), BF),
            jax.ShapeDtypeStruct((total, width), BF),
            jax.ShapeDtypeStruct((total, 2 * width), BF),
            jax.ShapeDtypeStruct((8, width), F32),
        ],
        compiler_params=pltpu.CompilerParams(vmem_limit_bytes=48 << 20),
        cost_estimate=cost(9),
        name="entry",
    )(tok, vec, qkv_w)


def leave_kernel(spots, where, dq_ref, near_ref, far_ref, act_ref, w_ref, tok_ref, dmid_ref, vec_ref,
                 grad_ref, mine_ref, yours_ref, sums_ref, d_all, da):
    step = pl.program_id(0)
    total = dq_ref.shape[0]
    sides, planes, places, fine = spots

    @pl.when(step == 0)
    def _():
        d_all[...] = dq_ref[...]
        da[...] = jnp.zeros_like(da)

    @pl.when(step > 0)
    def _():
        d_all[...] = (near_ref[0] + far_ref[0].astype(F32)).astype(BF)

    grad = t_mm(act_ref[...], d_all[...])

    def put(ref, side):
        for place in range(places):
            turned = lax.rem(place + places - where[0], places)
            for plane in range(planes):
                start = ((place * sides + side) * planes + plane) * fine
                ref[plane ^ where[2], turned] = grad[start : start + fine].astype(BF)

    for side in range(sides):
        pl.when(where[1] == side)(functools.partial(put, mine_ref, side))
        pl.when(where[1] != side)(functools.partial(put, yours_ref, side))

    def add(r, _):
        rows = pl.ds(pl.multiple_of(r * BLOCK, BLOCK), BLOCK)
        da[rows, :] += mm_t(d_all[rows, :], w_ref[...])
        return 0

    lax.fori_loop(0, total // BLOCK, add, 0)

    @pl.when(step == 2)
    def _():
        gain, lift, shift = (vec_ref[i : i + 1, :] for i in range(3))
        sums_ref[...] = jnp.zeros_like(sums_ref)

        def finish(r, _):
            rows = pl.ds(pl.multiple_of(r * BLOCK, BLOCK), BLOCK)
            normed, inv = layer_norm(tok_ref[rows, :].astype(F32))
            part = da[rows, :]
            grad_h = part * lift
            back = norm_back(grad_h * gain, normed, inv)
            grad_ref[rows, :] = (dmid_ref[rows, :] + back).astype(BF)
            for i, term in enumerate((part, part * (normed * gain), grad_h * normed)):
                sums_ref[i : i + 1, :] += jnp.sum(term, axis=0, keepdims=True)
            return 0

        lax.fori_loop(0, total // BLOCK, finish, 0)


def leave(where, q_grads, near, far, act, qkv_w, tok, dmid, vec, spots):
    total, width = q_grads.shape
    keep = pl.Buffered(1)
    whole = pl.BlockSpec((total, width), lambda j, w: (0, 0), pipeline_mode=keep)
    both = pl.BlockSpec((1, total, width), lambda j, w: (jnp.maximum(j - 1, 0), 0, 0))
    small = pl.BlockSpec((8, width), lambda j, w: (0, 0))
    part = pl.BlockSpec(tuple(spots[1:]) + (width,), lambda j, w: (0, 0, 0, j))
    return pl.pallas_call(
        functools.partial(leave_kernel, spots),
        grid_spec=pltpu.PrefetchScalarGridSpec(
            num_scalar_prefetch=1,
            grid=(3,),
            in_specs=[
                whole, both, both, whole,
                pl.BlockSpec((width, width), lambda j, w: (0, j)),
                whole, whole, small,
            ],
            out_specs=[
                whole,
                part, part,
                small,
            ],
            scratch_shapes=[pltpu.VMEM((total, width), BF), pltpu.VMEM((total, width), F32)],
        ),
        out_shape=[
            jax.ShapeDtypeStruct((total, width), BF),
            jax.ShapeDtypeStruct(tuple(spots[1:]) + (3 * width,), BF),
            jax.ShapeDtypeStruct(tuple(spots[1:]) + (3 * width,), BF),
            jax.ShapeDtypeStruct((8, width), F32),
        ],
        compiler_params=pltpu.CompilerParams(vmem_limit_bytes=56 << 20),
        cost_estimate=cost(14),
        name="leave",
    )(where, q_grads, near, far, act, qkv_w, tok, dmid, vec)


def settle_kernel(where, half_ref, other_ref, out_ref):
    c, plane = where[1], where[2]
    for side, source in ((c, half_ref), (1 - c, other_ref)):
        for j in range(half_ref.shape[0]):
            out_ref[side * half_ref.shape[0] + (plane ^ j)] = source[j].astype(F32)


def settle(where, half, other):
    planes, fine, width = half.shape
    full = lambda *shape: pl.BlockSpec(shape, lambda i, w: (0,) * len(shape))
    return pl.pallas_call(
        settle_kernel,
        grid_spec=pltpu.PrefetchScalarGridSpec(
            num_scalar_prefetch=1,
            grid=(1,),
            in_specs=[full(planes, fine, width)] * 2,
            out_specs=full(2 * planes, fine, width),
        ),
        out_shape=jax.ShapeDtypeStruct((2 * planes, fine, width), F32),
        compiler_params=pltpu.CompilerParams(vmem_limit_bytes=40 << 20),
        name="settle",
    )(where, half, other)


def unpack_kernel(count, where, half_ref, other_ref, out_ref, fc1_ref, fc2_ref):
    step = pl.program_id(0)
    c, plane = where[1], where[2]

    def fill(ref):
        for side, source in ((c, half_ref), (1 - c, other_ref)):
            for j in range(source.shape[0]):
                ref[2 * (plane ^ j) + side] = source[j].astype(F32).reshape(ref.shape[1:])

    @pl.when(step == 0)
    def _():
        fill(out_ref)

    @pl.when((step > 0) & (step <= count))
    def _():
        fill(fc1_ref)

    @pl.when(step > count)
    def _():
        fill(fc2_ref)


def unpack(where, half, other, width):
    planes, fine, total = half.shape
    groups, count = 2 * planes, total // width // 2
    block = pl.BlockSpec((planes, fine, width), lambda i, w: (0, 0, i))
    low = lambda i: jnp.clip(i, 0, count - 1)
    out, fc1, fc2 = pl.pallas_call(
        functools.partial(unpack_kernel, count),
        grid_spec=pltpu.PrefetchScalarGridSpec(
            num_scalar_prefetch=1,
            grid=(1 + 2 * count,),
            in_specs=[block, block],
            out_specs=[
                pl.BlockSpec((groups, fine, width), lambda i, w: (0, 0, 0)),
                pl.BlockSpec((groups, fine, width), lambda i, w: (0, 0, low(i - 1))),
                pl.BlockSpec((groups, 1, fine, width), lambda i, w: (0, low(i - 1 - count), 0, 0)),
            ],
        ),
        out_shape=[
            jax.ShapeDtypeStruct((groups, fine, width), F32),
            jax.ShapeDtypeStruct((groups, fine, count * width), F32),
            jax.ShapeDtypeStruct((groups, count, fine, width), F32),
        ],
        compiler_params=pltpu.CompilerParams(vmem_limit_bytes=40 << 20),
        cost_estimate=cost(4),
        name="unpack",
    )(where, half, other)
    return out.reshape(-1, width), fc1.reshape(-1, count * width), fc2.reshape(-1, width)


def cost(microseconds):
    return pl.CostEstimate(
        flops=int(microseconds * 1.15e9), bytes_accessed=1 << 20, transcendentals=0
    )


def middle_kernel(chunks, where, attn_ref, tok_ref, cot_ref, vec_ref, b1_ref, wo_ref, w1_ref, *rest):
    w2_refs, rest = rest[:chunks], rest[chunks:]
    (out_ref, dattn_ref, dmid_ref, grads_ref, sums_ref, gb1_ref) = rest[:6]
    (mid, branch, act, dy, two, da, hid, dpre, w2, wide, tall, sems) = rest[6:]
    width = attn_ref.shape[1]

    def send_wide(column):
        cols = pl.ds(pl.multiple_of(column * width, LANES), width)
        return pltpu.make_async_copy(wide, grads_ref.at[:, :, :, cols], sems.at[0])

    def turned(place):
        return lax.rem(place + chunks - where[0], chunks)

    def send_tall(place):
        cols = pl.ds((1 + chunks) * width, chunks * width)
        return pltpu.make_async_copy(tall, grads_ref.at[:, turned(place), :, cols], sems.at[1])

    step = pl.program_id(0)
    total = attn_ref.shape[0]
    blocks = total // BLOCK
    gate_one, gain, lift, shift, gate_two, fc2_b = (vec_ref[i : i + 1, :] for i in range(6))

    def rows_of(r):
        return pl.ds(pl.multiple_of(r * BLOCK, BLOCK), BLOCK)

    @pl.when(step == 0)
    def _():
        sums_ref[...] = jnp.zeros_like(sums_ref)

        def start(r, _):
            rows = rows_of(r)
            one = mm(attn_ref[rows, :], wo_ref[...])
            middle = tok_ref[rows, :].astype(F32) + gate_one * one
            normed, _unused = layer_norm(middle)
            branch[rows, :] = one
            mid[rows, :] = middle
            act[rows, :] = (normed * gain * lift + shift).astype(BF)
            dy[rows, :] = (cot_ref[rows, :].astype(F32) * gate_two).astype(BF)
            two[rows, :] = jnp.zeros((BLOCK, two.shape[1]), F32)
            da[rows, :] = jnp.zeros((BLOCK, da.shape[1]), F32)
            return 0

        lax.fori_loop(0, blocks, start, 0)

    @pl.when(step < chunks)
    def _():
        height = w2_refs[0].shape[0]
        for b in range(chunks):
            w2[b * height : (b + 1) * height, :] = w2_refs[b][...]
        gb1_ref[...] = jnp.zeros_like(gb1_ref)

        def chunk(r, _):
            rows = rows_of(r)
            value, slope = gelu_parts(mm(act[rows, :], w1_ref[...]) + b1_ref[...])
            hidden = value.astype(BF)
            hid[rows, :] = hidden
            two[rows, :] += mm(hidden, w2[...])
            grad = (mm_t(dy[rows, :], w2[...]) * slope).astype(BF)
            dpre[rows, :] = grad
            gb1_ref[...] += jnp.sum(grad.astype(F32), axis=0, keepdims=True)
            da[rows, :] += mm_t(grad, w1_ref[...])
            return 0

        lax.fori_loop(0, blocks, chunk, 0)
        grad_two = t_mm(hid[...], dy[...])
        grad_one = t_mm(act[...], dpre[...])

        @pl.when(step > 0)
        def _():
            send_wide(step).wait()
            send_tall(step - 1).wait()

        groups, fine = tall.shape[:2]
        for g in range(groups):
            for b in range(chunks):
                start = (g * chunks + b) * fine
                tall[g, :, b * width : (b + 1) * width] = grad_two[start : start + fine].astype(BF)
        put_blocks(wide, grad_one, turned)
        send_wide(step + 1).start()
        send_tall(step).start()

    @pl.when(step == chunks)
    def _():
        def finish(r, _):
            rows = rows_of(r)
            cot = cot_ref[rows, :].astype(F32)
            middle = mid[rows, :]
            second = two[rows, :] + fc2_b
            out_ref[rows, :] = (middle + gate_two * second).astype(BF)
            normed, inv = layer_norm(middle)
            lifted = normed * gain
            grad = da[rows, :]
            grad_h = grad * lift
            dmid = cot + norm_back(grad_h * gain, normed, inv)
            dmid_ref[rows, :] = dmid
            dy_one = (dmid * gate_one).astype(BF)
            dpre[rows, :] = dy_one
            dattn_ref[rows, :] = mm_t(dy_one, wo_ref[...]).astype(BF)
            parts = (
                dmid * branch[rows, :], grad, grad * lifted, cot * second,
                grad_h * normed, dy[rows, :].astype(F32),
            )
            for i, part in enumerate(parts):
                sums_ref[i : i + 1, :] += jnp.sum(part, axis=0, keepdims=True)
            return 0

        lax.fori_loop(0, blocks, finish, 0)
        grad_out = t_mm(attn_ref[...], dpre[...])
        send_wide(step).wait()
        send_tall(step - 1).wait()
        put_blocks(wide, grad_out, turned)
        send_wide(0).start()
        send_wide(0).wait()


def put_blocks(ref, grad, turned):
    groups, places, rows = ref.shape[:3]
    for s in range(places):
        for g in range(groups):
            start = (s * groups + g) * rows
            ref[g, turned(s)] = grad[start : start + rows].astype(BF)


def middle(where, attn, tok, cot, vec, fc1_b, pack, groups):
    total, width = attn.shape
    shards = pack.shape[1] // width - 5
    fine = width // shards // groups
    keep = pl.Buffered(1)
    whole = pl.BlockSpec((total, width), lambda i, w: (0, 0), pipeline_mode=keep)
    last = shards - 1
    low = lambda i: jnp.minimum(i, last)
    w2_spec = lambda b: pl.BlockSpec((width // shards, width), lambda i, w: (low(i), 5 + b))
    return pl.pallas_call(
        functools.partial(middle_kernel, shards),
        grid_spec=pltpu.PrefetchScalarGridSpec(
            num_scalar_prefetch=1,
            grid=(shards + 1,),
            in_specs=[
            whole, whole, whole,
            pl.BlockSpec((8, width), lambda i, w: (0, 0)),
            pl.BlockSpec((1, width), lambda i, w: (0, low(i))),
            pl.BlockSpec((width, width), lambda i, w: (0, 0), pipeline_mode=keep),
            pl.BlockSpec((width, width), lambda i, w: (0, 1 + low(i))),
        ] + [w2_spec(b) for b in range(shards)],
        out_specs=[
            whole, whole, whole,
            pl.BlockSpec(memory_space=pl.ANY),
            pl.BlockSpec((8, width), lambda i, w: (0, 0)),
            pl.BlockSpec((1, width), lambda i, w: (0, low(i))),
        ],
        scratch_shapes=[
            pltpu.VMEM((total, width), F32),
            pltpu.VMEM((total, width), F32),
            pltpu.VMEM((total, width), BF),
            pltpu.VMEM((total, width), BF),
            pltpu.VMEM((total, width), F32),
            pltpu.VMEM((total, width), F32),
            pltpu.VMEM((total, width), BF),
            pltpu.VMEM((total, width), BF),
            pltpu.VMEM((width, width), BF),
            pltpu.VMEM((groups, shards, fine, width), BF),
            pltpu.VMEM((groups, fine, shards * width), BF),
            pltpu.SemaphoreType.DMA((2,)),
        ],
        ),
        out_shape=[
            jax.ShapeDtypeStruct((total, width), BF),
            jax.ShapeDtypeStruct((total, width), BF),
            jax.ShapeDtypeStruct((total, width), F32),
            jax.ShapeDtypeStruct((groups, shards, fine, 9 * width), BF),
            jax.ShapeDtypeStruct((8, width), F32),
            jax.ShapeDtypeStruct((1, 4 * width), F32),
        ],
        compiler_params=pltpu.CompilerParams(vmem_limit_bytes=60 << 20),
        cost_estimate=cost(55),
        name="middle",
    )(where, attn, tok, cot, vec, fc1_b, pack, pack, *([pack] * shards))


class Links:
    def __init__(self, groups, shards):
        self.groups, self.shards, self.planes = groups, shards, groups // 2
        self.g = lax.axis_index("group")
        self.s = lax.axis_index("shard")
        self.c = self.g % 2
        self.plane = self.g // 2
        tilt = self.plane if self.planes == 4 else 0 * self.plane
        self.where = jnp.stack([self.s, self.c, tilt]).astype(jnp.int32)

    def swap(self, value):
        return lax.ppermute(value, "group", [(i, i ^ 1) for i in range(self.groups)])

    def turn(self, value, step):
        n = self.shards
        return lax.ppermute(value, "shard", [(i, (i + step) % n) for i in range(n)])

    def across(self, value, step):
        return lax.ppermute(value, "group", [(i, i ^ (2 * step)) for i in range(self.groups)])

    def give(self, value):
        batches, rows, width = value.shape
        halves = value.reshape(batches, 2, rows // 2, width)
        keep = lax.dynamic_index_in_dim(halves, self.c, 1, False)
        return keep, lax.dynamic_index_in_dim(halves, 1 - self.c, 1, False)

    def to_trees(self, keep, got):
        return self.exchange(self.by_core(keep, got).reshape(-1, *keep.shape[1:]))

    def exchange(self, by_tree):
        return lax.all_to_all(by_tree, "shard", 0, 0).reshape(-1, by_tree.shape[-1])

    def by_core(self, mine, other):
        return jnp.where(
            self.c == 0, jnp.stack([mine, other], axis=1), jnp.stack([other, mine], axis=1)
        )

    def from_trees(self, value):
        return lax.all_to_all(
            value.reshape(self.shards, -1, value.shape[1]), "shard", 0, 0
        )

    def back(self, value, batches):
        by_core = value.reshape(batches, 2, *value.shape[1:])
        keep = lax.dynamic_index_in_dim(by_core, self.c, 1, False)
        return keep, lax.dynamic_index_in_dim(by_core, 1 - self.c, 1, False)

    def lay_out(self, keep, got):
        return self.by_core(keep, got).reshape(keep.shape[0], 1, -1, keep.shape[-1])

    def plane_order(self, parts):
        stacked = jnp.stack(parts)
        if self.planes != 4:
            return stacked
        return jnp.stack(
            [lax.dynamic_index_in_dim(stacked, self.plane ^ j, 0, False) for j in range(4)]
        )

    def line_order(self, parts):
        stacked = jnp.stack(parts)
        return jnp.stack(
            [
                lax.dynamic_index_in_dim(stacked, (self.s - j) % self.shards, 0, False)
                for j in range(self.shards)
            ]
        )

    def gather_all(self, part):
        return lax.all_gather(part, ("shard", "group"), axis=0, tiled=True)

    def my_rows(self, weight):
        rows = weight.shape[-2] // self.groups
        return lax.dynamic_slice_in_dim(weight, self.g * rows, rows, weight.ndim - 2)

    def group_sum(self, blocks):
        out = lax.psum_scatter(blocks, "group", scatter_dimension=0, tiled=True)
        return out

    def plane_sum(self, value):
        if self.planes != 4:
            groups = [[2 * p + c for p in range(self.planes)] for c in range(2)]
            return lax.psum_scatter(
                value, "group", scatter_dimension=1, axis_index_groups=groups
            ).astype(F32)
        total = lax.dynamic_index_in_dim(value, self.plane, 1, False).astype(F32)
        for k in range(1, 4):
            piece = lax.dynamic_index_in_dim(value, self.plane ^ k, 1, False)
            total = total + self.across(piece, k).astype(F32)
        return total

    def plane_gather(self, value):
        if self.planes != 4:
            groups = [[2 * p + c for p in range(self.planes)] for c in range(2)]
            return lax.all_gather(value, "group", axis_index_groups=groups)
        parts = jnp.stack([value] + [self.across(value, k) for k in range(1, 4)])
        return jnp.stack(
            [lax.dynamic_index_in_dim(parts, self.plane ^ j, 0, False) for j in range(4)]
        )

    def turns(self, values):
        return [self.turn(values[k], k) for k in range(1, self.shards)]

    def spread(self, value):
        if self.planes != 4:
            every = self.plane_gather(value)
            return [every[j] for j in range(self.planes)]
        return [value] + [self.across(value, k) for k in range(1, 4)]


def total(terms):
    result = terms[0].astype(F32)
    for term in terms[1:]:
        result = result + term.astype(F32)
    return result


def on_device(
    tokens,
    cond,
    seg_ids,
    parents,
    cotangent,
    w_qkv,
    w_out,
    w_fc1,
    b_fc1,
    w_fc2,
    b_fc2,
    w_ada,
    b_ada,
    gain1,
    gain2,
    groups,
):
    batches, _, row_count, width = tokens.shape
    shards = lax.axis_size("shard")
    assert shards == 2 * batches and groups % 2 == 0
    head_dim = width // HEADS
    scale = 1.0 / math.sqrt(head_dim)
    net = Links(groups, shards)
    rows = row_count // 2
    mine = shards * rows
    tree_len = seg_ids.shape[2]
    labels = parents.shape[2]
    cond_dim = cond.shape[2]

    fc2_blocks = net.my_rows(w_fc2.reshape(shards, -1, width))
    share = jnp.concatenate(
        [net.my_rows(w_out), net.my_rows(w_fc1)] + [fc2_blocks[b] for b in range(shards)],
        axis=1,
    )

    packed = jnp.concatenate(
        [seg_ids[:, 0].astype(F32), parents[:, 0].astype(F32), cond[:, 0]], axis=1
    )
    part_rows = w_qkv.shape[0] // groups
    early_w = jnp.concatenate([w_qkv, w_ada.reshape(-1, width)], axis=1)
    own_part = lax.dynamic_index_in_dim(
        early_w.reshape(groups, part_rows, -1), net.c * (groups // 2) + net.plane, 0, False
    )
    tok_keep, tok_give = net.give(tokens[:, 0])
    other = net.swap(packed)
    line_w = net.turns([own_part] * shards)
    tok_got = net.swap(tok_give)
    other, line_w, tok_got, share = lax.optimization_barrier((other, line_w, tok_got, share))
    pack = net.gather_all(share)
    tok = net.to_trees(tok_keep, tok_got)
    plane_w = net.spread(jnp.stack(line_w))
    cot_keep, cot_give = net.give(cotangent[:, 0])
    trees = jnp.where(
        net.c == 0, jnp.stack([packed, other], axis=1), jnp.stack([other, packed], axis=1)
    ).reshape(shards, packed.shape[1])
    conds = trees[:, tree_len + labels :]
    my_tree = lax.dynamic_index_in_dim(trees, net.s, 0, False)
    tree_seg = my_tree[:tree_len]
    parent_row = my_tree[tree_len : tree_len + labels]
    ada_rows = jnp.dot(conds, w_ada.astype(F32), precision=HIGH) + b_ada.astype(F32)
    small = jnp.concatenate([b_fc1, b_fc2, gain1, gain2]).astype(F32)
    pieces = jnp.concatenate(
        [ada_rows, jnp.broadcast_to(small[None], (shards, small.shape[0]))], axis=1
    )
    plane_w, tok, pieces, cot_give = lax.optimization_barrier(
        (plane_w, tok, pieces, cot_give)
    )
    cot_got = net.swap(cot_give)
    got = [lax.dynamic_index_in_dim(pieces, net.s, 0, False)]
    for k in range(1, shards):
        piece = lax.dynamic_index_in_dim(pieces, (net.s + k) % shards, 0, False)
        got.append(net.turn(piece, k))
    half_w = jnp.stack(plane_w)
    qkv_w = assemble(net.where, early_w, half_w, net.swap(half_w), shards)
    line = net.line_order(got)
    cut = ada_rows.shape[1]
    ada = line[:, :cut].reshape(-1)
    ends = [cut]
    for vec in (b_fc1, b_fc2, gain1, gain2):
        ends.append(ends[-1] + vec.shape[0])
    fc1_b, fc2_b, gain_a, gain_b = (
        line[:, ends[i] : ends[i + 1]].reshape(-1) for i in range(4)
    )
    shift_one, scale_one, gate_one, shift_two, scale_two, gate_two = jnp.split(ada, 6)

    half_seg = tree_seg.reshape(shards, 2, rows)

    def row_segs(half):
        return lax.dynamic_index_in_dim(half_seg, half, 1, False).reshape(-1)

    query_seg = row_segs(net.c)
    key_seg = jnp.stack(
        [query_seg.reshape(shards, rows), row_segs(1 - net.c).reshape(shards, rows)], axis=1
    ).reshape(-1)
    lanes = jnp.arange(LANES, dtype=F32)
    table = jnp.zeros((LANES,), F32).at[:labels].set(parent_row)
    up_two = jnp.sum(jnp.where(table[:, None] == lanes[None, :], table[None, :], 0.0), axis=1)
    reach = (
        (lanes[:, None] == lanes[None, :])
        | (table[:, None] == lanes[None, :])
        | (up_two[:, None] == lanes[None, :])
    )
    hot = (key_seg[:, None] == lanes[None, :]).astype(BF)
    hot_mine = hot.reshape(shards, 2, rows, LANES)[:, 0].reshape(mine, LANES)
    feat = mm(hot_mine, jnp.where(reach, 0.0, BIG).astype(BF)).astype(BF)
    held = jnp.max(hot.reshape(-1, SPAN, LANES), axis=1)
    asking = jnp.max(hot_mine.reshape(-1, BLOCK, LANES), axis=1)
    wanted = mm(asking, reach.astype(BF)).astype(BF)
    flags = (mm_t(wanted, held) > 0.5).reshape(-1).astype(jnp.int32)

    vec_one = jnp.stack([gain_a, 1.0 + scale_one, shift_one] + [gain_a] * 5)
    cot_both = net.by_core(cot_keep, cot_got).reshape(shards, rows, width)
    act_one, query, kv, peak = entry(tok, vec_one, qkv_w)
    kv, cot_both = lax.optimization_barrier((kv, cot_both))
    far = net.swap(kv)
    grad_out = net.exchange(cot_both)
    bound = jnp.max(peak[:1]).reshape(1)
    attn, log_totals = attn_fwd(query, kv, far, feat, hot, flags, bound, scale, PAIRS)
    vec = jnp.stack(
        [gate_one, gain_b, 1.0 + scale_two, shift_two, gate_two, fc2_b, fc2_b, fc2_b]
    )
    result, grad_attn, grad_mid, blocks, sums, g_b1 = middle(
        net.where, attn, tok, grad_out, vec, fc1_b[None], pack, groups
    )
    out_rows = net.from_trees(result)

    parts = net.group_sum(blocks.reshape(-1, 9 * width)).reshape(shards, -1, 9 * width)
    q_grads, near_grads, far_grads = attn_bwd(
        query, kv, far, feat, hot, flags, bound, attn, grad_attn, log_totals, scale, PAIRS
    )
    near_grads, parts, out_rows = lax.optimization_barrier((near_grads, parts, out_rows))
    out_keep, out_give = net.back(out_rows, batches)
    out_got = net.swap(out_give)
    turned = net.turns(parts)
    grad_in, g_mine, g_yours, late_sums = leave(
        net.where, q_grads, near_grads, net.swap(far_grads), act_one, qkv_w, tok, grad_mid,
        vec_one, (2, groups // 2, shards, part_rows),
    )

    turned, out_got, grad_in, g_mine, g_yours, late_sums = lax.optimization_barrier(
        (turned, out_got, grad_in, g_mine, g_yours, late_sums)
    )
    span = g_mine.shape[-1]
    g_got = net.swap(g_yours)
    grads_rows = net.from_trees(grad_in)
    small = jnp.concatenate(
        [late_sums[:2], sums[:4], late_sums[2:3], sums[4:6], g_b1.reshape(-1, width)]
    ).astype(BF)
    n_ada = 6 * width
    small_got = net.swap(small)
    rest_line = total([parts[0]] + turned).astype(BF)
    my_cond = lax.dynamic_index_in_dim(conds, net.s, 0, False)
    cond_top = my_cond.astype(BF)
    tree_extra = jnp.concatenate([cond_top, (my_cond - cond_top.astype(F32)).astype(BF)])
    g_got, small_got, rest_line, tree_extra = lax.optimization_barrier(
        (g_got, small_got, rest_line, tree_extra)
    )
    pairs = [
        total([g_mine[k], g_got[k]]).astype(BF).reshape(-1, span) for k in range(groups // 2)
    ]
    pair_small = total([small, small_got]).astype(BF).reshape(-1)
    per_tree = jnp.concatenate([pair_small[:n_ada], tree_extra, pair_small[n_ada:]])
    n_tree = per_tree.shape[0]
    if groups == 8:
        plane_terms = [pairs[0]] + [net.across(pairs[k], k) for k in range(1, 4)]
    else:
        plane_terms = [net.plane_sum(jnp.stack(pairs)[None])[0]]
    plane_small = net.spread(per_tree)
    plane_terms, plane_small, grads_rows, rest_line = lax.optimization_barrier(
        (plane_terms, plane_small, grads_rows, rest_line)
    )

    line_terms = total(plane_terms).astype(BF).reshape(shards, -1, span)
    every_plane = net.plane_order(plane_small)
    mid_part = n_ada + 2 * cond_dim
    bias_sum = jnp.sum(every_plane[:, mid_part:].astype(F32), axis=0).astype(BF)
    line_small = jnp.concatenate([every_plane[:, :mid_part].reshape(-1), bias_sum])
    n_line = line_small.shape[0]
    more = -(-n_line // (8 * span)) * 8
    line_small = jnp.pad(line_small, (0, more * span - n_line)).reshape(more, span)
    line_sent = jnp.concatenate(
        [line_terms, jnp.broadcast_to(line_small[None], (shards, more, span))], axis=1
    )
    line_got = net.turns(line_sent)
    rest_plane = net.spread(rest_line)
    grads_keep, grads_give = net.back(grads_rows, batches)
    grads_got = net.swap(grads_give)
    line_got, rest_plane, grads_got = lax.optimization_barrier((line_got, rest_plane, grads_got))
    rest_half = jnp.stack(rest_plane)
    rest_other = net.swap(rest_half)

    fine = line_terms.shape[1]
    qkv_sum = total([line_terms[0]] + [got[:fine] for got in line_got]).astype(BF)
    qkv_plane = net.spread(qkv_sum)
    everyone = net.line_order([line_small] + [got[fine:] for got in line_got])
    everyone = everyone.reshape(shards, -1)[:, :n_line].astype(F32)
    by_tree = everyone[:, : (groups // 2) * mid_part].reshape(shards, groups // 2, mid_part)
    t_out, t_fc1, t_fc2 = unpack(net.where, rest_half, rest_other, width)
    out = net.lay_out(out_keep, out_got)
    grads_x = net.lay_out(grads_keep, grads_got)

    every_dada = by_tree[:, :, : 6 * width].reshape(-1, 6 * width)
    every_cond = (
        by_tree[:, :, 6 * width : 6 * width + cond_dim] + by_tree[:, :, 6 * width + cond_dim :]
    ).reshape(-1, cond_dim)
    dada = lax.dynamic_index_in_dim(by_tree[:, :, : 6 * width], net.plane, 1, False)
    g_one, g_two, g_bias2, g_bias1 = jnp.split(
        jnp.sum(everyone[:, (groups // 2) * mid_part :], axis=0), [width, 2 * width, 3 * width]
    )

    def place(vec):
        n = vec.shape[-1] // shards
        return lax.dynamic_slice_in_dim(vec, net.s * n, n, vec.ndim - 1)

    dada_here = place(every_dada)
    t_ada = lax.dot_general(
        every_cond, dada_here, (((0,), (0,)), ((), ())), precision=HIGH
    )
    t_bada = jnp.sum(dada_here, axis=0)
    own = lax.dynamic_index_in_dim(dada.reshape(batches, 2, -1), net.c, 1, False)
    ada_w = qkv_w[:, 3 * width :].reshape(shards, cond_dim, -1).astype(F32)
    cond_total = jnp.einsum(
        "bsn,scn->bc", own.reshape(batches, shards, -1), ada_w, precision=HIGH
    )
    qkv_half = jnp.stack(qkv_plane)
    t_qkv = settle(net.where, qkv_half, net.swap(qkv_half)).reshape(w_qkv.shape)
    return (
        out,
        grads_x,
        cond_total[:, None, :],
        t_qkv,
        t_out,
        t_fc1,
        place(g_bias1),
        t_fc2,
        place(g_bias2),
        t_ada,
        t_bada,
        place(g_one),
        place(g_two),
    )


def solution(mesh):
    in_specs = (
        P(None, "group", "shard", None),
        P(None, "group", None),
        P(None, "group", None),
        P(None, "group", None),
        P(None, "group", "shard", None),
        P("shard", None),
        P("shard", None),
        P("shard", None),
        P("shard"),
        P("shard", None),
        P("shard"),
        P(None, "shard"),
        P("shard"),
        P("shard"),
        P("shard"),
    )
    out_specs = (
        P(None, "group", "shard", None),
        P(None, "group", "shard", None),
        P(None, "group", None),
        P("shard", None),
        P("shard", None),
        P("shard", None),
        P("shard"),
        P("shard", None),
        P("shard"),
        P(None, "shard"),
        P("shard"),
        P("shard"),
        P("shard"),
    )
    groups = mesh.shape["group"]

    def run(*args):
        return on_device(*args, groups)

    return jax.shard_map(
        run, mesh=mesh, in_specs=in_specs, out_specs=out_specs, check_vma=False
    )
```

```python
import functools
import math

import jax
import jax.numpy as jnp
from jax import lax
from jax.experimental import pallas as pl
from jax.experimental.pallas import tpu as pltpu
from jax.sharding import PartitionSpec as P

HEADS = 12
EPS = 1e-05
GELU_C = 0.7978845608028654
GELU_K = 0.044715
HIGH = lax.Precision.HIGHEST
BF = jnp.bfloat16
F32 = jnp.float32
BLOCK = 256
SPAN = 512
LANES = 128
BIG = -float(2**30)
MASKED = -1000000000.0
PAIRS = 6


def layer_norm(values):
    centred = values - jnp.mean(values, axis=-1, keepdims=True)
    inv_std = lax.rsqrt(jnp.mean(centred * centred, axis=-1, keepdims=True) + EPS)
    return centred * inv_std, inv_std


def norm_back(grad_normed, normed, inv_std):
    first_mean = jnp.mean(grad_normed, axis=-1, keepdims=True)
    second = jnp.mean(grad_normed * normed, axis=-1, keepdims=True)
    return (grad_normed - first_mean - normed * second) * inv_std


def gelu_parts(pre_act):
    inner_arg = GELU_C * (pre_act + GELU_K * pre_act * pre_act * pre_act)
    tangent = jnp.tanh(inner_arg)
    gelu_value = 0.5 * pre_act * (1.0 + tangent)
    gelu_slope = 0.5 * (1.0 + tangent) + 0.5 * pre_act * (1.0 - tangent * tangent) * GELU_C * (
        1.0 + 3.0 * GELU_K * pre_act * pre_act
    )
    return gelu_value, gelu_slope


def mm(left, right):
    return jnp.dot(left, right, preferred_element_type=F32)


def mm_t(left, right):
    return lax.dot_general(left, right, (((1,), (1,)), ((), ())), preferred_element_type=F32)


def t_mm(left, right):
    return lax.dot_general(left, right, (((0,), (0,)), ((), ())), preferred_element_type=F32)


def split_heads(pair):
    first = lax.broadcasted_iota(jnp.int32, pair.shape, 1) < LANES // 2
    zero = jnp.zeros_like(pair)
    return jnp.concatenate([jnp.where(first, pair, zero), jnp.where(first, zero, pair)], axis=0)

def side_by_side(stack):
    n = stack.shape[0] // 2
    return jnp.concatenate([stack[:n], stack[n:]], axis=1)

def as_row(column):
    return jnp.transpose(jnp.broadcast_to(column, (column.shape[0], LANES)))[:1]

def interleave(into, near_ref, far_ref):
    for i in range(near_ref.shape[0] // BLOCK):
        rows = slice(i * BLOCK, (i + 1) * BLOCK)
        into[2 * i * BLOCK : (2 * i + 1) * BLOCK, :] = near_ref[rows, :]
        into[(2 * i + 1) * BLOCK : (2 * i + 2) * BLOCK, :] = far_ref[rows, :]

def lane_groups(x):
    return [x[:, i : i + LANES] for i in range(0, x.shape[1], LANES)]

def is_safe(peak, far_keys, scale):
    top = jnp.maximum(peak, jnp.max(jnp.abs(far_keys.astype(F32))))
    return (peak * top * (scale * (LANES // 2)) < 2.0**27).astype(jnp.int32)

def lanes_sum(x): return jnp.sum(x, axis=1, keepdims=True)

def fwd_kernel(near, pp, scale, flags, peak_ref, q_ref, kn_ref, vn_ref, kf_ref, vf_ref, feat_ref, hot_ref, o_ref, lse_ref,
               s_ref, m_ref, l_ref, acc_ref, k_all, v_all, safe_ref):
    qb = pl.program_id(1)
    nk = hot_ref.shape[0] // SPAN
    @pl.when(qb == 0)
    def _():
        interleave(k_all, kn_ref, kf_ref)
        interleave(v_all, vn_ref, vf_ref)
        safe_ref[0] = is_safe(peak_ref[0], kf_ref[...], scale)
    safe = safe_ref[0] == 1
    feat = feat_ref[...]
    feat2 = jnp.concatenate([feat, feat], axis=0)
    qs = [split_heads(q_ref[:, p*LANES:(p+1)*LANES] * scale) for p in range(pp)]
    m_ref[...] = jnp.full(m_ref.shape, -jnp.inf, F32)
    def scan_scores(exact):
        def step(j, _):
            @pl.when((flags[qb * nk + j] == 1) | jnp.logical_not(safe))
            def _():
                rows = pl.ds(pl.multiple_of(j * SPAN, SPAN), SPAN)
                hot = hot_ref[rows, :]
                for p in range(pp):
                    k = k_all[rows, p*LANES:(p+1)*LANES]
                    if exact:
                        ok = mm_t(feat2, hot) > -1.0
                        s = jnp.where(ok, mm_t(qs[p], k), MASKED)
                    else:
                        s = mm_t(jnp.concatenate([qs[p], feat2], axis=1), jnp.concatenate([k, hot], axis=1))
                    s_ref[p, j] = s
                    m_ref[p] = functools.reduce(jnp.maximum, lane_groups(s), m_ref[p])
            return 0
        lax.fori_loop(0, nk, step, 0)
    @pl.when(safe)
    def _(): scan_scores(False)
    @pl.when(jnp.logical_not(safe))
    def _(): scan_scores(True)
    tops = [jnp.max(m_ref[p], axis=1, keepdims=True) for p in range(pp)]
    l_ref[...] = jnp.zeros(l_ref.shape, F32)
    acc_ref[...] = jnp.zeros(acc_ref.shape, F32)
    def step(j, _):
        @pl.when((flags[qb * nk + j] == 1) | jnp.logical_not(safe))
        def _():
            rows = pl.ds(pl.multiple_of(j * SPAN, SPAN), SPAN)
            for p in range(pp):
                e = jnp.exp(s_ref[p, j] - tops[p])
                l_ref[p] += sum(lane_groups(e))
                v = split_heads(v_all[rows, p*LANES:(p+1)*LANES])
                acc_ref[p] += mm(side_by_side(e.astype(BF)), v)
        return 0
    lax.fori_loop(0, nk, step, 0)
    for p in range(pp):
        total = lanes_sum(l_ref[p])
        lse_ref[p, 0] = as_row(tops[p] + jnp.log(total))
        first = lax.broadcasted_iota(jnp.int32, (BLOCK, LANES), 1) < LANES // 2
        o_ref[:, p*LANES:(p+1)*LANES] = (acc_ref[p] / jnp.where(first, total[:BLOCK], total[BLOCK:])).astype(BF)

def attn_fwd(q, kv, far, feat, hot, flags, peak, scale, pp):
    near, width = q.shape
    total = hot.shape[0]
    steps = width // LANES // pp
    nq = near // BLOCK
    col = lambda c: (lambda h, i, f: (0, c * steps + h))
    return pl.pallas_call(
        functools.partial(fwd_kernel, near, pp, scale),
        grid_spec=pltpu.PrefetchScalarGridSpec(
            num_scalar_prefetch=1, grid=(steps, nq),
            in_specs=[
                pl.BlockSpec(memory_space=pltpu.SMEM),
                pl.BlockSpec((BLOCK, pp*LANES), lambda h, i, f: (i, h)),
                pl.BlockSpec((near, pp*LANES), col(0)),
                pl.BlockSpec((near, pp*LANES), col(1)),
                pl.BlockSpec((near, pp*LANES), col(0)),
                pl.BlockSpec((near, pp*LANES), col(1)),
                pl.BlockSpec((BLOCK, LANES), lambda h, i, f: (i, 0)),
                pl.BlockSpec((total, LANES), lambda h, i, f: (0, 0)),
            ],
            out_specs=[
                pl.BlockSpec((BLOCK, pp*LANES), lambda h, i, f: (i, h)),
                pl.BlockSpec((pp, 1, 1, 2*BLOCK), lambda h, i, f: (h, i, 0, 0)),
            ],
            scratch_shapes=[
                pltpu.VMEM((pp, total // SPAN, 2*BLOCK, SPAN), F32),
                pltpu.VMEM((pp, 2*BLOCK, LANES), F32),
                pltpu.VMEM((pp, 2*BLOCK, LANES), F32),
                pltpu.VMEM((pp, BLOCK, LANES), F32),
                pltpu.VMEM((total, pp*LANES), BF),
                pltpu.VMEM((total, pp*LANES), BF),
                pltpu.SMEM((1,), jnp.int32),
            ]),
        out_shape=[jax.ShapeDtypeStruct((near, width), BF), jax.ShapeDtypeStruct((width // LANES, nq, 1, 2*BLOCK), F32)],
        compiler_params=pltpu.CompilerParams(vmem_limit_bytes=56<<20),
        cost_estimate=cost(38),
        name="attn_forward",
    )(flags, peak, q, kv, kv, far, far, feat, hot)

def bwd_kernel(near, pp, scale, flags, peak_ref, q_ref, kn_ref, vn_ref, kf_ref, vf_ref, feat_ref, hot_ref, o_ref, do_ref, lse_ref,
               dq_ref, near_ref, far_ref, k_all, v_all, k_turned, dk_acc, dv_acc, dq_acc, safe_ref):
    half = LANES // 2
    qb = pl.program_id(1)
    nk = hot_ref.shape[0] // SPAN
    @pl.when(qb == 0)
    def _():
        interleave(k_all, kn_ref, kf_ref)
        interleave(v_all, vn_ref, vf_ref)
        safe_ref[0] = is_safe(peak_ref[0], kf_ref[...], scale)
        k_turned[...] = jnp.transpose(k_all[...])
        dk_acc[...] = jnp.zeros(dk_acc.shape, F32)
        dv_acc[...] = jnp.zeros(dv_acc.shape, F32)
    safe = safe_ref[0] == 1
    feat = feat_ref[...]
    feat2 = jnp.concatenate([feat, feat], axis=0)
    dq_acc[...] = jnp.zeros(dq_acc.shape, F32)
    qs, dos, deltas, lses = [], [], [], []
    for p in range(pp):
        cols = slice(p*LANES, (p+1)*LANES)
        qs.append(split_heads(q_ref[:, cols] * scale))
        do2 = split_heads(do_ref[:, cols])
        dos.append(do2)
        o = o_ref[:, cols].astype(F32)
        deltas.append(as_row(lanes_sum(do2.astype(F32) * jnp.concatenate([o, o], axis=0))))
        lses.append(lse_ref[p, 0])
    def sweep(exact):
        def step(j, _):
            @pl.when((flags[qb * nk + j] == 1) | jnp.logical_not(safe))
            def _():
                rows = pl.ds(pl.multiple_of(j * SPAN, SPAN), SPAN)
                hot = hot_ref[rows, :]
                for p in range(pp):
                    cols = slice(p*LANES, (p+1)*LANES)
                    k = k_all[rows, cols]; v = v_all[rows, cols]
                    if exact:
                        ok = mm_t(hot, feat2) > -1.0
                        s = jnp.where(ok, mm_t(k, qs[p]), MASKED)
                    else:
                        s = mm_t(jnp.concatenate([k, hot], axis=1), jnp.concatenate([qs[p], feat2], axis=1))
                    prob = jnp.exp(s - lses[p])
                    dprob = mm_t(v, dos[p])
                    ds = prob * (dprob - deltas[p])
                    if exact:
                        ds = jnp.where(ok, ds, 0.0)
                    ds = ds.astype(BF)
                    dv_acc[rows, cols] += mm(prob.astype(BF), dos[p])
                    dk_acc[rows, cols] += mm(ds, qs[p])
                    for h in range(2):
                        kt = k_turned[p*LANES + h*half : p*LANES + (h+1)*half, rows]
                        dq_acc[p, h*half:(h+1)*half] += mm(kt, ds[:, h*BLOCK:(h+1)*BLOCK])
            return 0
        lax.fori_loop(0, nk, step, 0)
    @pl.when(safe)
    def _(): sweep(False)
    @pl.when(jnp.logical_not(safe))
    def _(): sweep(True)
    for p in range(pp):
        dq_ref[:, p*LANES:(p+1)*LANES] = jnp.transpose(dq_acc[p] * scale).astype(BF)
    @pl.when(qb == pl.num_programs(1) - 1)
    def _():
        for i in range(near // BLOCK):
            rows = slice(i * BLOCK, (i + 1) * BLOCK)
            for side, acc in enumerate((dk_acc, dv_acc)):
                near_ref[side, rows] = acc[2 * i * BLOCK : (2 * i + 1) * BLOCK].astype(BF)
                far_ref[side, rows] = acc[(2 * i + 1) * BLOCK : (2 * i + 2) * BLOCK].astype(BF)

def attn_bwd(q, kv, far, feat, hot, flags, peak, attn, dattn, lse, scale, pp):
    near, width = q.shape
    total = hot.shape[0]
    steps = width // LANES // pp
    nq = near // BLOCK
    col = lambda c: (lambda h, i, f: (0, c * steps + h))
    rowblk = pl.BlockSpec((BLOCK, pp*LANES), lambda h, i, f: (i, h))
    whole = pl.BlockSpec((near, pp*LANES), col(0))
    both = pl.BlockSpec((2, near, pp*LANES), lambda h, i, f: (0, 0, h))
    return pl.pallas_call(
        functools.partial(bwd_kernel, near, pp, scale),
        grid_spec=pltpu.PrefetchScalarGridSpec(
            num_scalar_prefetch=1, grid=(steps, nq),
            in_specs=[
                pl.BlockSpec(memory_space=pltpu.SMEM),
                rowblk,
                pl.BlockSpec((near, pp*LANES), col(0)),
                pl.BlockSpec((near, pp*LANES), col(1)),
                whole,
                pl.BlockSpec((near, pp*LANES), col(1)),
                pl.BlockSpec((BLOCK, LANES), lambda h, i, f: (i, 0)),
                pl.BlockSpec((total, LANES), lambda h, i, f: (0, 0)),
                rowblk, rowblk,
                pl.BlockSpec((pp, 1, 1, 2*BLOCK), lambda h, i, f: (h, i, 0, 0)),
            ],
            out_specs=[rowblk, both, both],
            scratch_shapes=[
                pltpu.VMEM((total, pp*LANES), BF),
                pltpu.VMEM((total, pp*LANES), BF),
                pltpu.VMEM((pp*LANES, total), BF),
                pltpu.VMEM((total, pp*LANES), F32),
                pltpu.VMEM((total, pp*LANES), F32),
                pltpu.VMEM((pp, LANES, BLOCK), F32),
                pltpu.SMEM((1,), jnp.int32),
            ]),
        out_shape=[
            jax.ShapeDtypeStruct((near, width), BF),
            jax.ShapeDtypeStruct((2, near, width), BF),
            jax.ShapeDtypeStruct((2, near, width), BF),
        ],
        compiler_params=pltpu.CompilerParams(vmem_limit_bytes=56<<20),
        cost_estimate=cost(63),
        name="attn_backward",
    )(flags, peak, q, kv, kv, far, far, feat, hot, attn, dattn, lse)


def assemble_kernel(shards, where, own_ref, half_ref, other_ref, out_ref):
    s, c, plane = where[0], where[1], where[2]
    groups, planes = own_ref.shape[0], half_ref.shape[0]
    out_ref[pl.ds(s * groups, groups)] = own_ref[...]
    for side, source in ((c, half_ref), (1 - c, other_ref)):
        for j in range(planes):
            for k in range(1, shards):
                place = lax.rem(s + shards - k, shards)
                out_ref[place * groups + side * planes + (plane ^ j)] = source[j, k - 1]


def assemble(where, own, half, other, shards):
    rows, width = own.shape
    fine = half.shape[2]
    groups = rows // fine
    full = lambda *shape: pl.BlockSpec(shape, lambda i, w: (0,) * len(shape))
    out = pl.pallas_call(
        functools.partial(assemble_kernel, shards),
        grid_spec=pltpu.PrefetchScalarGridSpec(
            num_scalar_prefetch=1,
            grid=(1,),
            in_specs=[full(groups, fine, width), full(*half.shape), full(*half.shape)],
            out_specs=full(groups * shards, fine, width),
        ),
        out_shape=jax.ShapeDtypeStruct((groups * shards, fine, width), own.dtype),
        compiler_params=pltpu.CompilerParams(vmem_limit_bytes=60 << 20),
        name="assemble",
    )(where, own.reshape(groups, fine, width), half, other)
    return out.reshape(shards * rows, width)


def entry_kernel(tok_ref, vec_ref, w_ref, act_ref, q_ref, kv_ref, peak_ref):
    step = pl.program_id(0)
    rows, pieces = SPAN, tok_ref.shape[0] // SPAN

    @pl.when(step == 0)
    def _():
        gain, lift, shift = (vec_ref[i : i + 1, :] for i in range(3))
        for i in range(pieces):
            at = slice(i * rows, (i + 1) * rows)
            normed, _unused = layer_norm(tok_ref[at, :].astype(F32))
            act_ref[at, :] = (normed * gain * lift + shift).astype(BF)
        peak_ref[...] = jnp.zeros_like(peak_ref)

    top = jnp.zeros((1, w_ref.shape[1]), F32)
    for i in range(pieces):
        at = slice(i * rows, (i + 1) * rows)
        value = mm(act_ref[at, :], w_ref[...])
        low = value.astype(BF)
        top = jnp.maximum(top, jnp.max(jnp.abs(low.astype(F32)), axis=0, keepdims=True))

        @pl.when(step < 2)
        def _():
            kv_ref[at, :] = low

        @pl.when(step == 2)
        def _():
            q_ref[at, :] = low

    peak_ref[0:1, :] = jnp.maximum(peak_ref[0:1, :], top)


def entry(tok, vec, qkv_w):
    total, width = tok.shape
    fixed = lambda *shape: pl.BlockSpec(shape, lambda j: (0,) * len(shape))
    return pl.pallas_call(
        entry_kernel,
        grid=(3,),
        in_specs=[
            fixed(total, width), fixed(8, width),
            pl.BlockSpec((width, width), lambda j: (0, lax.rem(j + 1, 3))),
        ],
        out_specs=[
            fixed(total, width), fixed(total, width),
            pl.BlockSpec((total, width), lambda j: (0, jnp.minimum(j, 1))),
            fixed(8, width),
        ],
        out_shape=[
            jax.ShapeDtypeStruct((total, width), BF),
            jax.ShapeDtypeStruct((total, width), BF),
            jax.ShapeDtypeStruct((total, 2 * width), BF),
            jax.ShapeDtypeStruct((8, width), F32),
        ],
        compiler_params=pltpu.CompilerParams(vmem_limit_bytes=48 << 20),
        cost_estimate=cost(9),
        name="entry",
    )(tok, vec, qkv_w)


def leave_kernel(spots, where, dq_ref, near_ref, far_ref, act_ref, w_ref, tok_in, dmid_in, vec_ref,
                 grad_ref, mine_ref, yours_ref, sums_ref, d_all, da, tok_ref, dmid_ref, sems):
    step = pl.program_id(0)
    total = dq_ref.shape[0]
    sides, planes, places, fine = spots

    late = [
        pltpu.make_async_copy(tok_in, tok_ref, sems.at[0]),
        pltpu.make_async_copy(dmid_in, dmid_ref, sems.at[1]),
    ]

    @pl.when(step == 0)
    def _():
        for copy in late:
            copy.start()
        d_all[...] = dq_ref[...]
        da[...] = jnp.zeros_like(da)

    @pl.when(step > 0)
    def _():
        d_all[...] = (near_ref[0].astype(F32) + far_ref[0].astype(F32)).astype(BF)

    grad = t_mm(act_ref[...], d_all[...])

    def put(ref, side):
        for place in range(places):
            turned = lax.rem(place + places - where[0], places)
            for plane in range(planes):
                start = ((place * sides + side) * planes + plane) * fine
                ref[plane ^ where[2], turned] = grad[start : start + fine].astype(BF)

    for side in range(sides):
        pl.when(where[1] == side)(functools.partial(put, mine_ref, side))
        pl.when(where[1] != side)(functools.partial(put, yours_ref, side))

    def add(r, _):
        rows = pl.ds(pl.multiple_of(r * SPAN, SPAN), SPAN)
        da[rows, :] += mm_t(d_all[rows, :], w_ref[...])
        return 0

    lax.fori_loop(0, total // SPAN, add, 0)

    @pl.when(step == 2)
    def _():
        gain, lift, shift = (vec_ref[i : i + 1, :] for i in range(3))
        sums_ref[...] = jnp.zeros_like(sums_ref)
        for copy in late:
            copy.wait()

        def finish(r, _):
            rows = pl.ds(pl.multiple_of(r * BLOCK, BLOCK), BLOCK)
            normed, inv = layer_norm(tok_ref[rows, :].astype(F32))
            part = da[rows, :]
            grad_h = part * lift
            back = norm_back(grad_h * gain, normed, inv)
            grad_ref[rows, :] = (dmid_ref[rows, :] + back).astype(BF)
            for i, term in enumerate((part, part * (normed * gain), grad_h * normed)):
                sums_ref[i : i + 1, :] += jnp.sum(term, axis=0, keepdims=True)
            return 0

        lax.fori_loop(0, total // BLOCK, finish, 0)


def leave(where, q_grads, near, far, act, qkv_w, tok, dmid, vec, spots):
    total, width = q_grads.shape
    keep = pl.Buffered(1)
    whole = pl.BlockSpec((total, width), lambda j, w: (0, 0), pipeline_mode=keep)
    both = pl.BlockSpec((1, total, width), lambda j, w: (jnp.maximum(j - 1, 0), 0, 0))
    small = pl.BlockSpec((8, width), lambda j, w: (0, 0))
    part = pl.BlockSpec(tuple(spots[1:]) + (width,), lambda j, w: (0, 0, 0, j))
    return pl.pallas_call(
        functools.partial(leave_kernel, spots),
        grid_spec=pltpu.PrefetchScalarGridSpec(
            num_scalar_prefetch=1,
            grid=(3,),
            in_specs=[
                whole, both, both, whole,
                pl.BlockSpec((width, width), lambda j, w: (0, j)),
                pl.BlockSpec(memory_space=pl.ANY),
                pl.BlockSpec(memory_space=pl.ANY),
                small,
            ],
            out_specs=[
                whole,
                part, part,
                small,
            ],
            scratch_shapes=[
                pltpu.VMEM((total, width), BF),
                pltpu.VMEM((total, width), F32),
                pltpu.VMEM((total, width), BF),
                pltpu.VMEM((total, width), F32),
                pltpu.SemaphoreType.DMA((2,)),
            ],
        ),
        out_shape=[
            jax.ShapeDtypeStruct((total, width), BF),
            jax.ShapeDtypeStruct(tuple(spots[1:]) + (3 * width,), BF),
            jax.ShapeDtypeStruct(tuple(spots[1:]) + (3 * width,), BF),
            jax.ShapeDtypeStruct((8, width), F32),
        ],
        compiler_params=pltpu.CompilerParams(vmem_limit_bytes=56 << 20),
        cost_estimate=cost(14),
        name="leave",
    )(where, q_grads, near, far, act, qkv_w, tok, dmid, vec)


def settle_kernel(where, half_ref, other_ref, out_ref):
    c, plane = where[1], where[2]
    for side, source in ((c, half_ref), (1 - c, other_ref)):
        for j in range(half_ref.shape[0]):
            out_ref[side * half_ref.shape[0] + (plane ^ j)] = source[j].astype(F32)


def settle(where, half, other):
    planes, fine, width = half.shape
    full = lambda *shape: pl.BlockSpec(shape, lambda i, w: (0,) * len(shape))
    return pl.pallas_call(
        settle_kernel,
        grid_spec=pltpu.PrefetchScalarGridSpec(
            num_scalar_prefetch=1,
            grid=(1,),
            in_specs=[full(planes, fine, width)] * 2,
            out_specs=full(2 * planes, fine, width),
        ),
        out_shape=jax.ShapeDtypeStruct((2 * planes, fine, width), F32),
        compiler_params=pltpu.CompilerParams(vmem_limit_bytes=40 << 20),
        name="settle",
    )(where, half, other)


def unpack_kernel(count, where, half_ref, other_ref, out_ref, fc1_ref, fc2_ref):
    step = pl.program_id(0)
    c, plane = where[1], where[2]

    def fill(ref):
        for side, source in ((c, half_ref), (1 - c, other_ref)):
            for j in range(source.shape[0]):
                ref[2 * (plane ^ j) + side] = source[j].astype(F32).reshape(ref.shape[1:])

    @pl.when(step == 0)
    def _():
        fill(out_ref)

    @pl.when((step > 0) & (step <= count))
    def _():
        fill(fc1_ref)

    @pl.when(step > count)
    def _():
        fill(fc2_ref)


def unpack(where, half, other, width):
    planes, fine, total = half.shape
    groups, count = 2 * planes, total // width // 2
    block = pl.BlockSpec((planes, fine, width), lambda i, w: (0, 0, i))
    low = lambda i: jnp.clip(i, 0, count - 1)
    out, fc1, fc2 = pl.pallas_call(
        functools.partial(unpack_kernel, count),
        grid_spec=pltpu.PrefetchScalarGridSpec(
            num_scalar_prefetch=1,
            grid=(1 + 2 * count,),
            in_specs=[block, block],
            out_specs=[
                pl.BlockSpec((groups, fine, width), lambda i, w: (0, 0, 0)),
                pl.BlockSpec((groups, fine, width), lambda i, w: (0, 0, low(i - 1))),
                pl.BlockSpec((groups, 1, fine, width), lambda i, w: (0, low(i - 1 - count), 0, 0)),
            ],
        ),
        out_shape=[
            jax.ShapeDtypeStruct((groups, fine, width), F32),
            jax.ShapeDtypeStruct((groups, fine, count * width), F32),
            jax.ShapeDtypeStruct((groups, count, fine, width), F32),
        ],
        compiler_params=pltpu.CompilerParams(vmem_limit_bytes=40 << 20),
        cost_estimate=cost(4),
        name="unpack",
    )(where, half, other)
    return out.reshape(-1, width), fc1.reshape(-1, count * width), fc2.reshape(-1, width)


def cost(microseconds):
    return pl.CostEstimate(
        flops=int(microseconds * 1.15e9), bytes_accessed=1 << 20, transcendentals=0
    )


def middle_kernel(chunks, where, attn_ref, tok_ref, cot_ref, vec_ref, b1_ref, wo_ref, w1_ref, *rest):
    w2_refs, rest = rest[:chunks], rest[chunks:]
    (out_ref, dattn_ref, dmid_ref, grads_ref, sums_ref, gb1_ref) = rest[:6]
    (mid, branch, act, dy, two, da, hid, dpre, w2, wide, tall, sems) = rest[6:]
    width = attn_ref.shape[1]

    def send_wide(column):
        cols = pl.ds(pl.multiple_of(column * width, LANES), width)
        return pltpu.make_async_copy(wide, grads_ref.at[:, :, :, cols], sems.at[0])

    def turned(place):
        return lax.rem(place + chunks - where[0], chunks)

    def send_tall(place):
        cols = pl.ds((1 + chunks) * width, chunks * width)
        return pltpu.make_async_copy(tall, grads_ref.at[:, turned(place), :, cols], sems.at[1])

    step = pl.program_id(0)
    total = attn_ref.shape[0]
    blocks = total // BLOCK
    gate_one, gain, lift, shift, gate_two, fc2_b = (vec_ref[i : i + 1, :] for i in range(6))

    def rows_of(r):
        return pl.ds(pl.multiple_of(r * BLOCK, BLOCK), BLOCK)

    @pl.when(step == 0)
    def _():
        sums_ref[...] = jnp.zeros_like(sums_ref)

        def start(r, _):
            rows = rows_of(r)
            one = mm(attn_ref[rows, :], wo_ref[...])
            middle = tok_ref[rows, :].astype(F32) + gate_one * one
            normed, _unused = layer_norm(middle)
            branch[rows, :] = one
            mid[rows, :] = middle
            act[rows, :] = (normed * gain * lift + shift).astype(BF)
            dy[rows, :] = (cot_ref[rows, :].astype(F32) * gate_two).astype(BF)
            two[rows, :] = jnp.zeros((BLOCK, two.shape[1]), F32)
            da[rows, :] = jnp.zeros((BLOCK, da.shape[1]), F32)
            return 0

        lax.fori_loop(0, blocks, start, 0)

    @pl.when(step < chunks)
    def _():
        height = w2_refs[0].shape[0]
        for b in range(chunks):
            w2[b * height : (b + 1) * height, :] = w2_refs[b][...]
        gb1_ref[...] = jnp.zeros_like(gb1_ref)

        def chunk(r, _):
            rows = pl.ds(pl.multiple_of(r * SPAN, SPAN), SPAN)
            value, slope = gelu_parts(mm(act[rows, :], w1_ref[...]) + b1_ref[...])
            hidden = value.astype(BF)
            hid[rows, :] = hidden
            two[rows, :] += mm(hidden, w2[...])
            grad = (mm_t(dy[rows, :], w2[...]) * slope).astype(BF)
            dpre[rows, :] = grad
            gb1_ref[...] += jnp.sum(grad.astype(F32), axis=0, keepdims=True)
            da[rows, :] += mm_t(grad, w1_ref[...])
            return 0

        lax.fori_loop(0, total // SPAN, chunk, 0)
        grad_two = t_mm(hid[...], dy[...])
        grad_one = t_mm(act[...], dpre[...])

        @pl.when(step > 0)
        def _():
            send_wide(step).wait()
            send_tall(step - 1).wait()

        groups, fine = tall.shape[:2]
        for g in range(groups):
            for b in range(chunks):
                start = (g * chunks + b) * fine
                tall[g, :, b * width : (b + 1) * width] = grad_two[start : start + fine].astype(BF)
        put_blocks(wide, grad_one, turned)
        send_wide(step + 1).start()
        send_tall(step).start()

    @pl.when(step == chunks)
    def _():
        def finish(r, _):
            rows = rows_of(r)
            cot = cot_ref[rows, :].astype(F32)
            middle = mid[rows, :]
            second = two[rows, :] + fc2_b
            out_ref[rows, :] = (middle + gate_two * second).astype(BF)
            normed, inv = layer_norm(middle)
            lifted = normed * gain
            grad = da[rows, :]
            grad_h = grad * lift
            dmid = cot + norm_back(grad_h * gain, normed, inv)
            dmid_ref[rows, :] = dmid
            dy_one = (dmid * gate_one).astype(BF)
            dpre[rows, :] = dy_one
            dattn_ref[rows, :] = mm_t(dy_one, wo_ref[...]).astype(BF)
            parts = (
                dmid * branch[rows, :], grad, grad * lifted, cot * second,
                grad_h * normed, dy[rows, :].astype(F32),
            )
            for i, part in enumerate(parts):
                sums_ref[i : i + 1, :] += jnp.sum(part, axis=0, keepdims=True)
            return 0

        lax.fori_loop(0, blocks, finish, 0)
        grad_out = t_mm(attn_ref[...], dpre[...])
        send_wide(step).wait()
        send_tall(step - 1).wait()
        put_blocks(wide, grad_out, turned)
        send_wide(0).start()
        send_wide(0).wait()


def put_blocks(ref, grad, turned):
    groups, places, rows = ref.shape[:3]
    for s in range(places):
        for g in range(groups):
            start = (s * groups + g) * rows
            ref[g, turned(s)] = grad[start : start + rows].astype(BF)


def middle(where, attn, tok, cot, vec, fc1_b, pack, groups):
    total, width = attn.shape
    shards = pack.shape[1] // width - 5
    fine = width // shards // groups
    keep = pl.Buffered(1)
    whole = pl.BlockSpec((total, width), lambda i, w: (0, 0), pipeline_mode=keep)
    last = shards - 1
    low = lambda i: jnp.minimum(i, last)
    w2_spec = lambda b: pl.BlockSpec((width // shards, width), lambda i, w: (low(i), 5 + b))
    return pl.pallas_call(
        functools.partial(middle_kernel, shards),
        grid_spec=pltpu.PrefetchScalarGridSpec(
            num_scalar_prefetch=1,
            grid=(shards + 1,),
            in_specs=[
            whole, whole, whole,
            pl.BlockSpec((8, width), lambda i, w: (0, 0)),
            pl.BlockSpec((1, width), lambda i, w: (0, low(i))),
            pl.BlockSpec((width, width), lambda i, w: (0, 0), pipeline_mode=keep),
            pl.BlockSpec((width, width), lambda i, w: (0, 1 + low(i))),
        ] + [w2_spec(b) for b in range(shards)],
        out_specs=[
            whole, whole, whole,
            pl.BlockSpec(memory_space=pl.ANY),
            pl.BlockSpec((8, width), lambda i, w: (0, 0)),
            pl.BlockSpec((1, width), lambda i, w: (0, low(i))),
        ],
        scratch_shapes=[
            pltpu.VMEM((total, width), F32),
            pltpu.VMEM((total, width), F32),
            pltpu.VMEM((total, width), BF),
            pltpu.VMEM((total, width), BF),
            pltpu.VMEM((total, width), F32),
            pltpu.VMEM((total, width), F32),
            pltpu.VMEM((total, width), BF),
            pltpu.VMEM((total, width), BF),
            pltpu.VMEM((width, width), BF),
            pltpu.VMEM((groups, shards, fine, width), BF),
            pltpu.VMEM((groups, fine, shards * width), BF),
            pltpu.SemaphoreType.DMA((2,)),
        ],
        ),
        out_shape=[
            jax.ShapeDtypeStruct((total, width), BF),
            jax.ShapeDtypeStruct((total, width), BF),
            jax.ShapeDtypeStruct((total, width), F32),
            jax.ShapeDtypeStruct((groups, shards, fine, 9 * width), BF),
            jax.ShapeDtypeStruct((8, width), F32),
            jax.ShapeDtypeStruct((1, 4 * width), F32),
        ],
        compiler_params=pltpu.CompilerParams(vmem_limit_bytes=60 << 20),
        cost_estimate=cost(55),
        name="middle",
    )(where, attn, tok, cot, vec, fc1_b, pack, pack, *([pack] * shards))


class Links:
    def __init__(self, groups, shards):
        self.groups, self.shards, self.planes = groups, shards, groups // 2
        self.g = lax.axis_index("group")
        self.s = lax.axis_index("shard")
        self.c = self.g % 2
        self.plane = self.g // 2
        tilt = self.plane if self.planes == 4 else 0 * self.plane
        self.where = jnp.stack([self.s, self.c, tilt]).astype(jnp.int32)

    def swap(self, value):
        return lax.ppermute(value, "group", [(i, i ^ 1) for i in range(self.groups)])

    def turn(self, value, step):
        n = self.shards
        return lax.ppermute(value, "shard", [(i, (i + step) % n) for i in range(n)])

    def across(self, value, step):
        return lax.ppermute(value, "group", [(i, i ^ (2 * step)) for i in range(self.groups)])

    def give(self, value):
        batches, rows, width = value.shape
        halves = value.reshape(batches, 2, rows // 2, width)
        keep = lax.dynamic_index_in_dim(halves, self.c, 1, False)
        return keep, lax.dynamic_index_in_dim(halves, 1 - self.c, 1, False)

    def to_trees(self, keep, got):
        return self.exchange(self.by_core(keep, got).reshape(-1, *keep.shape[1:]))

    def exchange(self, by_tree):
        return lax.all_to_all(by_tree, "shard", 0, 0).reshape(-1, by_tree.shape[-1])

    def by_core(self, mine, other):
        return jnp.where(
            self.c == 0, jnp.stack([mine, other], axis=1), jnp.stack([other, mine], axis=1)
        )

    def from_trees(self, value):
        return lax.all_to_all(
            value.reshape(self.shards, -1, value.shape[1]), "shard", 0, 0
        )

    def back(self, value, batches):
        by_core = value.reshape(batches, 2, *value.shape[1:])
        keep = lax.dynamic_index_in_dim(by_core, self.c, 1, False)
        return keep, lax.dynamic_index_in_dim(by_core, 1 - self.c, 1, False)

    def lay_out(self, keep, got):
        return self.by_core(keep, got).reshape(keep.shape[0], 1, -1, keep.shape[-1])

    def plane_order(self, parts):
        stacked = jnp.stack(parts)
        if self.planes != 4:
            return stacked
        return jnp.stack(
            [lax.dynamic_index_in_dim(stacked, self.plane ^ j, 0, False) for j in range(4)]
        )

    def line_order(self, parts):
        stacked = jnp.stack(parts)
        return jnp.stack(
            [
                lax.dynamic_index_in_dim(stacked, (self.s - j) % self.shards, 0, False)
                for j in range(self.shards)
            ]
        )

    def gather_all(self, part):
        return lax.all_gather(part, ("shard", "group"), axis=0, tiled=True)

    def my_rows(self, weight):
        rows = weight.shape[-2] // self.groups
        return lax.dynamic_slice_in_dim(weight, self.g * rows, rows, weight.ndim - 2)

    def group_sum(self, blocks):
        out = lax.psum_scatter(blocks, "group", scatter_dimension=0, tiled=True)
        return out

    def plane_sum(self, value):
        if self.planes != 4:
            groups = [[2 * p + c for p in range(self.planes)] for c in range(2)]
            return lax.psum_scatter(
                value, "group", scatter_dimension=1, axis_index_groups=groups
            ).astype(F32)
        total = lax.dynamic_index_in_dim(value, self.plane, 1, False).astype(F32)
        for k in range(1, 4):
            piece = lax.dynamic_index_in_dim(value, self.plane ^ k, 1, False)
            total = total + self.across(piece, k).astype(F32)
        return total

    def plane_gather(self, value):
        if self.planes != 4:
            groups = [[2 * p + c for p in range(self.planes)] for c in range(2)]
            return lax.all_gather(value, "group", axis_index_groups=groups)
        parts = jnp.stack([value] + [self.across(value, k) for k in range(1, 4)])
        return jnp.stack(
            [lax.dynamic_index_in_dim(parts, self.plane ^ j, 0, False) for j in range(4)]
        )

    def turns(self, values):
        return [self.turn(values[k], k) for k in range(1, self.shards)]

    def spread(self, value):
        if self.planes != 4:
            every = self.plane_gather(value)
            return [every[j] for j in range(self.planes)]
        return [value] + [self.across(value, k) for k in range(1, 4)]


def total(terms):
    result = terms[0].astype(F32)
    for term in terms[1:]:
        result = result + term.astype(F32)
    return result


def on_device(
    tokens,
    cond,
    seg_ids,
    parents,
    cotangent,
    w_qkv,
    w_out,
    w_fc1,
    b_fc1,
    w_fc2,
    b_fc2,
    w_ada,
    b_ada,
    gain1,
    gain2,
    groups,
):
    batches, _, row_count, width = tokens.shape
    shards = lax.axis_size("shard")
    assert shards == 2 * batches and groups % 2 == 0
    head_dim = width // HEADS
    scale = 1.0 / math.sqrt(head_dim)
    net = Links(groups, shards)
    rows = row_count // 2
    mine = shards * rows
    tree_len = seg_ids.shape[2]
    labels = parents.shape[2]
    cond_dim = cond.shape[2]

    fc2_blocks = net.my_rows(w_fc2.reshape(shards, -1, width))
    share = jnp.concatenate(
        [net.my_rows(w_out), net.my_rows(w_fc1)] + [fc2_blocks[b] for b in range(shards)],
        axis=1,
    )

    packed = jnp.concatenate(
        [seg_ids[:, 0].astype(F32), parents[:, 0].astype(F32), cond[:, 0]], axis=1
    )
    part_rows = w_qkv.shape[0] // groups
    early_w = jnp.concatenate([w_qkv, w_ada.reshape(-1, width)], axis=1)
    own_part = lax.dynamic_index_in_dim(
        early_w.reshape(groups, part_rows, -1), net.c * (groups // 2) + net.plane, 0, False
    )
    tok_keep, tok_give = net.give(tokens[:, 0])
    other = net.swap(packed)
    line_w = net.turns([own_part] * shards)
    tok_got = net.swap(tok_give)
    other, line_w, tok_got, share = lax.optimization_barrier((other, line_w, tok_got, share))
    pack = net.gather_all(share)
    tok = net.to_trees(tok_keep, tok_got)
    plane_w = net.spread(jnp.stack(line_w))
    cot_keep, cot_give = net.give(cotangent[:, 0])
    trees = jnp.where(
        net.c == 0, jnp.stack([packed, other], axis=1), jnp.stack([other, packed], axis=1)
    ).reshape(shards, packed.shape[1])
    conds = trees[:, tree_len + labels :]
    my_tree = lax.dynamic_index_in_dim(trees, net.s, 0, False)
    tree_seg = my_tree[:tree_len]
    parent_row = my_tree[tree_len : tree_len + labels]
    ada_rows = jnp.dot(conds, w_ada.astype(F32), precision=HIGH) + b_ada.astype(F32)
    small = jnp.concatenate([b_fc1, b_fc2, gain1, gain2]).astype(F32)
    pieces = jnp.concatenate(
        [ada_rows, jnp.broadcast_to(small[None], (shards, small.shape[0]))], axis=1
    )
    plane_w, tok, pieces, cot_give = lax.optimization_barrier(
        (plane_w, tok, pieces, cot_give)
    )
    cot_got = net.swap(cot_give)
    got = [lax.dynamic_index_in_dim(pieces, net.s, 0, False)]
    for k in range(1, shards):
        piece = lax.dynamic_index_in_dim(pieces, (net.s + k) % shards, 0, False)
        got.append(net.turn(piece, k))
    half_w = jnp.stack(plane_w)
    qkv_w = assemble(net.where, early_w, half_w, net.swap(half_w), shards)
    line = net.line_order(got)
    cut = ada_rows.shape[1]
    ada = line[:, :cut].reshape(-1)
    ends = [cut]
    for vec in (b_fc1, b_fc2, gain1, gain2):
        ends.append(ends[-1] + vec.shape[0])
    fc1_b, fc2_b, gain_a, gain_b = (
        line[:, ends[i] : ends[i + 1]].reshape(-1) for i in range(4)
    )
    shift_one, scale_one, gate_one, shift_two, scale_two, gate_two = jnp.split(ada, 6)

    half_seg = tree_seg.reshape(shards, 2, rows)

    def row_segs(half):
        return lax.dynamic_index_in_dim(half_seg, half, 1, False).reshape(-1)

    query_seg = row_segs(net.c)
    key_seg = jnp.stack(
        [query_seg.reshape(shards, rows), row_segs(1 - net.c).reshape(shards, rows)], axis=1
    ).reshape(-1)
    lanes = jnp.arange(LANES, dtype=F32)
    table = jnp.zeros((LANES,), F32).at[:labels].set(parent_row)
    up_two = jnp.sum(jnp.where(table[:, None] == lanes[None, :], table[None, :], 0.0), axis=1)
    reach = (
        (lanes[:, None] == lanes[None, :])
        | (table[:, None] == lanes[None, :])
        | (up_two[:, None] == lanes[None, :])
    )
    hot = (key_seg[:, None] == lanes[None, :]).astype(BF)
    hot_mine = hot.reshape(shards, 2, rows, LANES)[:, 0].reshape(mine, LANES)
    feat = mm(hot_mine, jnp.where(reach, 0.0, BIG).astype(BF)).astype(BF)
    held = jnp.max(hot.reshape(-1, SPAN, LANES), axis=1)
    asking = jnp.max(hot_mine.reshape(-1, BLOCK, LANES), axis=1)
    wanted = mm(asking, reach.astype(BF)).astype(BF)
    flags = (mm_t(wanted, held) > 0.5).reshape(-1).astype(jnp.int32)

    vec_one = jnp.stack([gain_a, 1.0 + scale_one, shift_one] + [gain_a] * 5)
    cot_both = net.by_core(cot_keep, cot_got).reshape(shards, rows, width)
    act_one, query, kv, peak = entry(tok, vec_one, qkv_w)
    kv, cot_both = lax.optimization_barrier((kv, cot_both))
    far = net.swap(kv)
    grad_out = net.exchange(cot_both)
    bound = jnp.max(peak[:1]).reshape(1)
    attn, log_totals = attn_fwd(query, kv, far, feat, hot, flags, bound, scale, PAIRS)
    vec = jnp.stack(
        [gate_one, gain_b, 1.0 + scale_two, shift_two, gate_two, fc2_b, fc2_b, fc2_b]
    )
    result, grad_attn, grad_mid, blocks, sums, g_b1 = middle(
        net.where, attn, tok, grad_out, vec, fc1_b[None], pack, groups
    )
    out_rows = net.from_trees(result)

    parts = net.group_sum(blocks.reshape(-1, 9 * width)).reshape(shards, -1, 9 * width)
    q_grads, near_grads, far_grads = attn_bwd(
        query, kv, far, feat, hot, flags, bound, attn, grad_attn, log_totals, scale, PAIRS
    )
    near_grads, parts, out_rows = lax.optimization_barrier((near_grads, parts, out_rows))
    out_keep, out_give = net.back(out_rows, batches)
    out_got = net.swap(out_give)
    turned = net.turns(parts)
    grad_in, g_mine, g_yours, late_sums = leave(
        net.where, q_grads, near_grads, net.swap(far_grads), act_one, qkv_w, tok, grad_mid,
        vec_one, (2, groups // 2, shards, part_rows),
    )

    turned, out_got, grad_in, g_mine, g_yours, late_sums = lax.optimization_barrier(
        (turned, out_got, grad_in, g_mine, g_yours, late_sums)
    )
    span = g_mine.shape[-1]
    g_got = net.swap(g_yours)
    grads_rows = net.from_trees(grad_in)
    small = jnp.concatenate(
        [late_sums[:2], sums[:4], late_sums[2:3], sums[4:6], g_b1.reshape(-1, width)]
    ).astype(BF)
    n_ada = 6 * width
    small_got = net.swap(small)
    rest_line = total([parts[0]] + turned).astype(BF)
    my_cond = lax.dynamic_index_in_dim(conds, net.s, 0, False)
    cond_top = my_cond.astype(BF)
    tree_extra = jnp.concatenate([cond_top, (my_cond - cond_top.astype(F32)).astype(BF)])
    g_got, small_got, rest_line, tree_extra = lax.optimization_barrier(
        (g_got, small_got, rest_line, tree_extra)
    )
    pairs = [
        total([g_mine[k], g_got[k]]).astype(BF).reshape(-1, span) for k in range(groups // 2)
    ]
    pair_small = total([small, small_got]).astype(BF).reshape(-1)
    per_tree = jnp.concatenate([pair_small[:n_ada], tree_extra, pair_small[n_ada:]])
    n_tree = per_tree.shape[0]
    if groups == 8:
        plane_terms = [pairs[0]] + [net.across(pairs[k], k) for k in range(1, 4)]
    else:
        plane_terms = [net.plane_sum(jnp.stack(pairs)[None])[0]]
    plane_small = net.spread(per_tree)
    out = net.lay_out(out_keep, out_got)
    plane_terms, plane_small, grads_rows, rest_line, out = lax.optimization_barrier(
        (plane_terms, plane_small, grads_rows, rest_line, out)
    )

    line_terms = total(plane_terms).astype(BF).reshape(shards, -1, span)
    every_plane = net.plane_order(plane_small)
    mid_part = n_ada + 2 * cond_dim
    bias_sum = jnp.sum(every_plane[:, mid_part:].astype(F32), axis=0).astype(BF)
    line_small = jnp.concatenate([every_plane[:, :mid_part].reshape(-1), bias_sum])
    n_line = line_small.shape[0]
    more = -(-n_line // (8 * span)) * 8
    line_small = jnp.pad(line_small, (0, more * span - n_line)).reshape(more, span)
    line_sent = jnp.concatenate(
        [line_terms, jnp.broadcast_to(line_small[None], (shards, more, span))], axis=1
    )
    line_got = net.turns(line_sent)
    rest_plane = net.spread(rest_line)
    grads_keep, grads_give = net.back(grads_rows, batches)
    grads_got = net.swap(grads_give)
    line_got, rest_plane, grads_got = lax.optimization_barrier((line_got, rest_plane, grads_got))
    rest_half = jnp.stack(rest_plane)
    rest_other = net.swap(rest_half)

    fine = line_terms.shape[1]
    qkv_sum = total([line_terms[0]] + [got[:fine] for got in line_got]).astype(BF)
    qkv_plane = net.spread(qkv_sum)
    everyone = net.line_order([line_small] + [got[fine:] for got in line_got])
    everyone = everyone.reshape(shards, -1)[:, :n_line].astype(F32)
    by_tree = everyone[:, : (groups // 2) * mid_part].reshape(shards, groups // 2, mid_part)
    t_out, t_fc1, t_fc2 = unpack(net.where, rest_half, rest_other, width)
    grads_x = net.lay_out(grads_keep, grads_got)

    every_dada = by_tree[:, :, : 6 * width].reshape(-1, 6 * width)
    every_cond = (
        by_tree[:, :, 6 * width : 6 * width + cond_dim] + by_tree[:, :, 6 * width + cond_dim :]
    ).reshape(-1, cond_dim)
    dada = lax.dynamic_index_in_dim(by_tree[:, :, : 6 * width], net.plane, 1, False)
    g_one, g_two, g_bias2, g_bias1 = jnp.split(
        jnp.sum(everyone[:, (groups // 2) * mid_part :], axis=0), [width, 2 * width, 3 * width]
    )

    def place(vec):
        n = vec.shape[-1] // shards
        return lax.dynamic_slice_in_dim(vec, net.s * n, n, vec.ndim - 1)

    dada_here = place(every_dada)
    t_ada = lax.dot_general(
        every_cond, dada_here, (((0,), (0,)), ((), ())), precision=HIGH
    )
    t_bada = jnp.sum(dada_here, axis=0)
    own = lax.dynamic_index_in_dim(dada.reshape(batches, 2, -1), net.c, 1, False)
    ada_w = qkv_w[:, 3 * width :].reshape(shards, cond_dim, -1).astype(F32)
    cond_total = jnp.einsum(
        "bsn,scn->bc", own.reshape(batches, shards, -1), ada_w, precision=HIGH
    )
    qkv_half = jnp.stack(qkv_plane)
    t_qkv = settle(net.where, qkv_half, net.swap(qkv_half)).reshape(w_qkv.shape)
    return (
        out,
        grads_x,
        cond_total[:, None, :],
        t_qkv,
        t_out,
        t_fc1,
        place(g_bias1),
        t_fc2,
        place(g_bias2),
        t_ada,
        t_bada,
        place(g_one),
        place(g_two),
    )


def solution(mesh):
    in_specs = (
        P(None, "group", "shard", None),
        P(None, "group", None),
        P(None, "group", None),
        P(None, "group", None),
        P(None, "group", "shard", None),
        P("shard", None),
        P("shard", None),
        P("shard", None),
        P("shard"),
        P("shard", None),
        P("shard"),
        P(None, "shard"),
        P("shard"),
        P("shard"),
        P("shard"),
    )
    out_specs = (
        P(None, "group", "shard", None),
        P(None, "group", "shard", None),
        P(None, "group", None),
        P("shard", None),
        P("shard", None),
        P("shard", None),
        P("shard"),
        P("shard", None),
        P("shard"),
        P(None, "shard"),
        P("shard"),
        P("shard"),
        P("shard"),
    )
    groups = mesh.shape["group"]

    def run(*args):
        return on_device(*args, groups)

    return jax.shard_map(
        run, mesh=mesh, in_specs=in_specs, out_specs=out_specs, check_vma=False
    )
```

```python
import functools
import math

import jax
import jax.numpy as jnp
from jax import lax
from jax.experimental import pallas as pl
from jax.experimental.pallas import tpu as pltpu
from jax.sharding import PartitionSpec as P

HEADS = 12
EPS = 1e-05
GELU_C = 0.7978845608028654
GELU_K = 0.044715
HIGH = lax.Precision.HIGHEST
BF = jnp.bfloat16
F32 = jnp.float32
BLOCK = 256
SPAN = 512
LANES = 128
BIG = -float(2**30)
MASKED = -1000000000.0
PAIRS = 6


def layer_norm(values):
    centred = values - jnp.mean(values, axis=-1, keepdims=True)
    inv_std = lax.rsqrt(jnp.mean(centred * centred, axis=-1, keepdims=True) + EPS)
    return centred * inv_std, inv_std


def norm_back(grad_normed, normed, inv_std):
    first_mean = jnp.mean(grad_normed, axis=-1, keepdims=True)
    second = jnp.mean(grad_normed * normed, axis=-1, keepdims=True)
    return (grad_normed - first_mean - normed * second) * inv_std


def gelu_parts(pre_act):
    inner_arg = GELU_C * (pre_act + GELU_K * pre_act * pre_act * pre_act)
    tangent = jnp.tanh(inner_arg)
    gelu_value = 0.5 * pre_act * (1.0 + tangent)
    gelu_slope = 0.5 * (1.0 + tangent) + 0.5 * pre_act * (1.0 - tangent * tangent) * GELU_C * (
        1.0 + 3.0 * GELU_K * pre_act * pre_act
    )
    return gelu_value, gelu_slope


def mm(left, right):
    return jnp.dot(left, right, preferred_element_type=F32)


def mm_t(left, right):
    return lax.dot_general(left, right, (((1,), (1,)), ((), ())), preferred_element_type=F32)


def t_mm(left, right):
    return lax.dot_general(left, right, (((0,), (0,)), ((), ())), preferred_element_type=F32)


def split_heads(pair):
    first = lax.broadcasted_iota(jnp.int32, pair.shape, 1) < LANES // 2
    zero = jnp.zeros_like(pair)
    return jnp.concatenate([jnp.where(first, pair, zero), jnp.where(first, zero, pair)], axis=0)

def side_by_side(stack):
    n = stack.shape[0] // 2
    return jnp.concatenate([stack[:n], stack[n:]], axis=1)

def as_row(column):
    return jnp.transpose(jnp.broadcast_to(column, (column.shape[0], LANES)))[:1]

def interleave(into, near_ref, far_ref):
    for i in range(near_ref.shape[0] // BLOCK):
        rows = slice(i * BLOCK, (i + 1) * BLOCK)
        into[2 * i * BLOCK : (2 * i + 1) * BLOCK, :] = near_ref[rows, :]
        into[(2 * i + 1) * BLOCK : (2 * i + 2) * BLOCK, :] = far_ref[rows, :]

def lane_groups(x):
    return [x[:, i : i + LANES] for i in range(0, x.shape[1], LANES)]

def is_safe(peak, far_keys, scale):
    top = jnp.maximum(peak, jnp.max(jnp.abs(far_keys.astype(F32))))
    return (peak * top * (scale * (LANES // 2)) < 2.0**27).astype(jnp.int32)

def lanes_sum(x): return jnp.sum(x, axis=1, keepdims=True)

def fwd_kernel(near, pp, scale, flags, peak_ref, q_ref, kn_ref, vn_ref, kf_ref, vf_ref, feat_ref, hot_ref, o_ref, lse_ref,
               s_ref, m_ref, l_ref, acc_ref, k_all, v_all, safe_ref):
    qb = pl.program_id(1)
    nk = hot_ref.shape[0] // SPAN
    @pl.when(qb == 0)
    def _():
        interleave(k_all, kn_ref, kf_ref)
        interleave(v_all, vn_ref, vf_ref)
        safe_ref[0] = is_safe(peak_ref[0], kf_ref[...], scale)
    safe = safe_ref[0] == 1
    feat = feat_ref[...]
    feat2 = jnp.concatenate([feat, feat], axis=0)
    qs = [split_heads(q_ref[:, p*LANES:(p+1)*LANES] * scale) for p in range(pp)]
    m_ref[...] = jnp.full(m_ref.shape, -jnp.inf, F32)
    def scan_scores(exact):
        def step(j, _):
            @pl.when((flags[qb * nk + j] == 1) | jnp.logical_not(safe))
            def _():
                rows = pl.ds(pl.multiple_of(j * SPAN, SPAN), SPAN)
                hot = hot_ref[rows, :]
                for p in range(pp):
                    k = k_all[rows, p*LANES:(p+1)*LANES]
                    if exact:
                        ok = mm_t(feat2, hot) > -1.0
                        s = jnp.where(ok, mm_t(qs[p], k), MASKED)
                    else:
                        s = mm_t(jnp.concatenate([qs[p], feat2], axis=1), jnp.concatenate([k, hot], axis=1))
                    s_ref[p, j] = s
                    m_ref[p] = functools.reduce(jnp.maximum, lane_groups(s), m_ref[p])
            return 0
        lax.fori_loop(0, nk, step, 0)
    @pl.when(safe)
    def _(): scan_scores(False)
    @pl.when(jnp.logical_not(safe))
    def _(): scan_scores(True)
    tops = [jnp.max(m_ref[p], axis=1, keepdims=True) for p in range(pp)]
    l_ref[...] = jnp.zeros(l_ref.shape, F32)
    acc_ref[...] = jnp.zeros(acc_ref.shape, F32)
    def step(j, _):
        @pl.when((flags[qb * nk + j] == 1) | jnp.logical_not(safe))
        def _():
            rows = pl.ds(pl.multiple_of(j * SPAN, SPAN), SPAN)
            for p in range(pp):
                e = jnp.exp(s_ref[p, j] - tops[p])
                l_ref[p] += sum(lane_groups(e))
                v = split_heads(v_all[rows, p*LANES:(p+1)*LANES])
                acc_ref[p] += mm(side_by_side(e.astype(BF)), v)
        return 0
    lax.fori_loop(0, nk, step, 0)
    for p in range(pp):
        total = lanes_sum(l_ref[p])
        lse_ref[p, 0] = as_row(tops[p] + jnp.log(total))
        first = lax.broadcasted_iota(jnp.int32, (BLOCK, LANES), 1) < LANES // 2
        o_ref[:, p*LANES:(p+1)*LANES] = (acc_ref[p] / jnp.where(first, total[:BLOCK], total[BLOCK:])).astype(BF)

def attn_fwd(q, kv, far, feat, hot, flags, peak, scale, pp):
    near, width = q.shape
    total = hot.shape[0]
    steps = width // LANES // pp
    nq = near // BLOCK
    col = lambda c: (lambda h, i, f: (0, c * steps + h))
    return pl.pallas_call(
        functools.partial(fwd_kernel, near, pp, scale),
        grid_spec=pltpu.PrefetchScalarGridSpec(
            num_scalar_prefetch=1, grid=(steps, nq),
            in_specs=[
                pl.BlockSpec(memory_space=pltpu.SMEM),
                pl.BlockSpec((BLOCK, pp*LANES), lambda h, i, f: (i, h)),
                pl.BlockSpec((near, pp*LANES), col(0)),
                pl.BlockSpec((near, pp*LANES), col(1)),
                pl.BlockSpec((near, pp*LANES), col(0)),
                pl.BlockSpec((near, pp*LANES), col(1)),
                pl.BlockSpec((BLOCK, LANES), lambda h, i, f: (i, 0)),
                pl.BlockSpec((total, LANES), lambda h, i, f: (0, 0)),
            ],
            out_specs=[
                pl.BlockSpec((BLOCK, pp*LANES), lambda h, i, f: (i, h)),
                pl.BlockSpec((pp, 1, 1, 2*BLOCK), lambda h, i, f: (h, i, 0, 0)),
            ],
            scratch_shapes=[
                pltpu.VMEM((pp, total // SPAN, 2*BLOCK, SPAN), F32),
                pltpu.VMEM((pp, 2*BLOCK, LANES), F32),
                pltpu.VMEM((pp, 2*BLOCK, LANES), F32),
                pltpu.VMEM((pp, BLOCK, LANES), F32),
                pltpu.VMEM((total, pp*LANES), BF),
                pltpu.VMEM((total, pp*LANES), BF),
                pltpu.SMEM((1,), jnp.int32),
            ]),
        out_shape=[jax.ShapeDtypeStruct((near, width), BF), jax.ShapeDtypeStruct((width // LANES, nq, 1, 2*BLOCK), F32)],
        compiler_params=pltpu.CompilerParams(vmem_limit_bytes=56<<20),
        cost_estimate=cost(38),
        name="attn_forward",
    )(flags, peak, q, kv, kv, far, far, feat, hot)

def bwd_kernel(near, pp, scale, flags, peak_ref, q_ref, kn_ref, vn_ref, kf_ref, vf_ref, feat_ref, hot_ref, o_ref, do_ref, lse_ref,
               dq_ref, near_ref, far_ref, k_all, v_all, k_turned, dk_acc, dv_acc, dq_acc, safe_ref):
    half = LANES // 2
    qb = pl.program_id(1)
    nk = hot_ref.shape[0] // SPAN
    @pl.when(qb == 0)
    def _():
        interleave(k_all, kn_ref, kf_ref)
        interleave(v_all, vn_ref, vf_ref)
        safe_ref[0] = is_safe(peak_ref[0], kf_ref[...], scale)
        k_turned[...] = jnp.transpose(k_all[...])
        dk_acc[...] = jnp.zeros(dk_acc.shape, F32)
        dv_acc[...] = jnp.zeros(dv_acc.shape, F32)
    safe = safe_ref[0] == 1
    feat = feat_ref[...]
    feat2 = jnp.concatenate([feat, feat], axis=0)
    dq_acc[...] = jnp.zeros(dq_acc.shape, F32)
    qs, dos, deltas, lses = [], [], [], []
    for p in range(pp):
        cols = slice(p*LANES, (p+1)*LANES)
        qs.append(split_heads(q_ref[:, cols] * scale))
        do2 = split_heads(do_ref[:, cols])
        dos.append(do2)
        o = o_ref[:, cols].astype(F32)
        deltas.append(as_row(lanes_sum(do2.astype(F32) * jnp.concatenate([o, o], axis=0))))
        lses.append(lse_ref[p, 0])
    def sweep(exact):
        def step(j, _):
            @pl.when((flags[qb * nk + j] == 1) | jnp.logical_not(safe))
            def _():
                rows = pl.ds(pl.multiple_of(j * SPAN, SPAN), SPAN)
                hot = hot_ref[rows, :]
                for p in range(pp):
                    cols = slice(p*LANES, (p+1)*LANES)
                    k = k_all[rows, cols]; v = v_all[rows, cols]
                    if exact:
                        ok = mm_t(hot, feat2) > -1.0
                        s = jnp.where(ok, mm_t(k, qs[p]), MASKED)
                    else:
                        s = mm_t(jnp.concatenate([k, hot], axis=1), jnp.concatenate([qs[p], feat2], axis=1))
                    prob = jnp.exp(s - lses[p])
                    dprob = mm_t(v, dos[p])
                    ds = prob * (dprob - deltas[p])
                    if exact:
                        ds = jnp.where(ok, ds, 0.0)
                    ds = ds.astype(BF)
                    dv_acc[rows, cols] += mm(prob.astype(BF), dos[p])
                    dk_acc[rows, cols] += mm(ds, qs[p])
                    for h in range(2):
                        kt = k_turned[p*LANES + h*half : p*LANES + (h+1)*half, rows]
                        dq_acc[p, h*half:(h+1)*half] += mm(kt, ds[:, h*BLOCK:(h+1)*BLOCK])
            return 0
        lax.fori_loop(0, nk, step, 0)
    @pl.when(safe)
    def _(): sweep(False)
    @pl.when(jnp.logical_not(safe))
    def _(): sweep(True)
    for p in range(pp):
        dq_ref[:, p*LANES:(p+1)*LANES] = jnp.transpose(dq_acc[p] * scale).astype(BF)
    @pl.when(qb == pl.num_programs(1) - 1)
    def _():
        for i in range(near // BLOCK):
            rows = slice(i * BLOCK, (i + 1) * BLOCK)
            for side, acc in enumerate((dk_acc, dv_acc)):
                near_ref[side, rows] = acc[2 * i * BLOCK : (2 * i + 1) * BLOCK].astype(BF)
                far_ref[side, rows] = acc[(2 * i + 1) * BLOCK : (2 * i + 2) * BLOCK].astype(BF)

def attn_bwd(q, kv, far, feat, hot, flags, peak, attn, dattn, lse, scale, pp):
    near, width = q.shape
    total = hot.shape[0]
    steps = width // LANES // pp
    nq = near // BLOCK
    col = lambda c: (lambda h, i, f: (0, c * steps + h))
    rowblk = pl.BlockSpec((BLOCK, pp*LANES), lambda h, i, f: (i, h))
    whole = pl.BlockSpec((near, pp*LANES), col(0))
    both = pl.BlockSpec((2, near, pp*LANES), lambda h, i, f: (0, 0, h))
    return pl.pallas_call(
        functools.partial(bwd_kernel, near, pp, scale),
        grid_spec=pltpu.PrefetchScalarGridSpec(
            num_scalar_prefetch=1, grid=(steps, nq),
            in_specs=[
                pl.BlockSpec(memory_space=pltpu.SMEM),
                rowblk,
                pl.BlockSpec((near, pp*LANES), col(0)),
                pl.BlockSpec((near, pp*LANES), col(1)),
                whole,
                pl.BlockSpec((near, pp*LANES), col(1)),
                pl.BlockSpec((BLOCK, LANES), lambda h, i, f: (i, 0)),
                pl.BlockSpec((total, LANES), lambda h, i, f: (0, 0)),
                rowblk, rowblk,
                pl.BlockSpec((pp, 1, 1, 2*BLOCK), lambda h, i, f: (h, i, 0, 0)),
            ],
            out_specs=[rowblk, both, both],
            scratch_shapes=[
                pltpu.VMEM((total, pp*LANES), BF),
                pltpu.VMEM((total, pp*LANES), BF),
                pltpu.VMEM((pp*LANES, total), BF),
                pltpu.VMEM((total, pp*LANES), F32),
                pltpu.VMEM((total, pp*LANES), F32),
                pltpu.VMEM((pp, LANES, BLOCK), F32),
                pltpu.SMEM((1,), jnp.int32),
            ]),
        out_shape=[
            jax.ShapeDtypeStruct((near, width), BF),
            jax.ShapeDtypeStruct((2, near, width), BF),
            jax.ShapeDtypeStruct((2, near, width), BF),
        ],
        compiler_params=pltpu.CompilerParams(vmem_limit_bytes=56<<20),
        cost_estimate=cost(63),
        name="attn_backward",
    )(flags, peak, q, kv, kv, far, far, feat, hot, attn, dattn, lse)


def assemble_kernel(shards, where, own_ref, half_ref, other_ref, out_ref):
    s, c, plane = where[0], where[1], where[2]
    groups, planes = own_ref.shape[0], half_ref.shape[0]
    out_ref[pl.ds(s * groups, groups)] = own_ref[...]
    for side, source in ((c, half_ref), (1 - c, other_ref)):
        for j in range(planes):
            for k in range(1, shards):
                place = lax.rem(s + shards - k, shards)
                out_ref[place * groups + side * planes + (plane ^ j)] = source[j, k - 1]


def assemble(where, own, half, other, shards):
    rows, width = own.shape
    fine = half.shape[2]
    groups = rows // fine
    full = lambda *shape: pl.BlockSpec(shape, lambda i, w: (0,) * len(shape))
    out = pl.pallas_call(
        functools.partial(assemble_kernel, shards),
        grid_spec=pltpu.PrefetchScalarGridSpec(
            num_scalar_prefetch=1,
            grid=(1,),
            in_specs=[full(groups, fine, width), full(*half.shape), full(*half.shape)],
            out_specs=full(groups * shards, fine, width),
        ),
        out_shape=jax.ShapeDtypeStruct((groups * shards, fine, width), own.dtype),
        compiler_params=pltpu.CompilerParams(vmem_limit_bytes=60 << 20),
        name="assemble",
    )(where, own.reshape(groups, fine, width), half, other)
    return out.reshape(shards * rows, width)


def entry_kernel(tok_ref, vec_ref, w_ref, act_ref, q_ref, kv_ref, peak_ref):
    step = pl.program_id(0)
    rows, pieces = SPAN, tok_ref.shape[0] // SPAN

    @pl.when(step == 0)
    def _():
        gain, lift, shift = (vec_ref[i : i + 1, :] for i in range(3))
        for i in range(pieces):
            at = slice(i * rows, (i + 1) * rows)
            normed, _unused = layer_norm(tok_ref[at, :].astype(F32))
            act_ref[at, :] = (normed * gain * lift + shift).astype(BF)
        peak_ref[...] = jnp.zeros_like(peak_ref)

    top = jnp.zeros((1, w_ref.shape[1]), F32)
    for i in range(pieces):
        at = slice(i * rows, (i + 1) * rows)
        value = mm(act_ref[at, :], w_ref[...])
        low = value.astype(BF)
        top = jnp.maximum(top, jnp.max(jnp.abs(low.astype(F32)), axis=0, keepdims=True))

        @pl.when(step < 2)
        def _():
            kv_ref[at, :] = low

        @pl.when(step == 2)
        def _():
            q_ref[at, :] = low

    peak_ref[0:1, :] = jnp.maximum(peak_ref[0:1, :], top)


def entry(tok, vec, qkv_w):
    total, width = tok.shape
    fixed = lambda *shape: pl.BlockSpec(shape, lambda j: (0,) * len(shape))
    return pl.pallas_call(
        entry_kernel,
        grid=(3,),
        in_specs=[
            fixed(total, width), fixed(8, width),
            pl.BlockSpec((width, width), lambda j: (0, lax.rem(j + 1, 3))),
        ],
        out_specs=[
            fixed(total, width), fixed(total, width),
            pl.BlockSpec((total, width), lambda j: (0, jnp.minimum(j, 1))),
            fixed(8, width),
        ],
        out_shape=[
            jax.ShapeDtypeStruct((total, width), BF),
            jax.ShapeDtypeStruct((total, width), BF),
            jax.ShapeDtypeStruct((total, 2 * width), BF),
            jax.ShapeDtypeStruct((8, width), F32),
        ],
        compiler_params=pltpu.CompilerParams(vmem_limit_bytes=48 << 20),
        cost_estimate=cost(9),
        name="entry",
    )(tok, vec, qkv_w)


def leave_kernel(spots, where, dq_ref, near_ref, far_ref, act_ref, w_ref, tok_in, dmid_in, vec_ref,
                 grad_ref, mine_ref, yours_ref, sums_ref, d_all, da, tok_ref, dmid_ref, sems):
    step = pl.program_id(0)
    total = dq_ref.shape[0]
    sides, planes, places, fine = spots

    late = [
        pltpu.make_async_copy(tok_in, tok_ref, sems.at[0]),
        pltpu.make_async_copy(dmid_in, dmid_ref, sems.at[1]),
    ]

    @pl.when(step == 0)
    def _():
        for copy in late:
            copy.start()
        d_all[...] = dq_ref[...]
        da[...] = jnp.zeros_like(da)

    @pl.when(step > 0)
    def _():
        d_all[...] = (near_ref[0].astype(F32) + far_ref[0].astype(F32)).astype(BF)

    grad = t_mm(act_ref[...], d_all[...])

    def put(ref, side):
        for place in range(places):
            turned = lax.rem(place + places - where[0], places)
            for plane in range(planes):
                start = ((place * sides + side) * planes + plane) * fine
                ref[plane ^ where[2], turned] = grad[start : start + fine].astype(BF)

    for side in range(sides):
        pl.when(where[1] == side)(functools.partial(put, mine_ref, side))
        pl.when(where[1] != side)(functools.partial(put, yours_ref, side))

    def add(r, _):
        rows = pl.ds(pl.multiple_of(r * SPAN, SPAN), SPAN)
        da[rows, :] += mm_t(d_all[rows, :], w_ref[...])
        return 0

    lax.fori_loop(0, total // SPAN, add, 0)

    @pl.when(step == 2)
    def _():
        gain, lift, shift = (vec_ref[i : i + 1, :] for i in range(3))
        sums_ref[...] = jnp.zeros_like(sums_ref)
        for copy in late:
            copy.wait()

        def finish(r, _):
            rows = pl.ds(pl.multiple_of(r * SPAN, SPAN), SPAN)
            normed, inv = layer_norm(tok_ref[rows, :].astype(F32))
            part = da[rows, :]
            grad_h = part * lift
            back = norm_back(grad_h * gain, normed, inv)
            grad_ref[rows, :] = (dmid_ref[rows, :] + back).astype(BF)
            for i, term in enumerate((part, part * (normed * gain), grad_h * normed)):
                sums_ref[i : i + 1, :] += jnp.sum(term, axis=0, keepdims=True)
            return 0

        lax.fori_loop(0, total // SPAN, finish, 0)


def leave(where, q_grads, near, far, act, qkv_w, tok, dmid, vec, spots):
    total, width = q_grads.shape
    keep = pl.Buffered(1)
    whole = pl.BlockSpec((total, width), lambda j, w: (0, 0), pipeline_mode=keep)
    both = pl.BlockSpec((1, total, width), lambda j, w: (jnp.maximum(j - 1, 0), 0, 0))
    small = pl.BlockSpec((8, width), lambda j, w: (0, 0))
    part = pl.BlockSpec(tuple(spots[1:]) + (width,), lambda j, w: (0, 0, 0, j))
    return pl.pallas_call(
        functools.partial(leave_kernel, spots),
        grid_spec=pltpu.PrefetchScalarGridSpec(
            num_scalar_prefetch=1,
            grid=(3,),
            in_specs=[
                whole, both, both, whole,
                pl.BlockSpec((width, width), lambda j, w: (0, j)),
                pl.BlockSpec(memory_space=pl.ANY),
                pl.BlockSpec(memory_space=pl.ANY),
                small,
            ],
            out_specs=[
                whole,
                part, part,
                small,
            ],
            scratch_shapes=[
                pltpu.VMEM((total, width), BF),
                pltpu.VMEM((total, width), F32),
                pltpu.VMEM((total, width), BF),
                pltpu.VMEM((total, width), F32),
                pltpu.SemaphoreType.DMA((2,)),
            ],
        ),
        out_shape=[
            jax.ShapeDtypeStruct((total, width), BF),
            jax.ShapeDtypeStruct(tuple(spots[1:]) + (3 * width,), BF),
            jax.ShapeDtypeStruct(tuple(spots[1:]) + (3 * width,), BF),
            jax.ShapeDtypeStruct((8, width), F32),
        ],
        compiler_params=pltpu.CompilerParams(vmem_limit_bytes=56 << 20),
        cost_estimate=cost(14),
        name="leave",
    )(where, q_grads, near, far, act, qkv_w, tok, dmid, vec)


def settle_kernel(where, half_ref, other_ref, out_ref):
    c, plane = where[1], where[2]
    for side, source in ((c, half_ref), (1 - c, other_ref)):
        for j in range(half_ref.shape[0]):
            out_ref[side * half_ref.shape[0] + (plane ^ j)] = source[j].astype(F32)


def settle(where, half, other):
    planes, fine, width = half.shape
    full = lambda *shape: pl.BlockSpec(shape, lambda i, w: (0,) * len(shape))
    return pl.pallas_call(
        settle_kernel,
        grid_spec=pltpu.PrefetchScalarGridSpec(
            num_scalar_prefetch=1,
            grid=(1,),
            in_specs=[full(planes, fine, width)] * 2,
            out_specs=full(2 * planes, fine, width),
        ),
        out_shape=jax.ShapeDtypeStruct((2 * planes, fine, width), F32),
        compiler_params=pltpu.CompilerParams(vmem_limit_bytes=40 << 20),
        name="settle",
    )(where, half, other)


def unpack_kernel(count, where, half_ref, other_ref, out_ref, fc1_ref, fc2_ref):
    step = pl.program_id(0)
    c, plane = where[1], where[2]

    def fill(ref):
        for side, source in ((c, half_ref), (1 - c, other_ref)):
            for j in range(source.shape[0]):
                ref[2 * (plane ^ j) + side] = source[j].astype(F32).reshape(ref.shape[1:])

    @pl.when(step == 0)
    def _():
        fill(out_ref)

    @pl.when((step > 0) & (step <= count))
    def _():
        fill(fc1_ref)

    @pl.when(step > count)
    def _():
        fill(fc2_ref)


def unpack(where, half, other, width):
    planes, fine, total = half.shape
    groups, count = 2 * planes, total // width // 2
    block = pl.BlockSpec((planes, fine, width), lambda i, w: (0, 0, i))
    low = lambda i: jnp.clip(i, 0, count - 1)
    out, fc1, fc2 = pl.pallas_call(
        functools.partial(unpack_kernel, count),
        grid_spec=pltpu.PrefetchScalarGridSpec(
            num_scalar_prefetch=1,
            grid=(1 + 2 * count,),
            in_specs=[block, block],
            out_specs=[
                pl.BlockSpec((groups, fine, width), lambda i, w: (0, 0, 0)),
                pl.BlockSpec((groups, fine, width), lambda i, w: (0, 0, low(i - 1))),
                pl.BlockSpec((groups, 1, fine, width), lambda i, w: (0, low(i - 1 - count), 0, 0)),
            ],
        ),
        out_shape=[
            jax.ShapeDtypeStruct((groups, fine, width), F32),
            jax.ShapeDtypeStruct((groups, fine, count * width), F32),
            jax.ShapeDtypeStruct((groups, count, fine, width), F32),
        ],
        compiler_params=pltpu.CompilerParams(vmem_limit_bytes=40 << 20),
        cost_estimate=cost(4),
        name="unpack",
    )(where, half, other)
    return out.reshape(-1, width), fc1.reshape(-1, count * width), fc2.reshape(-1, width)


def cost(microseconds):
    return pl.CostEstimate(
        flops=int(microseconds * 1.15e9), bytes_accessed=1 << 20, transcendentals=0
    )


def middle_kernel(chunks, where, attn_ref, tok_ref, cot_ref, vec_ref, b1_ref, wo_ref, w1_ref, *rest):
    w2_refs, rest = rest[:chunks], rest[chunks:]
    (out_ref, dattn_ref, dmid_ref, grads_ref, sums_ref, gb1_ref) = rest[:6]
    (mid, branch, act, dy, two, da, hid, dpre, w2, wide, tall, sems) = rest[6:]
    width = attn_ref.shape[1]

    def send_wide(column):
        cols = pl.ds(pl.multiple_of(column * width, LANES), width)
        return pltpu.make_async_copy(wide, grads_ref.at[:, :, :, cols], sems.at[0])

    def turned(place):
        return lax.rem(place + chunks - where[0], chunks)

    def send_tall(place):
        cols = pl.ds((1 + chunks) * width, chunks * width)
        return pltpu.make_async_copy(tall, grads_ref.at[:, turned(place), :, cols], sems.at[1])

    step = pl.program_id(0)
    total = attn_ref.shape[0]
    blocks = total // SPAN
    gate_one, gain, lift, shift, gate_two, fc2_b = (vec_ref[i : i + 1, :] for i in range(6))

    def rows_of(r):
        return pl.ds(pl.multiple_of(r * SPAN, SPAN), SPAN)

    @pl.when(step == 0)
    def _():
        sums_ref[...] = jnp.zeros_like(sums_ref)

        def start(r, _):
            rows = rows_of(r)
            one = mm(attn_ref[rows, :], wo_ref[...])
            middle = tok_ref[rows, :].astype(F32) + gate_one * one
            normed, _unused = layer_norm(middle)
            branch[rows, :] = one
            mid[rows, :] = middle
            act[rows, :] = (normed * gain * lift + shift).astype(BF)
            dy[rows, :] = (cot_ref[rows, :].astype(F32) * gate_two).astype(BF)
            two[rows, :] = jnp.zeros((SPAN, two.shape[1]), F32)
            da[rows, :] = jnp.zeros((SPAN, da.shape[1]), F32)
            return 0

        lax.fori_loop(0, blocks, start, 0)

    @pl.when(step < chunks)
    def _():
        height = w2_refs[0].shape[0]
        for b in range(chunks):
            w2[b * height : (b + 1) * height, :] = w2_refs[b][...]
        gb1_ref[...] = jnp.zeros_like(gb1_ref)

        def chunk(r, _):
            rows = rows_of(r)
            value, slope = gelu_parts(mm(act[rows, :], w1_ref[...]) + b1_ref[...])
            hidden = value.astype(BF)
            hid[rows, :] = hidden
            two[rows, :] += mm(hidden, w2[...])
            grad = (mm_t(dy[rows, :], w2[...]) * slope).astype(BF)
            dpre[rows, :] = grad
            gb1_ref[...] += jnp.sum(grad.astype(F32), axis=0, keepdims=True)
            da[rows, :] += mm_t(grad, w1_ref[...])
            return 0

        lax.fori_loop(0, blocks, chunk, 0)
        grad_two = t_mm(hid[...], dy[...])
        grad_one = t_mm(act[...], dpre[...])

        @pl.when(step > 0)
        def _():
            send_wide(step).wait()
            send_tall(step - 1).wait()

        groups, fine = tall.shape[:2]
        for g in range(groups):
            for b in range(chunks):
                start = (g * chunks + b) * fine
                tall[g, :, b * width : (b + 1) * width] = grad_two[start : start + fine].astype(BF)
        put_blocks(wide, grad_one, turned)
        send_wide(step + 1).start()
        send_tall(step).start()

    @pl.when(step == chunks)
    def _():
        def finish(r, _):
            rows = rows_of(r)
            cot = cot_ref[rows, :].astype(F32)
            middle = mid[rows, :]
            second = two[rows, :] + fc2_b
            out_ref[rows, :] = (middle + gate_two * second).astype(BF)
            normed, inv = layer_norm(middle)
            lifted = normed * gain
            grad = da[rows, :]
            grad_h = grad * lift
            dmid = cot + norm_back(grad_h * gain, normed, inv)
            dmid_ref[rows, :] = dmid
            dy_one = (dmid * gate_one).astype(BF)
            dpre[rows, :] = dy_one
            dattn_ref[rows, :] = mm_t(dy_one, wo_ref[...]).astype(BF)
            parts = (
                dmid * branch[rows, :], grad, grad * lifted, cot * second,
                grad_h * normed, dy[rows, :].astype(F32),
            )
            for i, part in enumerate(parts):
                sums_ref[i : i + 1, :] += jnp.sum(part, axis=0, keepdims=True)
            return 0

        lax.fori_loop(0, blocks, finish, 0)
        grad_out = t_mm(attn_ref[...], dpre[...])
        send_wide(step).wait()
        send_tall(step - 1).wait()
        put_blocks(wide, grad_out, turned)
        send_wide(0).start()
        send_wide(0).wait()


def put_blocks(ref, grad, turned):
    groups, places, rows = ref.shape[:3]
    for s in range(places):
        for g in range(groups):
            start = (s * groups + g) * rows
            ref[g, turned(s)] = grad[start : start + rows].astype(BF)


def middle(where, attn, tok, cot, vec, fc1_b, pack, groups):
    total, width = attn.shape
    shards = pack.shape[1] // width - 5
    fine = width // shards // groups
    keep = pl.Buffered(1)
    whole = pl.BlockSpec((total, width), lambda i, w: (0, 0), pipeline_mode=keep)
    last = shards - 1
    low = lambda i: jnp.minimum(i, last)
    w2_spec = lambda b: pl.BlockSpec((width // shards, width), lambda i, w: (low(i), 5 + b))
    return pl.pallas_call(
        functools.partial(middle_kernel, shards),
        grid_spec=pltpu.PrefetchScalarGridSpec(
            num_scalar_prefetch=1,
            grid=(shards + 1,),
            in_specs=[
            whole, whole, whole,
            pl.BlockSpec((8, width), lambda i, w: (0, 0)),
            pl.BlockSpec((1, width), lambda i, w: (0, low(i))),
            pl.BlockSpec((width, width), lambda i, w: (0, 0), pipeline_mode=keep),
            pl.BlockSpec((width, width), lambda i, w: (0, 1 + low(i))),
        ] + [w2_spec(b) for b in range(shards)],
        out_specs=[
            whole, whole, whole,
            pl.BlockSpec(memory_space=pl.ANY),
            pl.BlockSpec((8, width), lambda i, w: (0, 0)),
            pl.BlockSpec((1, width), lambda i, w: (0, low(i))),
        ],
        scratch_shapes=[
            pltpu.VMEM((total, width), F32),
            pltpu.VMEM((total, width), F32),
            pltpu.VMEM((total, width), BF),
            pltpu.VMEM((total, width), BF),
            pltpu.VMEM((total, width), F32),
            pltpu.VMEM((total, width), F32),
            pltpu.VMEM((total, width), BF),
            pltpu.VMEM((total, width), BF),
            pltpu.VMEM((width, width), BF),
            pltpu.VMEM((groups, shards, fine, width), BF),
            pltpu.VMEM((groups, fine, shards * width), BF),
            pltpu.SemaphoreType.DMA((2,)),
        ],
        ),
        out_shape=[
            jax.ShapeDtypeStruct((total, width), BF),
            jax.ShapeDtypeStruct((total, width), BF),
            jax.ShapeDtypeStruct((total, width), F32),
            jax.ShapeDtypeStruct((groups, shards, fine, 9 * width), BF),
            jax.ShapeDtypeStruct((8, width), F32),
            jax.ShapeDtypeStruct((1, 4 * width), F32),
        ],
        compiler_params=pltpu.CompilerParams(vmem_limit_bytes=60 << 20),
        cost_estimate=cost(55),
        name="middle",
    )(where, attn, tok, cot, vec, fc1_b, pack, pack, *([pack] * shards))


class Links:
    def __init__(self, groups, shards):
        self.groups, self.shards, self.planes = groups, shards, groups // 2
        self.g = lax.axis_index("group")
        self.s = lax.axis_index("shard")
        self.c = self.g % 2
        self.plane = self.g // 2
        tilt = self.plane if self.planes == 4 else 0 * self.plane
        self.where = jnp.stack([self.s, self.c, tilt]).astype(jnp.int32)

    def swap(self, value):
        return lax.ppermute(value, "group", [(i, i ^ 1) for i in range(self.groups)])

    def turn(self, value, step):
        n = self.shards
        return lax.ppermute(value, "shard", [(i, (i + step) % n) for i in range(n)])

    def across(self, value, step):
        return lax.ppermute(value, "group", [(i, i ^ (2 * step)) for i in range(self.groups)])

    def give(self, value):
        batches, rows, width = value.shape
        halves = value.reshape(batches, 2, rows // 2, width)
        keep = lax.dynamic_index_in_dim(halves, self.c, 1, False)
        return keep, lax.dynamic_index_in_dim(halves, 1 - self.c, 1, False)

    def to_trees(self, keep, got):
        return self.exchange(self.by_core(keep, got).reshape(-1, *keep.shape[1:]))

    def exchange(self, by_tree):
        return lax.all_to_all(by_tree, "shard", 0, 0).reshape(-1, by_tree.shape[-1])

    def by_core(self, mine, other):
        return jnp.where(
            self.c == 0, jnp.stack([mine, other], axis=1), jnp.stack([other, mine], axis=1)
        )

    def from_trees(self, value):
        return lax.all_to_all(
            value.reshape(self.shards, -1, value.shape[1]), "shard", 0, 0
        )

    def back(self, value, batches):
        by_core = value.reshape(batches, 2, *value.shape[1:])
        keep = lax.dynamic_index_in_dim(by_core, self.c, 1, False)
        return keep, lax.dynamic_index_in_dim(by_core, 1 - self.c, 1, False)

    def lay_out(self, keep, got):
        return self.by_core(keep, got).reshape(keep.shape[0], 1, -1, keep.shape[-1])

    def plane_order(self, parts):
        stacked = jnp.stack(parts)
        if self.planes != 4:
            return stacked
        return jnp.stack(
            [lax.dynamic_index_in_dim(stacked, self.plane ^ j, 0, False) for j in range(4)]
        )

    def line_order(self, parts):
        stacked = jnp.stack(parts)
        return jnp.stack(
            [
                lax.dynamic_index_in_dim(stacked, (self.s - j) % self.shards, 0, False)
                for j in range(self.shards)
            ]
        )

    def gather_all(self, part):
        return lax.all_gather(part, ("shard", "group"), axis=0, tiled=True)

    def my_rows(self, weight):
        rows = weight.shape[-2] // self.groups
        return lax.dynamic_slice_in_dim(weight, self.g * rows, rows, weight.ndim - 2)

    def group_sum(self, blocks):
        out = lax.psum_scatter(blocks, "group", scatter_dimension=0, tiled=True)
        return out

    def plane_sum(self, value):
        if self.planes != 4:
            groups = [[2 * p + c for p in range(self.planes)] for c in range(2)]
            return lax.psum_scatter(
                value, "group", scatter_dimension=1, axis_index_groups=groups
            ).astype(F32)
        total = lax.dynamic_index_in_dim(value, self.plane, 1, False).astype(F32)
        for k in range(1, 4):
            piece = lax.dynamic_index_in_dim(value, self.plane ^ k, 1, False)
            total = total + self.across(piece, k).astype(F32)
        return total

    def plane_gather(self, value):
        if self.planes != 4:
            groups = [[2 * p + c for p in range(self.planes)] for c in range(2)]
            return lax.all_gather(value, "group", axis_index_groups=groups)
        parts = jnp.stack([value] + [self.across(value, k) for k in range(1, 4)])
        return jnp.stack(
            [lax.dynamic_index_in_dim(parts, self.plane ^ j, 0, False) for j in range(4)]
        )

    def turns(self, values):
        return [self.turn(values[k], k) for k in range(1, self.shards)]

    def spread(self, value):
        if self.planes != 4:
            every = self.plane_gather(value)
            return [every[j] for j in range(self.planes)]
        return [value] + [self.across(value, k) for k in range(1, 4)]


def total(terms):
    result = terms[0].astype(F32)
    for term in terms[1:]:
        result = result + term.astype(F32)
    return result


def on_device(
    tokens,
    cond,
    seg_ids,
    parents,
    cotangent,
    w_qkv,
    w_out,
    w_fc1,
    b_fc1,
    w_fc2,
    b_fc2,
    w_ada,
    b_ada,
    gain1,
    gain2,
    groups,
):
    batches, _, row_count, width = tokens.shape
    shards = lax.axis_size("shard")
    assert shards == 2 * batches and groups % 2 == 0
    head_dim = width // HEADS
    scale = 1.0 / math.sqrt(head_dim)
    net = Links(groups, shards)
    rows = row_count // 2
    mine = shards * rows
    tree_len = seg_ids.shape[2]
    labels = parents.shape[2]
    cond_dim = cond.shape[2]

    fc2_blocks = net.my_rows(w_fc2.reshape(shards, -1, width))
    share = jnp.concatenate(
        [net.my_rows(w_out), net.my_rows(w_fc1)] + [fc2_blocks[b] for b in range(shards)],
        axis=1,
    )

    packed = jnp.concatenate(
        [seg_ids[:, 0].astype(F32), parents[:, 0].astype(F32), cond[:, 0]], axis=1
    )
    part_rows = w_qkv.shape[0] // groups
    early_w = jnp.concatenate([w_qkv, w_ada.reshape(-1, width)], axis=1)
    own_part = lax.dynamic_index_in_dim(
        early_w.reshape(groups, part_rows, -1), net.c * (groups // 2) + net.plane, 0, False
    )
    tok_keep, tok_give = net.give(tokens[:, 0])
    other = net.swap(packed)
    line_w = net.turns([own_part] * shards)
    tok_got = net.swap(tok_give)
    other, line_w, tok_got, share = lax.optimization_barrier((other, line_w, tok_got, share))
    pack = net.gather_all(share)
    tok = net.to_trees(tok_keep, tok_got)
    plane_w = net.spread(jnp.stack(line_w))
    cot_keep, cot_give = net.give(cotangent[:, 0])
    trees = jnp.where(
        net.c == 0, jnp.stack([packed, other], axis=1), jnp.stack([other, packed], axis=1)
    ).reshape(shards, packed.shape[1])
    conds = trees[:, tree_len + labels :]
    my_tree = lax.dynamic_index_in_dim(trees, net.s, 0, False)
    tree_seg = my_tree[:tree_len]
    parent_row = my_tree[tree_len : tree_len + labels]
    ada_rows = jnp.dot(conds, w_ada.astype(F32), precision=HIGH) + b_ada.astype(F32)
    small = jnp.concatenate([b_fc1, b_fc2, gain1, gain2]).astype(F32)
    pieces = jnp.concatenate(
        [ada_rows, jnp.broadcast_to(small[None], (shards, small.shape[0]))], axis=1
    )
    plane_w, tok, pieces, cot_give = lax.optimization_barrier(
        (plane_w, tok, pieces, cot_give)
    )
    cot_got = net.swap(cot_give)
    got = [lax.dynamic_index_in_dim(pieces, net.s, 0, False)]
    for k in range(1, shards):
        piece = lax.dynamic_index_in_dim(pieces, (net.s + k) % shards, 0, False)
        got.append(net.turn(piece, k))
    half_w = jnp.stack(plane_w)
    qkv_w = assemble(net.where, early_w, half_w, net.swap(half_w), shards)
    line = net.line_order(got)
    cut = ada_rows.shape[1]
    ada = line[:, :cut].reshape(-1)
    ends = [cut]
    for vec in (b_fc1, b_fc2, gain1, gain2):
        ends.append(ends[-1] + vec.shape[0])
    fc1_b, fc2_b, gain_a, gain_b = (
        line[:, ends[i] : ends[i + 1]].reshape(-1) for i in range(4)
    )
    shift_one, scale_one, gate_one, shift_two, scale_two, gate_two = jnp.split(ada, 6)

    half_seg = tree_seg.reshape(shards, 2, rows)

    def row_segs(half):
        return lax.dynamic_index_in_dim(half_seg, half, 1, False).reshape(-1)

    query_seg = row_segs(net.c)
    key_seg = jnp.stack(
        [query_seg.reshape(shards, rows), row_segs(1 - net.c).reshape(shards, rows)], axis=1
    ).reshape(-1)
    lanes = jnp.arange(LANES, dtype=F32)
    table = jnp.zeros((LANES,), F32).at[:labels].set(parent_row)
    up_two = jnp.sum(jnp.where(table[:, None] == lanes[None, :], table[None, :], 0.0), axis=1)
    reach = (
        (lanes[:, None] == lanes[None, :])
        | (table[:, None] == lanes[None, :])
        | (up_two[:, None] == lanes[None, :])
    )
    hot = (key_seg[:, None] == lanes[None, :]).astype(BF)
    hot_mine = hot.reshape(shards, 2, rows, LANES)[:, 0].reshape(mine, LANES)
    feat = mm(hot_mine, jnp.where(reach, 0.0, BIG).astype(BF)).astype(BF)
    held = jnp.max(hot.reshape(-1, SPAN, LANES), axis=1)
    asking = jnp.max(hot_mine.reshape(-1, BLOCK, LANES), axis=1)
    wanted = mm(asking, reach.astype(BF)).astype(BF)
    flags = (mm_t(wanted, held) > 0.5).reshape(-1).astype(jnp.int32)

    vec_one = jnp.stack([gain_a, 1.0 + scale_one, shift_one] + [gain_a] * 5)
    cot_both = net.by_core(cot_keep, cot_got).reshape(shards, rows, width)
    act_one, query, kv, peak = entry(tok, vec_one, qkv_w)
    kv, cot_both = lax.optimization_barrier((kv, cot_both))
    far = net.swap(kv)
    grad_out = net.exchange(cot_both)
    bound = jnp.max(peak[:1]).reshape(1)
    attn, log_totals = attn_fwd(query, kv, far, feat, hot, flags, bound, scale, PAIRS)
    vec = jnp.stack(
        [gate_one, gain_b, 1.0 + scale_two, shift_two, gate_two, fc2_b, fc2_b, fc2_b]
    )
    result, grad_attn, grad_mid, blocks, sums, g_b1 = middle(
        net.where, attn, tok, grad_out, vec, fc1_b[None], pack, groups
    )
    out_rows = net.from_trees(result)

    parts = net.group_sum(blocks.reshape(-1, 9 * width)).reshape(shards, -1, 9 * width)
    q_grads, near_grads, far_grads = attn_bwd(
        query, kv, far, feat, hot, flags, bound, attn, grad_attn, log_totals, scale, PAIRS
    )
    near_grads, parts, out_rows = lax.optimization_barrier((near_grads, parts, out_rows))
    out_keep, out_give = net.back(out_rows, batches)
    out_got = net.swap(out_give)
    turned = net.turns(parts)
    grad_in, g_mine, g_yours, late_sums = leave(
        net.where, q_grads, near_grads, net.swap(far_grads), act_one, qkv_w, tok, grad_mid,
        vec_one, (2, groups // 2, shards, part_rows),
    )

    turned, out_got, grad_in, g_mine, g_yours, late_sums = lax.optimization_barrier(
        (turned, out_got, grad_in, g_mine, g_yours, late_sums)
    )
    span = g_mine.shape[-1]
    g_got = net.swap(g_yours)
    grads_rows = net.from_trees(grad_in)
    small = jnp.concatenate(
        [late_sums[:2], sums[:4], late_sums[2:3], sums[4:6], g_b1.reshape(-1, width)]
    ).astype(BF)
    n_ada = 6 * width
    small_got = net.swap(small)
    rest_line = total([parts[0]] + turned).astype(BF)
    my_cond = lax.dynamic_index_in_dim(conds, net.s, 0, False)
    cond_top = my_cond.astype(BF)
    tree_extra = jnp.concatenate([cond_top, (my_cond - cond_top.astype(F32)).astype(BF)])
    g_got, small_got, rest_line, tree_extra = lax.optimization_barrier(
        (g_got, small_got, rest_line, tree_extra)
    )
    pairs = [
        total([g_mine[k], g_got[k]]).astype(BF).reshape(-1, span) for k in range(groups // 2)
    ]
    pair_small = total([small, small_got]).astype(BF).reshape(-1)
    per_tree = jnp.concatenate([pair_small[:n_ada], tree_extra, pair_small[n_ada:]])
    n_tree = per_tree.shape[0]
    if groups == 8:
        plane_terms = [pairs[0]] + [net.across(pairs[k], k) for k in range(1, 4)]
    else:
        plane_terms = [net.plane_sum(jnp.stack(pairs)[None])[0]]
    plane_small = net.spread(per_tree)
    out = net.lay_out(out_keep, out_got)
    plane_terms, plane_small, grads_rows, rest_line, out = lax.optimization_barrier(
        (plane_terms, plane_small, grads_rows, rest_line, out)
    )

    line_terms = total(plane_terms).astype(BF).reshape(shards, -1, span)
    every_plane = net.plane_order(plane_small)
    mid_part = n_ada + 2 * cond_dim
    bias_sum = jnp.sum(every_plane[:, mid_part:].astype(F32), axis=0).astype(BF)
    line_small = jnp.concatenate([every_plane[:, :mid_part].reshape(-1), bias_sum])
    n_line = line_small.shape[0]
    more = -(-n_line // (8 * span)) * 8
    line_small = jnp.pad(line_small, (0, more * span - n_line)).reshape(more, span)
    line_sent = jnp.concatenate(
        [line_terms, jnp.broadcast_to(line_small[None], (shards, more, span))], axis=1
    )
    line_got = net.turns(line_sent)
    rest_plane = net.spread(rest_line)
    grads_keep, grads_give = net.back(grads_rows, batches)
    grads_got = net.swap(grads_give)
    line_got, rest_plane, grads_got = lax.optimization_barrier((line_got, rest_plane, grads_got))
    rest_half = jnp.stack(rest_plane)
    rest_other = net.swap(rest_half)

    fine = line_terms.shape[1]
    qkv_sum = total([line_terms[0]] + [got[:fine] for got in line_got]).astype(BF)
    qkv_plane = net.spread(qkv_sum)
    everyone = net.line_order([line_small] + [got[fine:] for got in line_got])
    everyone = everyone.reshape(shards, -1)[:, :n_line].astype(F32)
    by_tree = everyone[:, : (groups // 2) * mid_part].reshape(shards, groups // 2, mid_part)
    t_out, t_fc1, t_fc2 = unpack(net.where, rest_half, rest_other, width)
    grads_x = net.lay_out(grads_keep, grads_got)

    every_dada = by_tree[:, :, : 6 * width].reshape(-1, 6 * width)
    every_cond = (
        by_tree[:, :, 6 * width : 6 * width + cond_dim] + by_tree[:, :, 6 * width + cond_dim :]
    ).reshape(-1, cond_dim)
    dada = lax.dynamic_index_in_dim(by_tree[:, :, : 6 * width], net.plane, 1, False)
    g_one, g_two, g_bias2, g_bias1 = jnp.split(
        jnp.sum(everyone[:, (groups // 2) * mid_part :], axis=0), [width, 2 * width, 3 * width]
    )

    def place(vec):
        n = vec.shape[-1] // shards
        return lax.dynamic_slice_in_dim(vec, net.s * n, n, vec.ndim - 1)

    dada_here = place(every_dada)
    t_ada = lax.dot_general(
        every_cond, dada_here, (((0,), (0,)), ((), ())), precision=HIGH
    )
    t_bada = jnp.sum(dada_here, axis=0)
    own = lax.dynamic_index_in_dim(dada.reshape(batches, 2, -1), net.c, 1, False)
    ada_w = qkv_w[:, 3 * width :].reshape(shards, cond_dim, -1).astype(F32)
    cond_total = jnp.einsum(
        "bsn,scn->bc", own.reshape(batches, shards, -1), ada_w, precision=HIGH
    )
    qkv_half = jnp.stack(qkv_plane)
    t_qkv = settle(net.where, qkv_half, net.swap(qkv_half)).reshape(w_qkv.shape)
    return (
        out,
        grads_x,
        cond_total[:, None, :],
        t_qkv,
        t_out,
        t_fc1,
        place(g_bias1),
        t_fc2,
        place(g_bias2),
        t_ada,
        t_bada,
        place(g_one),
        place(g_two),
    )


def solution(mesh):
    in_specs = (
        P(None, "group", "shard", None),
        P(None, "group", None),
        P(None, "group", None),
        P(None, "group", None),
        P(None, "group", "shard", None),
        P("shard", None),
        P("shard", None),
        P("shard", None),
        P("shard"),
        P("shard", None),
        P("shard"),
        P(None, "shard"),
        P("shard"),
        P("shard"),
        P("shard"),
    )
    out_specs = (
        P(None, "group", "shard", None),
        P(None, "group", "shard", None),
        P(None, "group", None),
        P("shard", None),
        P("shard", None),
        P("shard", None),
        P("shard"),
        P("shard", None),
        P("shard"),
        P(None, "shard"),
        P("shard"),
        P("shard"),
        P("shard"),
    )
    groups = mesh.shape["group"]

    def run(*args):
        return on_device(*args, groups)

    return jax.shard_map(
        run, mesh=mesh, in_specs=in_specs, out_specs=out_specs, check_vma=False
    )
```
